512 devices in a mesh: dp: 2 (over core), row: 16 (over y, z_lo), col: 16 (over z_hi, x).
Axes of the slice: x: 4, y: 4, z: 16 (z_hi: 4, z_lo: 4; z = z_hi * 4 + z_lo), core: 2. Of those that a mesh axis runs over, the one named last changes fastest.
Arguments:
- queries: bfloat16 [2, 2048, 4096], P('dp', 'row', 'col'), may hold values from -6 to 6
- key_vectors: bfloat16 [2, 2048, 4096], P('dp', 'row', 'col'), may hold values from -6 to 6
- value_vectors: bfloat16 [2, 2048, 4096], P('dp', 'row', 'col'), may hold values from -6 to 6
- out_weight: bfloat16 [4096, 3072], P('row', 'col'), may hold values from -0.09375 to 0.09375
- out_grad: bfloat16 [2, 2048, 3072], P('dp', 'row', 'col'), may hold values from -6 to 6
Outputs:
- output: bfloat16 [2, 2048, 3072], P('dp', 'row', 'col')
- grad_queries: bfloat16 [2, 2048, 4096], P('dp', 'row', 'col')
- grad_keys: bfloat16 [2, 2048, 4096], P('dp', 'row', 'col')
- grad_values: bfloat16 [2, 2048, 4096], P('dp', 'row', 'col')
- grad_weight: float32 [4096, 3072], P(('dp', 'row'), 'col')
The draws below stay inside these ranges and needn't reach their ends.
All inputs are finite; a program needn't handle non-finite values.
Results may differ from the reference program's by a relative error of at most 0.038.
Values may be sent and summed in bfloat16 or wider, within the bound.
A program may use at most 64 MiB of HBM per device.

```python
import math
import jax
import jax.numpy as jnp
from jax import lax

D = 3072
HEADS = 32
HEAD = 128
ROWS = 128
L = 2048
SEQS = 2
N_ROW = 16
N_COL = 16


def paired_draw(key):
    full_shape = (SEQS, L, HEADS * HEAD)
    query_out = jnp.clip(jax.random.normal(jax.random.fold_in(key, 21), full_shape, jnp.float32), -4.0, 4.0)
    key_out = jnp.clip(jax.random.normal(jax.random.fold_in(key, 22), full_shape, jnp.float32), -4.0, 4.0)
    return (query_out, key_out)


def draw_queries(key, part):
    return paired_draw(key)[0].astype(jnp.bfloat16)


def draw_key_vectors(key, part):
    return paired_draw(key)[1].astype(jnp.bfloat16)


def steps_of(stream_key, shape, shards, least, high):
    loudness, own = 1.0, jax.random.fold_in(stream_key, 6)
    for dim, parts in shards:
        steps = jnp.exp(jax.random.uniform(jax.random.fold_in(own, dim), (parts,), jnp.float32, least / len(shards), high / len(shards)))
        loudness = loudness * jnp.repeat(steps, shape[dim] // parts).reshape([-1 if axis == dim else 1 for axis in range(len(shape))])
    return loudness


def bell_draw(rng, extent, deviation, reach, split=(), kind=jnp.bfloat16):
    level = steps_of(rng, extent, split, -0.22, 0.18) if split else 1.0
    values = jax.random.normal(rng, extent, jnp.float32) * deviation * level
    return jnp.minimum(jnp.maximum(values, -reach), reach).astype(kind)


def setup_inputs(seed: int = 0) -> dict:
    key_of = jax.random.split(jax.random.key(seed), 6)
    return {
        "queries": draw_queries(jax.random.fold_in(key_of[5], 71), 0),
        "key_vectors": draw_key_vectors(jax.random.fold_in(key_of[5], 71), 0),
        "value_vectors": bell_draw(key_of[2], (SEQS, L, HEADS * HEAD), 1.0, 6.0, ((0, 2), (1, 16), (2, 16))),
        "out_weight": bell_draw(key_of[3], (HEADS * HEAD, D), (HEADS * HEAD) ** -0.5, 0.09375, ((0, 16), (1, 16))),
        "out_grad": bell_draw(key_of[4], (SEQS, L, D), 1.0, 6.0, ((0, 2), (1, 16), (2, 16))),
    }


NEG = -1e+30

def reference(queries, key_vectors, value_vectors, out_weight, out_grad):
    inverse_root = 1.0 / math.sqrt(HEAD)
    positions = jnp.arange(L, dtype=jnp.int32)
    visible = positions[None, :] <= positions[:, None]
    col_width = D // N_COL
    width_all = HEADS * HEAD

    def by_heads(array_in):
        return array_in.reshape(L, HEADS, HEAD).transpose(1, 0, 2)

    def from_heads(array_in):
        return array_in.transpose(1, 0, 2).reshape(L, width_all)

    def forward_head(operands):
        query_h, key_h, value_h = operands
        scores = jnp.dot(query_h, key_h.T, preferred_element_type=jnp.float32) * inverse_root
        scores = jnp.where(visible, scores, NEG)
        row_max = lax.optimization_barrier(jnp.max(scores, axis=1))
        weights = jnp.where(visible, jnp.exp(scores - row_max[:, None]), 0.0)
        norm_sum = lax.optimization_barrier(jnp.sum(weights, axis=1))
        result = jnp.dot(weights, value_h.astype(jnp.float32), precision=lax.Precision.HIGHEST, preferred_element_type=jnp.float32) / norm_sum[:, None]
        return (result, row_max + jnp.log(norm_sum))

    def backward_head(operands):
        query_h, key_h, value_h, upstream, log_norm, row_dot = operands
        scores = jnp.dot(query_h, key_h.T, preferred_element_type=jnp.float32) * inverse_root
        scores = jnp.where(visible, scores, NEG)
        probs = jnp.where(visible, jnp.exp(scores - log_norm[:, None]), 0.0)
        grad_v = jnp.dot(probs.astype(jnp.bfloat16).T, upstream, preferred_element_type=jnp.float32)
        grad_probs = jnp.dot(upstream, value_h.T, preferred_element_type=jnp.float32)
        grad_scores = (probs * (grad_probs - row_dot[:, None])).astype(jnp.bfloat16)
        grad_q = jnp.dot(grad_scores, key_h, preferred_element_type=jnp.float32) * inverse_root
        grad_k = jnp.dot(grad_scores.T, query_h, preferred_element_type=jnp.float32) * inverse_root
        return (grad_q.astype(jnp.bfloat16), grad_k.astype(jnp.bfloat16), grad_v.astype(jnp.bfloat16))
    outputs = []
    grads_query = []
    grads_key = []
    grads_value = []
    grad_weight = jnp.zeros((width_all, D), jnp.float32)
    for sequence in range(SEQS):
        query_s = by_heads(queries[sequence])
        key_s = by_heads(key_vectors[sequence])
        value_s = by_heads(value_vectors[sequence])
        head_out, log_norm = lax.map(forward_head, (query_s, key_s, value_s))
        attended = from_heads(head_out).astype(jnp.bfloat16)
        outputs.append(jnp.dot(attended, out_weight, preferred_element_type=jnp.float32).astype(jnp.bfloat16))
        grad_out_s = out_grad[sequence]

        def add_cols(carry, index):
            grad_cols = lax.dynamic_slice_in_dim(grad_out_s, index * col_width, col_width, 1)
            weight_cols = lax.dynamic_slice_in_dim(out_weight, index * col_width, col_width, 1)
            partial_sum = lax.dot_general(grad_cols, weight_cols, (((1,), (1,)), ((), ())), preferred_element_type=jnp.float32)
            partial_sum = lax.optimization_barrier(partial_sum.astype(jnp.bfloat16)).astype(jnp.float32)
            return (carry + partial_sum, None)
        grad_att, unused = lax.scan(add_cols, jnp.zeros((L, width_all), jnp.float32), jnp.arange(N_COL, dtype=jnp.int32))
        grad_att = grad_att.astype(jnp.bfloat16)
        row_dot = lax.optimization_barrier(jnp.sum((grad_att.astype(jnp.float32) * attended.astype(jnp.float32)).reshape(L, HEADS, HEAD), axis=2)).T
        grad_q, grad_k, grad_v = lax.map(backward_head, (query_s, key_s, value_s, by_heads(grad_att), log_norm, row_dot))
        grads_query.append(from_heads(grad_q))
        grads_key.append(from_heads(grad_k))
        grads_value.append(from_heads(grad_v))

        def add_rows(carry, index):
            att_rows = lax.dynamic_slice_in_dim(attended, index * ROWS, ROWS, 0)
            grad_rows = lax.dynamic_slice_in_dim(grad_out_s, index * ROWS, ROWS, 0)
            partial_sum = lax.dot_general(att_rows, grad_rows, (((0,), (0,)), ((), ())), preferred_element_type=jnp.float32)
            return (carry + partial_sum, None)
        grad_weight, unused = lax.scan(add_rows, grad_weight, jnp.arange(N_ROW, dtype=jnp.int32))
    return (jnp.stack(outputs), jnp.stack(grads_query), jnp.stack(grads_key), jnp.stack(grads_value), grad_weight)
```

```python
import functools
import math

import jax
import jax.numpy as jnp
from jax import lax
from jax.experimental import pallas as pl
from jax.experimental.pallas import tpu as pltpu
from jax.sharding import PartitionSpec as P

HEAD = 128
NEG = -1e30
SCALE = 1.0 / math.sqrt(HEAD)
F32 = jnp.float32
BF16 = jnp.bfloat16
NT = (((1,), (1,)), ((), ()))


def dot(a, b):
    return jnp.dot(a, b, preferred_element_type=F32)


def dot_nt(a, b):
    return lax.dot_general(a, b, NT, preferred_element_type=F32)


def kernel(
    n,
    rows,
    cols,
    q_ref,
    k_ref,
    v_ref,
    wt_ref,
    g_ref,
    gt_ref,
    out_ref,
    dq_ref,
    dk_ref,
    dv_ref,
    gw_ref,
    kf,
    vf,
    qf,
    df,
    st,
    wf,
    hs,
    hx,
    hz,
    hr,
    of,
    gp,
    gd,
    gy,
    gyr,
    gz,
    gzr,
    send_sems,
    recv_sems,
):
    dp, row, col = lax.axis_index("dp"), lax.axis_index("row"), lax.axis_index("col")
    y, z = row // n, lax.rem(row, n)
    u, x = col // n, lax.rem(col, n)
    chunk = n * rows
    others = list(range(1, n))
    far = sorted(others, key=lambda d: -min(d, n - d))

    def at(base, d):
        return lax.rem(base + d + n, n)

    dp_peer = {"dp": 1 - dp}

    def z_peer(d):
        return {"row": y * n + at(z, d)}

    def y_peer(d):
        return {"row": at(y, d) * n + z}

    def u_peer(d):
        return {"col": at(u, d) * n + x}

    def x_peer(d):
        return {"col": u * n + at(x, d)}

    barrier = pltpu.get_barrier_semaphore()
    peers = [dp_peer] + [f(d) for f in (z_peer, y_peer, u_peer, x_peer) for d in others]
    for peer in peers:
        pl.semaphore_signal(
            barrier, inc=1, device_id=peer, device_id_type=pl.DeviceIdType.MESH
        )

    issued = []

    def when(cond, body):
        if cond is None:
            body()
        else:
            pl.when(cond)(body)

    def send(src, dst, landed, peer, sends=None, receives=None):
        index = len(issued)

        def describe(source, target):
            return pltpu.make_async_remote_copy(
                src_ref=source,
                dst_ref=target,
                send_sem=send_sems.at[index],
                recv_sem=recv_sems.at[index],
                device_id=peer,
                device_id_type=pl.DeviceIdType.MESH,
            )

        when(sends, lambda: describe(src, dst).start())
        issued.append(lambda: when(sends, lambda: describe(src, dst).wait_send()))
        return lambda: when(receives, lambda: describe(landed, landed).wait_recv())

    def wait(handles):
        for handle in handles:
            handle()

    def block(i):
        return pl.ds(pl.multiple_of(i * rows, rows), rows)

    def group(i):
        return pl.ds(pl.multiple_of(i * chunk, chunk), chunk)

    def gather_z(view):
        return [
            send(view(row), view(row), view(y * n + at(z, -d)), z_peer(d))
            for d in others
        ]

    def gather_y(view, up):
        handles = []
        for d in others:
            target, source = (y + d, y - d) if up else (y - d, y + d)
            sends = target < n if up else target >= 0
            receives = source >= 0 if up else source < n
            handles.append(
                send(
                    view(y),
                    view(y),
                    view(at(y, -d if up else d)),
                    y_peer(d if up else -d),
                    sends,
                    receives,
                )
            )
        return handles

    kf[block(row), :] = k_ref[...]
    vf[block(row), :] = v_ref[...]
    qf[block(row), :] = q_ref[...]
    half = cols // 2
    mine = pl.ds(pl.multiple_of(dp * half, half), half)
    theirs = pl.ds(pl.multiple_of((1 - dp) * half, half), half)
    wf[row, mine, :] = wt_ref[mine, :]
    pl.semaphore_wait(barrier, len(peers))

    def w_view(i):
        return wf.at[i, mine, :]

    def w_group(i, part=mine):
        return wf.at[pl.ds(i * n, n), part, :]

    k_z = gather_z(lambda i: kf.at[block(i), :])
    v_z = gather_z(lambda i: vf.at[block(i), :])
    w_z = gather_z(w_view)
    wait(k_z)
    k_y = gather_y(lambda i: kf.at[group(i), :], True)
    wait(v_z)
    v_y = gather_y(lambda i: vf.at[group(i), :], True)
    wait(w_z)
    w_y = [
        send(w_group(y), w_group(y), w_group(at(y, -d)), y_peer(d)) for d in others
    ]
    w_d = [send(w_group(y), w_group(y), w_group(y, theirs), dp_peer)]
    q_z = gather_z(lambda i: qf.at[block(i), :])

    heads = [slice(h * HEAD, (h + 1) * HEAD) for h in range(2)]
    query_pos = row * rows + lax.broadcasted_iota(jnp.int32, (rows, chunk), 0)
    key_pos = lax.broadcasted_iota(jnp.int32, (rows, chunk), 1)

    def forward(j, carry):
        visible = key_pos + j * chunk <= query_pos
        result = []
        for lanes, (top, total, acc) in zip(heads, carry):
            scores = dot_nt(q_ref[:, lanes], kf[group(j), lanes]) * SCALE
            scores = jnp.where(visible, scores, NEG)
            new_top = jnp.maximum(top, jnp.max(scores, axis=1, keepdims=True))
            weights = jnp.exp(scores - new_top)
            fade = jnp.exp(top - new_top)
            total = fade * total + jnp.sum(weights, axis=1, keepdims=True)
            acc = fade * acc + dot(weights.astype(BF16), vf[group(j), lanes])
            result.append((new_top, total, acc))
        return tuple(result)

    wait(k_y)
    wait(v_y)
    start = tuple(
        (
            jnp.full((rows, 1), NEG, F32),
            jnp.zeros((rows, 1), F32),
            jnp.zeros((rows, HEAD), F32),
        )
        for _ in heads
    )
    done = lax.fori_loop(0, y + 1, forward, start)
    log_norms = []
    own_of = x * n + u
    for lanes, (top, total, acc) in zip(heads, done):
        of[own_of, :, lanes] = (acc / total).astype(BF16)
        log_norms.append(top + jnp.log(total))

    o_u = [
        send(of.at[own_of], of.at[own_of], of.at[x * n + at(u, -d)], u_peer(d))
        for d in far
    ]

    for d, handle in zip(others, w_y):
        handle()
        source = at(y, -d)
        w_d.append(send(w_group(source), w_group(source), w_group(source, theirs), dp_peer))
    wait(q_z)
    q_y = gather_y(lambda i: qf.at[group(i), :], False)
    wait(w_d)

    h_x = {}
    for d in far + [0]:
        for e in far + [0]:
            target_x, target_u = at(x, d), at(u, e)
            slot = target_x * n + target_u
            hs[slot] = dot(g_ref[...], wf[target_u * n + target_x]).astype(BF16)
            if d:
                h_x[d, e] = send(
                    hs.at[slot], hx.at[d - 1, e], hx.at[d - 1, e], x_peer(d)
                )

    wait(o_u)
    mine_x = pl.ds(x * n, n)
    o_x = [
        send(of.at[mine_x], of.at[mine_x], of.at[pl.ds(at(x, -d) * n, n)], x_peer(d))
        for d in far
    ]

    h_u = []
    for e in far + [0]:
        total = hs[x * n + at(u, e)].astype(F32)
        for d in far:
            h_x[d, e]()
            total = total + hx[d - 1, e].astype(F32)
        hz[e] = total.astype(BF16)
        if e:
            h_u.append(send(hz.at[e], hr.at[e - 1], hr.at[e - 1], u_peer(e)))

    wait(h_u)
    upstream = hz[0].astype(F32)
    for e in others:
        upstream = upstream + hr[e - 1].astype(F32)
    df[block(row), :] = upstream.astype(BF16)
    d_z = gather_z(lambda i: df.at[block(i), :])
    own_up = df[block(row), :].astype(F32)
    attended = of[own_of].astype(F32)
    dots = [
        jnp.sum(own_up[:, lanes] * attended[:, lanes], axis=1, keepdims=True)
        for lanes in heads
    ]
    lane = lax.broadcasted_iota(jnp.int32, (rows, rows), 1)
    table = jnp.zeros((rows, rows), F32)
    for i, column in enumerate(log_norms + dots):
        table = jnp.where(lane == i, column, table)
    st[:, block(row)] = jnp.transpose(table)[:8, :]
    s_z = gather_z(lambda i: st.at[:, block(i)])

    wait(o_x)

    def weight_part(which, target_y):
        first = (which * n * n + target_y * n) // 2
        for i in range(n // 2):
            c = first + i
            part = dot(gt_ref[...], of[lax.rem(c, n) * n + c // n]).astype(BF16)
            gp[2 * c] = part[:, :HEAD]
            gp[2 * c + 1] = part[:, HEAD:]

    g_d = {}
    for d in far + [0]:
        target_y = at(y, d)
        weight_part(1 - dp, target_y)
        away = pl.ds((1 - dp) * n * n + target_y * n, n)
        here = pl.ds(target_y * n, n)
        g_d[d] = send(gp.at[away], gd.at[here], gd.at[here], dp_peer)
    for d in far + [0]:
        weight_part(dp, at(y, d))

    wait(d_z)
    d_y = gather_y(lambda i: df.at[group(i), :], False)
    wait(s_z)
    s_y = gather_y(lambda i: st.at[:, group(i)], False)

    g_y = []
    for d in far + [0]:
        target_y = at(y, d)
        g_d[d]()
        for i in range(n):
            slot = target_y * n + i
            gy[slot] = (
                gp[dp * n * n + slot].astype(F32) + gd[slot].astype(F32)
            ).astype(BF16)
        if d:
            here = pl.ds(target_y * n, n)
            g_y.append(send(gy.at[here], gyr.at[d - 1], gyr.at[d - 1], y_peer(d)))

    def queries_pass(j, carry):
        visible = key_pos + j * chunk <= query_pos
        result = []
        for h, lanes in enumerate(heads):
            keys = kf[group(j), lanes]
            scores = dot_nt(q_ref[:, lanes], keys) * SCALE
            probs = jnp.where(visible, jnp.exp(scores - log_norms[h]), 0.0)
            slopes = dot_nt(df[block(row), lanes], vf[group(j), lanes])
            slopes = (probs * (slopes - dots[h])).astype(BF16)
            result.append(carry[h] + dot(slopes, keys))
        return tuple(result)

    zero = jnp.zeros((rows, HEAD), F32)
    sums = lax.fori_loop(0, y + 1, queries_pass, (zero, zero))
    for lanes, value in zip(heads, sums):
        dq_ref[:, lanes] = (value * SCALE).astype(BF16)

    def project(c, acc):
        return acc + dot_nt(of[lax.rem(c, n) * n + c // n], wf[c])

    out_ref[...] = lax.fori_loop(
        0, n * n, project, jnp.zeros((rows, cols), F32)
    ).astype(BF16)

    wait(g_y)
    g_z = []
    for d in others + [0]:
        target_z = at(z, d)
        total = gy[y * n + target_z].astype(F32)
        for e in others:
            total = total + gyr[e - 1, target_z].astype(F32)
        gz[d] = total.astype(BF16)
        if d:
            g_z.append(send(gz.at[d], gzr.at[d - 1], gzr.at[d - 1], z_peer(d)))

    wait(q_y)
    wait(d_y)
    wait(s_y)
    own_key = row * rows + lax.broadcasted_iota(jnp.int32, (rows, chunk), 0)

    def keys_pass(j, carry):
        visible = key_pos + j * chunk >= own_key
        result = []
        for h, lanes in enumerate(heads):
            queries = qf[group(j), lanes]
            ups = df[group(j), lanes]
            norm = st[h : h + 1, group(j)]
            away = st[2 + h : 3 + h, group(j)]
            scores = dot_nt(k_ref[:, lanes], queries) * SCALE
            probs = jnp.where(visible, jnp.exp(scores - norm), 0.0)
            slopes = dot_nt(v_ref[:, lanes], ups)
            slopes = (probs * (slopes - away)).astype(BF16)
            sum_k, sum_v = carry[h]
            result.append(
                (sum_k + dot(slopes, queries), sum_v + dot(probs.astype(BF16), ups))
            )
        return tuple(result)

    sums = lax.fori_loop(y, n, keys_pass, ((zero, zero), (zero, zero)))
    for lanes, (sum_k, sum_v) in zip(heads, sums):
        dk_ref[:, lanes] = (sum_k * SCALE).astype(BF16)
        dv_ref[:, lanes] = sum_v.astype(BF16)

    wait(g_z)
    total = gz[0].astype(F32)
    for d in others:
        total = total + gzr[d - 1].astype(F32)
    gw_ref[...] = total

    for finish in issued:
        finish()


def shards(n, queries, key_vectors, value_vectors, out_weight, out_grad):
    rows, width = queries.shape[1:]
    cols = out_grad.shape[2]
    blocks = n * n
    copies = (17 + n) * (n - 1) + 2 * n
    vmem = pl.BlockSpec(memory_space=pltpu.VMEM)
    full = pltpu.VMEM((blocks * rows, width), BF16)
    result = pl.pallas_call(
        functools.partial(kernel, n, rows, cols),
        out_shape=(
            jax.ShapeDtypeStruct((rows, cols), BF16),
            jax.ShapeDtypeStruct((rows, width), BF16),
            jax.ShapeDtypeStruct((rows, width), BF16),
            jax.ShapeDtypeStruct((rows, width), BF16),
            jax.ShapeDtypeStruct((cols, HEAD), F32),
        ),
        in_specs=[vmem] * 6,
        out_specs=(vmem,) * 5,
        scratch_shapes=[
            full,
            full,
            full,
            full,
            pltpu.VMEM((8, blocks * rows), F32),
            pltpu.VMEM((blocks, cols, width), BF16),
            pltpu.VMEM((blocks, rows, width), BF16),
            pltpu.VMEM((n - 1, n, rows, width), BF16),
            pltpu.VMEM((n, rows, width), BF16),
            pltpu.VMEM((n - 1, rows, width), BF16),
            pltpu.VMEM((blocks, rows, width), BF16),
            pltpu.VMEM((2 * blocks, cols, HEAD), BF16),
            pltpu.VMEM((blocks, cols, HEAD), BF16),
            pltpu.VMEM((blocks, cols, HEAD), BF16),
            pltpu.VMEM((n - 1, n, cols, HEAD), BF16),
            pltpu.VMEM((n, cols, HEAD), BF16),
            pltpu.VMEM((n - 1, cols, HEAD), BF16),
            pltpu.SemaphoreType.DMA((copies,)),
            pltpu.SemaphoreType.DMA((copies,)),
        ],
        compiler_params=pltpu.CompilerParams(
            collective_id=0, has_side_effects=True, vmem_limit_bytes=48 << 20
        ),
    )(
        queries[0],
        key_vectors[0],
        value_vectors[0],
        out_weight.T,
        out_grad[0],
        out_grad[0].T,
    )
    output, grad_queries, grad_keys, grad_values, grad_weight = result
    return (
        output[None],
        grad_queries[None],
        grad_keys[None],
        grad_values[None],
        grad_weight.T,
    )


def solution(mesh):
    n = math.isqrt(mesh.shape["row"])
    return jax.shard_map(
        functools.partial(shards, n),
        mesh=mesh,
        in_specs=(
            P("dp", "row", "col"),
            P("dp", "row", "col"),
            P("dp", "row", "col"),
            P("row", "col"),
            P("dp", "row", "col"),
        ),
        out_specs=(
            P("dp", "row", "col"),
            P("dp", "row", "col"),
            P("dp", "row", "col"),
            P("dp", "row", "col"),
            P(("dp", "row"), "col"),
        ),
        check_vma=False,
    )
```

```python
import functools
import math

import jax
import jax.numpy as jnp
from jax import lax
from jax.experimental import pallas as pl
from jax.experimental.pallas import tpu as pltpu
from jax.sharding import PartitionSpec as P

HEAD = 128
NEG = -1e30
SCALE = 1.0 / math.sqrt(HEAD)
F32 = jnp.float32
BF16 = jnp.bfloat16
NT = (((1,), (1,)), ((), ()))
TN = (((0,), (0,)), ((), ()))


def dot(a, b):
    return jnp.dot(a, b, preferred_element_type=F32)


def dot_nt(a, b):
    return lax.dot_general(a, b, NT, preferred_element_type=F32)


def flip(a):
    size = a.shape[0]
    eye = (
        lax.broadcasted_iota(jnp.int32, (size, size), 0)
        == lax.broadcasted_iota(jnp.int32, (size, size), 1)
    )
    eye = jnp.where(eye, 1.0, 0.0).astype(BF16)
    return lax.dot_general(a, eye, TN, preferred_element_type=F32).astype(BF16)


def kernel(
    n,
    rows,
    cols,
    q_hbm,
    k_hbm,
    v_hbm,
    w_hbm,
    g_hbm,
    out_ref,
    dq_ref,
    dk_ref,
    dv_ref,
    gw_ref,
    q_in,
    k_in,
    v_in,
    w_in,
    qs,
    ks,
    vs,
    ws,
    kf,
    vf,
    qf,
    df,
    st,
    wf,
    gf,
    gt,
    hs,
    hx,
    hz,
    hr,
    of,
    top_ref,
    sum_ref,
    acc_ref,
    gp,
    gd,
    gy,
    gyr,
    gz,
    gzr,
    ox,
    oxr,
    dx,
    dxr,
    load_sems,
    send_sems,
    recv_sems,
):
    dp, row, col = lax.axis_index("dp"), lax.axis_index("row"), lax.axis_index("col")
    m = n // 2
    y, z = row // n, lax.rem(row, n)
    zh, side = z // 2, lax.rem(z, 2)
    u, x = col // n, lax.rem(col, n)
    pair = y * m + zh
    span = 2 * rows
    chunk = n * rows
    others = list(range(1, n))
    far = sorted(others, key=lambda d: -min(d, n - d))
    near = far[::-1]

    def at(base, d):
        return lax.rem(base + d + n, n)

    dp_peer = {"dp": 1 - dp}
    twin = {"row": row + 1 - 2 * side}

    def z_peer(d):
        return {"row": y * n + at(z, d)}

    def h_peer(d):
        return {"row": y * n + 2 * lax.rem(zh + d, m) + side}

    def y_peer(d):
        return {"row": at(y, d) * n + z}

    def u_peer(d):
        return {"col": at(u, d) * n + x}

    def x_peer(d):
        return {"col": u * n + at(x, d)}

    def block(i):
        return pl.ds(pl.multiple_of(i * rows, rows), rows)

    def span_of(i):
        return pl.ds(pl.multiple_of(i * span, span), span)

    def group(i):
        return pl.ds(pl.multiple_of(i * chunk, chunk), chunk)

    loads = [
        pltpu.make_async_copy(source, target, load_sems.at[i])
        for i, (source, target) in enumerate(
            [
                (w_hbm, w_in),
                (g_hbm, gf.at[block(side), :]),
                (k_hbm, k_in),
                (q_hbm, q_in),
                (v_hbm, v_in),
            ]
        )
    ]
    for load in loads:
        load.start()

    barrier = pltpu.get_barrier_semaphore()
    peers = [dp_peer] + [f(d) for f in (z_peer, y_peer, u_peer, x_peer) for d in others]
    for peer in peers:
        pl.semaphore_signal(
            barrier, inc=1, device_id=peer, device_id_type=pl.DeviceIdType.MESH
        )

    issued = []

    def when(cond, body):
        if cond is None:
            body()
        else:
            pl.when(cond)(body)

    def send(src, dst, landed, peer, sends=None, receives=None):
        index = len(issued)

        def describe(source, target):
            return pltpu.make_async_remote_copy(
                src_ref=source,
                dst_ref=target,
                send_sem=send_sems.at[index],
                recv_sem=recv_sems.at[index],
                device_id=peer,
                device_id_type=pl.DeviceIdType.MESH,
            )

        when(sends, lambda: describe(src, dst).start())
        issued.append(lambda: when(sends, lambda: describe(src, dst).wait_send()))
        return lambda inside=False: when(
            None if inside else receives, lambda: describe(landed, landed).wait_recv()
        )

    def wait(handles):
        for handle in handles:
            handle()

    half = cols // 2
    mine = pl.ds(pl.multiple_of(dp * half, half), half)
    theirs = pl.ds(pl.multiple_of((1 - dp) * half, half), half)
    lanes = [slice(h * HEAD, (h + 1) * HEAD) for h in range(2)]

    for load in loads:
        load.wait()
    for h in range(2):
        ws[h] = flip(w_in[lanes[h], :])
    wf[row, mine, :] = ws[side, mine, :]
    for source, split, full in ((k_in, ks, kf), (q_in, qs, qf), (v_in, vs, vf)):
        for h in range(2):
            split[h] = source[:, lanes[h]]
        full[block(row), :] = split[side]
    pl.semaphore_wait(barrier, len(peers))

    def spread_z(split, full, d):
        source = y * n + at(z, -d)
        return send(
            split.at[lax.rem(at(z, d), 2)],
            full.at[block(row), :],
            full.at[block(source), :],
            z_peer(d),
        )

    def gather_h(view):
        return [
            send(view(pair), view(pair), view(y * m + lax.rem(zh + m - d, m)), h_peer(d))
            for d in range(1, m)
        ]

    def gather_y(view, up):
        handles = {}
        for d in near:
            target, source = (y + d, y - d) if up else (y - d, y + d)
            sends = target < n if up else target >= 0
            receives = source >= 0 if up else source < n
            handles[d] = send(
                view(y),
                view(y),
                view(at(y, -d if up else d)),
                y_peer(d if up else -d),
                sends,
                receives,
            )
        return handles

    def w_group(i, part=mine):
        return wf.at[pl.ds(i * n, n), part, :]

    w_z = [
        send(
            ws.at[lax.rem(at(z, d), 2), mine, :],
            wf.at[row, mine, :],
            wf.at[y * n + at(z, -d), mine, :],
            z_peer(d),
        )
        for d in others
    ]
    g_s = send(
        gf.at[block(side), :], gf.at[block(side), :], gf.at[block(1 - side), :], twin
    )
    k_z = [spread_z(ks, kf, d) for d in others]
    q_s = send(
        qs.at[1 - side],
        qf.at[block(row), :],
        qf.at[block(row + 1 - 2 * side), :],
        twin,
    )
    v_z = [spread_z(vs, vf, d) for d in others]

    wait(w_z)
    w_y = {
        d: send(w_group(y), w_group(y), w_group(at(y, -d)), y_peer(d)) for d in near
    }
    w_d = [send(w_group(y), w_group(y), w_group(y, theirs), dp_peer)]
    wait(k_z)
    k_y = gather_y(lambda i: kf.at[group(i), :], True)
    wait(v_z)
    v_y = gather_y(lambda i: vf.at[group(i), :], True)
    g_s()
    gt[:, : rows] = flip(gf[:rows, :])
    gt[:, rows:] = flip(gf[rows:, :])
    q_s()

    query_pos = pair * span + lax.broadcasted_iota(jnp.int32, (span, chunk), 0)
    key_pos = y * chunk + lax.broadcasted_iota(jnp.int32, (span, chunk), 1)

    def forward(j, first):
        scores = dot_nt(qf[span_of(pair), :], kf[group(j), :]) * SCALE
        if first:
            scores = jnp.where(key_pos <= query_pos, scores, NEG)
        new_top = jnp.max(scores, axis=1, keepdims=True)
        if not first:
            top = top_ref[:, :1]
            new_top = jnp.maximum(top, new_top)
        weights = jnp.exp(scores - new_top)
        total = jnp.sum(weights, axis=1, keepdims=True)
        acc = dot(weights.astype(BF16), vf[group(j), :])
        if not first:
            fade = jnp.exp(top - new_top)
            total = fade * sum_ref[:, :1] + total
            acc = fade * acc_ref[...] + acc
        top_ref[...] = jnp.broadcast_to(new_top, top_ref.shape)
        sum_ref[...] = jnp.broadcast_to(total, sum_ref.shape)
        acc_ref[...] = acc

    forward(y, True)
    for d in near:
        w_y[d]()
        source = at(y, -d)
        w_d.append(
            send(w_group(source), w_group(source), w_group(source, theirs), dp_peer)
        )
    q_z = [
        send(
            qs.at[lax.rem(at(z, d), 2)],
            qf.at[block(row), :],
            qf.at[block(y * n + at(z, -d)), :],
            z_peer(d),
            at(z, d) != z + 1 - 2 * side,
            at(z, -d) != z + 1 - 2 * side,
        )
        for d in others
    ]
    wait(w_d)

    h_x = {}
    for d in far + [0]:
        for e in far + [0]:
            target_x, target_u = at(x, d), at(u, e)
            slot = target_x * n + target_u
            hs[slot] = dot(gf[...], wf[target_u * n + target_x]).astype(BF16)
            if d:
                h_x[d, e] = send(
                    hs.at[slot], hx.at[d - 1, e], hx.at[d - 1, e], x_peer(d)
                )

    for d in near:

        @pl.when(y >= d)
        def _(d=d):
            k_y[d](True)
            v_y[d](True)
            forward(y - d, False)

    own_of = x * n + u
    total = sum_ref[:, :1]
    of[own_of] = (acc_ref[...] / total).astype(BF16)
    log_norm = top_ref[:, :1] + jnp.log(total)
    o_u = {
        d: send(of.at[own_of], of.at[own_of], of.at[x * n + at(u, -d)], u_peer(d))
        for d in far
    }

    def spread_x(e):
        return [
            send(
                of.at[x * n + at(u, -e)],
                of.at[x * n + at(u, -e)],
                of.at[at(x, -d) * n + at(u, -e)],
                x_peer(d),
            )
            for d in far
        ]

    o_x = spread_x(0)
    wait(q_z)
    q_y = gather_y(lambda i: qf.at[group(i), :], False)

    h_u = []
    for e in far + [0]:
        total = hs[x * n + at(u, e)].astype(F32)
        for d in far:
            h_x[d, e]()
            total = total + hx[d - 1, e].astype(F32)
        hz[e] = total.astype(BF16)
        if e:
            h_u.append(send(hz.at[e], hr.at[e - 1], hr.at[e - 1], u_peer(e)))

    for d in near:
        o_u[d]()
        o_x += spread_x(d)

    wait(h_u)
    upstream = hz[0].astype(F32)
    for e in others:
        upstream = upstream + hr[e - 1].astype(F32)
    df[span_of(pair), :] = upstream.astype(BF16)
    d_h = gather_h(lambda i: df.at[span_of(i), :])
    attended = of[own_of].astype(F32)
    row_dot = jnp.sum(
        df[span_of(pair), :].astype(F32) * attended, axis=1, keepdims=True
    )
    lane = lax.broadcasted_iota(jnp.int32, (span, HEAD), 1)
    table = jnp.where(lane == 0, log_norm, jnp.where(lane == 1, row_dot, 0.0))
    st[:, span_of(pair)] = jnp.transpose(table)[:8, :]
    s_h = gather_h(lambda i: st.at[:, span_of(i)])

    wait(d_h)
    d_y = gather_y(lambda i: df.at[group(i), :], False)
    wait(s_h)
    s_y = gather_y(lambda i: st.at[:, group(i)], False)

    wait(o_x)

    def weight_part(which, target_y):
        first = which * n * m + target_y * m
        for i in range(m):
            c = first + i
            part = dot(gt[...], of[lax.rem(c, n) * n + c // n])
            gp[c] = part.astype(BF16)

    g_d = {}
    for d in far + [0]:
        target_y = at(y, d)
        weight_part(1 - dp, target_y)
        away = pl.ds((1 - dp) * n * m + target_y * m, m)
        here = pl.ds(target_y * m, m)
        g_d[d] = send(gp.at[away], gd.at[here], gd.at[here], dp_peer)
    for d in far + [0]:
        weight_part(dp, at(y, d))

    g_y = []
    for d in far + [0]:
        target_y = at(y, d)
        g_d[d]()
        for i in range(m):
            slot = target_y * m + i
            gy[slot] = (
                gp[dp * n * m + slot].astype(F32) + gd[slot].astype(F32)
            ).astype(BF16)
        if d:
            here = pl.ds(target_y * m, m)
            g_y.append(send(gy.at[here], gyr.at[d - 1], gyr.at[d - 1], y_peer(d)))

    def project(c, acc):
        return acc + dot_nt(wf[c], of[lax.rem(c, n) * n + c // n])

    projected = lax.fori_loop(0, n * n, project, jnp.zeros((cols, span), F32))
    for h in range(2):
        ox[h] = projected[:, lanes[h]].astype(BF16)
    o_s = send(ox.at[1 - side], oxr, oxr, twin)

    def queries_pass(j, first, acc):
        keys = kf[group(j), :]
        scores = dot_nt(qf[span_of(pair), :], keys) * SCALE
        probs = jnp.exp(scores - log_norm)
        if first:
            probs = jnp.where(key_pos <= query_pos, probs, 0.0)
        slopes = dot_nt(df[span_of(pair), :], vf[group(j), :])
        slopes = (probs * (slopes - row_dot)).astype(BF16)
        return acc + dot(slopes, keys)

    acc = queries_pass(y, True, jnp.zeros((span, HEAD), F32))
    acc = lax.fori_loop(0, y, lambda j, acc: queries_pass(j, False, acc), acc)
    acc = (acc * SCALE).astype(BF16)
    dx[0, 0], dx[0, 1] = acc[:rows], acc[rows:]
    swaps = [send(dx.at[0, 1 - side], dxr.at[0], dxr.at[0], twin)]

    wait(g_y)
    g_z = []
    for d in list(range(1, m)) + [0]:
        target = lax.rem(zh + d, m)
        total = gy[y * m + target].astype(F32)
        for e in others:
            total = total + gyr[e - 1, target].astype(F32)
        gz[d] = total.astype(BF16)
        if d:
            g_z.append(send(gz.at[d], gzr.at[d - 1], gzr.at[d - 1], h_peer(d)))

    own_key = pair * span + lax.broadcasted_iota(jnp.int32, (span, chunk), 0)
    ask_pos = y * chunk + lax.broadcasted_iota(jnp.int32, (span, chunk), 1)

    def keys_pass(j, first):
        queries = qf[group(j), :]
        ups = df[group(j), :]
        norm = st[0:1, group(j)]
        away = st[1:2, group(j)]
        scores = dot_nt(kf[span_of(pair), :], queries) * SCALE
        probs = jnp.exp(scores - norm)
        if first:
            probs = jnp.where(ask_pos >= own_key, probs, 0.0)
        slopes = dot_nt(vf[span_of(pair), :], ups)
        slopes = (probs * (slopes - away)).astype(BF16)
        sum_k, sum_v = dot(slopes, queries), dot(probs.astype(BF16), ups)
        if first:
            acc_ref[...], sum_ref[...] = sum_k, sum_v
        else:
            acc_ref[...] += sum_k
            sum_ref[...] += sum_v

    keys_pass(y, True)
    for d in near:

        @pl.when(y + d < n)
        def _(d=d):
            q_y[d](True)
            d_y[d](True)
            s_y[d](True)
            keys_pass(y + d, False)

    for i, value in ((1, acc_ref[...] * SCALE), (2, sum_ref[...])):
        value = value.astype(BF16)
        dx[i, 0], dx[i, 1] = value[:rows], value[rows:]
        swaps.append(send(dx.at[i, 1 - side], dxr.at[i], dxr.at[i], twin))

    wait(g_z)
    total = gz[0].astype(F32)
    for d in range(1, m):
        total = total + gzr[d - 1].astype(F32)
    gw_ref[...] = total
    o_s()
    out_ref[...] = (ox[side].astype(F32) + oxr[...].astype(F32)).astype(BF16)
    for i, target in enumerate((dq_ref, dk_ref, dv_ref)):
        swaps[i]()
        own, other = dx[i, side], dxr[i]
        for h in range(2):
            target[:, lanes[h]] = jnp.where(side == h, own, other)

    for finish in issued:
        finish()


def shards(n, queries, key_vectors, value_vectors, out_weight, out_grad):
    rows, width = queries.shape[1:]
    cols = out_grad.shape[2]
    blocks, m = n * n, n // 2
    copies = 27 * (n - 1) + n * (n - 1) + 2 * n + 8 * m + 16
    vmem = pl.BlockSpec(memory_space=pltpu.VMEM)

    def buffer(*shape, kind=BF16):
        return pltpu.VMEM(shape, kind)

    full = buffer(blocks * rows, HEAD)
    span = 2 * rows
    result = pl.pallas_call(
        functools.partial(kernel, n, rows, cols),
        out_shape=(
            jax.ShapeDtypeStruct((cols, rows), BF16),
            jax.ShapeDtypeStruct((rows, width), BF16),
            jax.ShapeDtypeStruct((rows, width), BF16),
            jax.ShapeDtypeStruct((rows, width), BF16),
            jax.ShapeDtypeStruct((cols, HEAD), F32),
        ),
        in_specs=[pl.BlockSpec(memory_space=pl.ANY)] * 5,
        out_specs=(vmem,) * 5,
        scratch_shapes=[
            buffer(rows, width),
            buffer(rows, width),
            buffer(rows, width),
            buffer(width, cols),
            buffer(2, rows, HEAD),
            buffer(2, rows, HEAD),
            buffer(2, rows, HEAD),
            buffer(2, cols, HEAD),
            full,
            full,
            full,
            full,
            buffer(8, blocks * rows, kind=F32),
            buffer(blocks, cols, HEAD),
            buffer(span, cols),
            buffer(cols, span),
            buffer(blocks, span, HEAD),
            buffer(n - 1, n, span, HEAD),
            buffer(n, span, HEAD),
            buffer(n - 1, span, HEAD),
            buffer(blocks, span, HEAD),
            buffer(span, HEAD, kind=F32),
            buffer(span, HEAD, kind=F32),
            buffer(span, HEAD, kind=F32),
            buffer(blocks, cols, HEAD),
            buffer(n * m, cols, HEAD),
            buffer(n * m, cols, HEAD),
            buffer(n - 1, m, cols, HEAD),
            buffer(m, cols, HEAD),
            buffer(max(m - 1, 1), cols, HEAD),
            buffer(2, cols, rows),
            buffer(cols, rows),
            buffer(3, 2, rows, HEAD),
            buffer(3, rows, HEAD),
            pltpu.SemaphoreType.DMA((5,)),
            pltpu.SemaphoreType.DMA((copies,)),
            pltpu.SemaphoreType.DMA((copies,)),
        ],
        compiler_params=pltpu.CompilerParams(
            collective_id=0, has_side_effects=True, vmem_limit_bytes=48 << 20
        ),
    )(queries[0], key_vectors[0], value_vectors[0], out_weight, out_grad[0])
    output, grad_queries, grad_keys, grad_values, grad_weight = result
    return (
        output.T[None],
        grad_queries[None],
        grad_keys[None],
        grad_values[None],
        grad_weight.T,
    )


def solution(mesh):
    n = math.isqrt(mesh.shape["row"])
    return jax.shard_map(
        functools.partial(shards, n),
        mesh=mesh,
        in_specs=(
            P("dp", "row", "col"),
            P("dp", "row", "col"),
            P("dp", "row", "col"),
            P("row", "col"),
            P("dp", "row", "col"),
        ),
        out_specs=(
            P("dp", "row", "col"),
            P("dp", "row", "col"),
            P("dp", "row", "col"),
            P("dp", "row", "col"),
            P(("dp", "row"), "col"),
        ),
        check_vma=False,
    )
```

```python
import functools
import math

import jax
import jax.numpy as jnp
from jax import lax
from jax.experimental import pallas as pl
from jax.experimental.pallas import tpu as pltpu
from jax.sharding import PartitionSpec as P

HEAD = 128
NEG = -1e30
SCALE = 1.0 / math.sqrt(HEAD)
F32 = jnp.float32
BF16 = jnp.bfloat16
NT = (((1,), (1,)), ((), ()))
TN = (((0,), (0,)), ((), ()))


def dot(a, b):
    return jnp.dot(a, b, preferred_element_type=F32)


def dot_nt(a, b):
    return lax.dot_general(a, b, NT, preferred_element_type=F32)


def flip(a):
    size = a.shape[0]
    eye = (
        lax.broadcasted_iota(jnp.int32, (size, size), 0)
        == lax.broadcasted_iota(jnp.int32, (size, size), 1)
    )
    eye = jnp.where(eye, 1.0, 0.0).astype(BF16)
    return lax.dot_general(a, eye, TN, preferred_element_type=F32).astype(BF16)


def kernel(
    n,
    rows,
    cols,
    q_hbm,
    k_hbm,
    v_hbm,
    w_hbm,
    g_hbm,
    out_ref,
    dq_ref,
    dk_ref,
    dv_ref,
    gw_ref,
    qs,
    ks,
    vs,
    ws,
    kf,
    vf,
    qf,
    df,
    st,
    wf,
    gf,
    gt,
    hs,
    hx,
    hz,
    hr,
    of,
    top_ref,
    sum_ref,
    acc_ref,
    gp,
    gd,
    gy,
    gyr,
    gz,
    gzr,
    ox,
    oxr,
    dx,
    dxr,
    load_sems,
    send_sems,
    recv_sems,
):
    dp, row, col = lax.axis_index("dp"), lax.axis_index("row"), lax.axis_index("col")
    m = n // 2
    y, z = row // n, lax.rem(row, n)
    zh, side = z // 2, lax.rem(z, 2)
    u, x = col // n, lax.rem(col, n)
    pair = y * m + zh
    span = 2 * rows
    chunk = n * rows
    others = list(range(1, n))
    far = sorted(others, key=lambda d: -min(d, n - d))
    near = far[::-1]
    z_steps = [(h, t) for h in range(m) for t in (1, 0) if h or t]

    def at(base, d):
        return lax.rem(base + d + n, n)

    def at_h(d):
        return lax.rem(zh + d + m, m)

    dp_peer = {"dp": 1 - dp}
    twin = {"row": row + 1 - 2 * side}

    def z_row(h, t):
        return y * n + 2 * at_h(h) + (1 - side if t else side)

    def h_peer(d):
        return {"row": z_row(d, 0)}

    def y_peer(d):
        return {"row": at(y, d) * n + z}

    def u_peer(d):
        return {"col": at(u, d) * n + x}

    def x_peer(d):
        return {"col": u * n + at(x, d)}

    def block(i):
        return pl.ds(pl.multiple_of(i * rows, rows), rows)

    def span_of(i):
        return pl.ds(pl.multiple_of(i * span, span), span)

    def group(i):
        return pl.ds(pl.multiple_of(i * chunk, chunk), chunk)

    half = cols // 2
    mine = pl.ds(pl.multiple_of(dp * half, half), half)
    theirs = pl.ds(pl.multiple_of((1 - dp) * half, half), half)
    own_lanes = block(side)
    other_lanes = block(1 - side)

    pieces = [
        (w_hbm.at[mine, own_lanes], wf.at[row, mine, :]),
        (w_hbm.at[mine, other_lanes], ws.at[mine, :]),
        (g_hbm, gt.at[:, own_lanes]),
    ]
    for source, split, full in ((k_hbm, ks, kf), (q_hbm, qs, qf), (v_hbm, vs, vf)):
        pieces.append((source.at[:, own_lanes], full.at[block(row), :]))
        pieces.append((source.at[:, other_lanes], split))
    loads = [
        pltpu.make_async_copy(source, target, load_sems.at[i])
        for i, (source, target) in enumerate(pieces)
    ]

    barrier = pltpu.get_barrier_semaphore()
    peers = [dp_peer] + [{"row": z_row(h, t)} for h, t in z_steps]
    peers += [f(d) for f in (u_peer, y_peer, x_peer) for d in far]
    for peer in peers:
        pl.semaphore_signal(
            barrier, inc=1, device_id=peer, device_id_type=pl.DeviceIdType.MESH
        )
    for load in loads:
        load.start()

    issued = []
    slots = [0]

    def when(cond, body):
        if cond is None:
            body()
        else:
            pl.when(cond)(body)

    def take(count):
        slots[0] += count
        return slots[0] - count

    def send(src, dst, landed, peer, sends=None, receives=None, index=None, hears=None):
        index = take(1) if index is None else index
        hears = index if hears is None else hears

        def describe(source, target, which):
            return pltpu.make_async_remote_copy(
                src_ref=source,
                dst_ref=target,
                send_sem=send_sems.at[which],
                recv_sem=recv_sems.at[which],
                device_id=peer,
                device_id_type=pl.DeviceIdType.MESH,
            )

        when(sends, lambda: describe(src, dst, index).start())
        issued.append(
            lambda: when(sends, lambda: describe(src, dst, index).wait_send())
        )
        return lambda inside=False: when(
            None if inside else receives,
            lambda: describe(landed, landed, hears).wait_recv(),
        )

    def wait(handles, *inside):
        for handle in handles:
            handle(*inside)

    def spread_z(own, split, view, steps):
        return {
            (h, t): send(
                split if t else own, view(row), view(z_row(-h, t)), {"row": z_row(h, t)}
            )
            for h, t in steps
        }

    def gather_h(view):
        return [
            send(view(pair), view(pair), view(y * m + at_h(-d)), h_peer(d))
            for d in range(1, m)
        ]

    def gather_y(view, h, up):
        handles = {}
        for d in near:
            if up is None:
                sends = receives = None
            elif up:
                sends, receives = y + d < n, y >= d
            else:
                sends, receives = y >= d, y + d < n
            s = -1 if up is False else 1
            mid = at_h(-h)
            handles[d] = send(
                view(y * m + mid),
                view(y * m + mid),
                view(at(y, -s * d) * m + mid),
                y_peer(s * d),
                sends,
                receives,
            )
        return handles

    def gather_full(arrived, view, up):
        handles = []
        for h in range(m):
            wait([arrived[step] for step in z_steps if step[0] == h and step in arrived])
            handles.append(gather_y(view, h, up))
        return {d: [piece[d] for piece in handles] for d in near}

    def k_view(i):
        return kf.at[block(i), :]

    def w_pair(i):
        return wf.at[pl.ds(2 * i, 2), mine, :]

    def w_group(i, part=mine):
        return wf.at[pl.ds(i * n, n), part, :]

    wait([load.wait for load in loads])
    pl.semaphore_wait(barrier, len(peers))

    w_z = spread_z(
        wf.at[row, mine, :], ws.at[mine, :], lambda i: wf.at[i, mine, :], z_steps
    )
    g_s = send(gt.at[:, own_lanes], gt.at[:, own_lanes], gt.at[:, other_lanes], twin)
    k_z = spread_z(kf.at[block(row), :], ks, lambda i: kf.at[block(i), :], z_steps)
    q_s = spread_z(qf.at[block(row), :], qs, lambda i: qf.at[block(i), :], z_steps[:1])
    v_z = spread_z(vf.at[block(row), :], vs, lambda i: vf.at[block(i), :], z_steps)

    w_y = gather_full(w_z, w_pair, None)
    w_d = {0: send(w_group(y), w_group(y), w_group(y, theirs), dp_peer)}
    k_y = gather_full(k_z, lambda i: kf.at[span_of(i), :], True)
    v_y = gather_full(v_z, lambda i: vf.at[span_of(i), :], True)
    g_s()
    gf[...] = flip(gt[...])

    h_x = {}

    def head_terms(d):
        w_d[d]()
        for e in far + [0]:
            hs[d, e] = dot(gf[...], wf[at(y, d) * n + at(x, e)]).astype(BF16)
            if e:
                h_x[d, e] = send(
                    hs.at[d, e], hx.at[d, e - 1], hx.at[d, e - 1], x_peer(e)
                )

    u_base = take(n)

    def head_sums(d):
        total = hs[d, 0].astype(F32)
        for e in far:
            h_x[d, e]()
            total = total + hx[d, e - 1].astype(F32)
        hz[d] = total.astype(BF16)
        target = at(y, d)
        e = lax.rem(target - u + n, n)
        send(
            hz.at[d],
            hr.at[e],
            hr.at[e],
            {"col": target * n + x},
            target != u,
            index=u_base + e,
        )

    head_terms(0)

    query_pos = pair * span + lax.broadcasted_iota(jnp.int32, (span, chunk), 0)
    key_pos = y * chunk + lax.broadcasted_iota(jnp.int32, (span, chunk), 1)

    def forward(j, first):
        scores = dot_nt(qf[span_of(pair), :], kf[group(j), :]) * SCALE
        if first:
            scores = jnp.where(key_pos <= query_pos, scores, NEG)
        new_top = jnp.max(scores, axis=1, keepdims=True)
        if not first:
            top = top_ref[:, :1]
            new_top = jnp.maximum(top, new_top)
        weights = jnp.exp(scores - new_top)
        total = jnp.sum(weights, axis=1, keepdims=True)
        acc = dot(weights.astype(BF16), vf[group(j), :])
        if not first:
            fade = jnp.exp(top - new_top)
            total = fade * sum_ref[:, :1] + total
            acc = fade * acc_ref[...] + acc
        top_ref[...] = jnp.broadcast_to(new_top, top_ref.shape)
        sum_ref[...] = jnp.broadcast_to(total, sum_ref.shape)
        acc_ref[...] = acc

    for d in near:
        wait(w_y[d])
        source = at(y, -d)
        w_d[n - d] = send(w_group(source), w_group(source), w_group(source, theirs), dp_peer)
    wait(q_s.values())
    forward(y, True)
    for d in near:
        head_terms(n - d)
    q_z = spread_z(qf.at[block(row), :], qs, lambda i: qf.at[block(i), :], z_steps[1:])
    head_sums(0)

    for d in near:

        @pl.when(y >= d)
        def _(d=d):
            wait(k_y[d], True)
            wait(v_y[d], True)
            forward(y - d, False)

    own_of = x * n + u
    total = sum_ref[:, :1]
    of[own_of] = (acc_ref[...] / total).astype(BF16)
    log_norm = top_ref[:, :1] + jnp.log(total)
    o_u = {
        d: send(of.at[own_of], of.at[own_of], of.at[x * n + at(u, -d)], u_peer(d))
        for d in far
    }

    def spread_x(e):
        return [
            send(
                of.at[x * n + at(u, -e)],
                of.at[x * n + at(u, -e)],
                of.at[at(x, -d) * n + at(u, -e)],
                x_peer(d),
            )
            for d in far
        ]

    o_x = spread_x(0)
    for d in near:
        head_sums(n - d)
    q_y = gather_full(q_z, lambda i: qf.at[span_of(i), :], False)

    for d in near:
        o_u[d]()
        o_x += spread_x(d)

    for e in others:
        pltpu.make_async_remote_copy(
            src_ref=hr.at[e],
            dst_ref=hr.at[e],
            send_sem=send_sems.at[u_base + e],
            recv_sem=recv_sems.at[u_base + e],
            device_id=u_peer(e),
            device_id_type=pl.DeviceIdType.MESH,
        ).wait_recv()
    upstream = hz[lax.rem(u - y + n, n)].astype(F32)
    for e in others:
        upstream = upstream + hr[e].astype(F32)
    df[span_of(pair), :] = upstream.astype(BF16)
    d_h = gather_h(lambda i: df.at[span_of(i), :])
    d_y = [gather_y(lambda i: df.at[span_of(i), :], 0, False)]
    attended = of[own_of].astype(F32)
    row_dot = jnp.sum(
        df[span_of(pair), :].astype(F32) * attended, axis=1, keepdims=True
    )
    lane = lax.broadcasted_iota(jnp.int32, (span, HEAD), 1)
    table = jnp.where(lane == 0, log_norm, jnp.where(lane == 1, row_dot, 0.0))
    st[:, span_of(pair)] = jnp.transpose(table)[:8, :]
    s_h = gather_h(lambda i: st.at[:, span_of(i)])
    s_y = [gather_y(lambda i: st.at[:, span_of(i)], 0, False)]

    for h in range(1, m):
        d_h[h - 1]()
        d_y.append(gather_y(lambda i: df.at[span_of(i), :], h, False))
        s_h[h - 1]()
        s_y.append(gather_y(lambda i: st.at[:, span_of(i)], h, False))

    wait(o_x)

    def weight_part(which, target_y):
        first = which * n * m + target_y * m
        for i in range(m):
            c = first + i
            part = dot(gt[...], of[lax.rem(c, n) * n + c // n])
            gp[c] = part.astype(BF16)

    g_d = {}
    for d in far + [0]:
        target_y = at(y, d)
        weight_part(1 - dp, target_y)
        away = pl.ds((1 - dp) * n * m + target_y * m, m)
        here = pl.ds(target_y * m, m)
        g_d[d] = send(gp.at[away], gd.at[here], gd.at[here], dp_peer)
    for d in far + [0]:
        weight_part(dp, at(y, d))

    g_y = []
    for d in far + [0]:
        target_y = at(y, d)
        g_d[d]()
        for i in range(m):
            slot = target_y * m + i
            gy[slot] = (
                gp[dp * n * m + slot].astype(F32) + gd[slot].astype(F32)
            ).astype(BF16)
        if d:
            here = pl.ds(target_y * m, m)
            g_y.append(send(gy.at[here], gyr.at[d - 1], gyr.at[d - 1], y_peer(d)))

    lanes = [slice(h * HEAD, (h + 1) * HEAD) for h in range(2)]

    def project(c, acc):
        return acc + dot_nt(wf[c], of[lax.rem(c, n) * n + c // n])

    projected = lax.fori_loop(0, n * n, project, jnp.zeros((cols, span), F32))
    for h in range(2):
        ox[h] = projected[:, lanes[h]].astype(BF16)
    o_s = send(ox.at[1 - side], oxr, oxr, twin)

    def queries_pass(j, first, acc):
        keys = kf[group(j), :]
        scores = dot_nt(qf[span_of(pair), :], keys) * SCALE
        probs = jnp.exp(scores - log_norm)
        if first:
            probs = jnp.where(key_pos <= query_pos, probs, 0.0)
        slopes = dot_nt(df[span_of(pair), :], vf[group(j), :])
        slopes = (probs * (slopes - row_dot)).astype(BF16)
        return acc + dot(slopes, keys)

    acc = queries_pass(y, True, jnp.zeros((span, HEAD), F32))
    acc = lax.fori_loop(0, y, lambda j, acc: queries_pass(j, False, acc), acc)
    acc = (acc * SCALE).astype(BF16)
    dx[0, 0], dx[0, 1] = acc[:rows], acc[rows:]
    swaps = [send(dx.at[0, 1 - side], dxr.at[0], dxr.at[0], twin)]

    wait(g_y)
    g_z = []
    for d in list(range(1, m)) + [0]:
        target = at_h(d)
        total = gy[y * m + target].astype(F32)
        for e in others:
            total = total + gyr[e - 1, target].astype(F32)
        gz[d] = total.astype(BF16)
        if d:
            g_z.append(send(gz.at[d], gzr.at[d - 1], gzr.at[d - 1], h_peer(d)))

    own_key = pair * span + lax.broadcasted_iota(jnp.int32, (span, chunk), 0)
    ask_pos = y * chunk + lax.broadcasted_iota(jnp.int32, (span, chunk), 1)

    def keys_pass(j, first):
        queries = qf[group(j), :]
        ups = df[group(j), :]
        norm = st[0:1, group(j)]
        away = st[1:2, group(j)]
        scores = dot_nt(kf[span_of(pair), :], queries) * SCALE
        probs = jnp.exp(scores - norm)
        if first:
            probs = jnp.where(ask_pos >= own_key, probs, 0.0)
        slopes = dot_nt(vf[span_of(pair), :], ups)
        slopes = (probs * (slopes - away)).astype(BF16)
        sum_k, sum_v = dot(slopes, queries), dot(probs.astype(BF16), ups)
        if first:
            acc_ref[...], sum_ref[...] = sum_k, sum_v
        else:
            acc_ref[...] += sum_k
            sum_ref[...] += sum_v

    keys_pass(y, True)
    for d in near:

        @pl.when(y + d < n)
        def _(d=d):
            wait(q_y[d], True)
            for h in range(m):
                d_y[h][d](True)
                s_y[h][d](True)
            keys_pass(y + d, False)

    for i, value in ((1, acc_ref[...] * SCALE), (2, sum_ref[...])):
        value = value.astype(BF16)
        dx[i, 0], dx[i, 1] = value[:rows], value[rows:]
        swaps.append(send(dx.at[i, 1 - side], dxr.at[i], dxr.at[i], twin))

    wait(g_z)
    total = gz[0].astype(F32)
    for d in range(1, m):
        total = total + gzr[d - 1].astype(F32)
    gw_ref[...] = total
    o_s()
    out_ref[...] = (ox[side].astype(F32) + oxr[...].astype(F32)).astype(BF16)
    for i, target in enumerate((dq_ref, dk_ref, dv_ref)):
        swaps[i]()
        own, other = dx[i, side], dxr[i]
        for h in range(2):
            target[:, lanes[h]] = jnp.where(side == h, own, other)

    for finish in issued:
        finish()


def store_all(*refs):
    count = len(refs) // 2
    copies = [
        pltpu.make_async_copy(refs[i], refs[count + i], refs[-1].at[i])
        for i in range(count)
    ]
    for copy in copies:
        copy.start()
    for copy in copies:
        copy.wait()


def shards(n, queries, key_vectors, value_vectors, out_weight, out_grad):
    rows, width = queries.shape[1:]
    cols = out_grad.shape[2]
    blocks, m = n * n, n // 2
    copies = 112
    vmem = pl.BlockSpec(memory_space=pltpu.VMEM)

    def buffer(*shape, kind=BF16):
        return pltpu.VMEM(shape, kind)

    full = buffer(blocks * rows, HEAD)
    span = 2 * rows
    result = pl.pallas_call(
        functools.partial(kernel, n, rows, cols),
        out_shape=(
            jax.ShapeDtypeStruct((cols, rows), BF16),
            jax.ShapeDtypeStruct((rows, width), BF16),
            jax.ShapeDtypeStruct((rows, width), BF16),
            jax.ShapeDtypeStruct((rows, width), BF16),
            jax.ShapeDtypeStruct((cols, HEAD), F32),
        ),
        in_specs=[pl.BlockSpec(memory_space=pltpu.HBM)] * 5,
        out_specs=(vmem,) * 5,
        scratch_shapes=[
            buffer(rows, HEAD),
            buffer(rows, HEAD),
            buffer(rows, HEAD),
            buffer(cols, HEAD),
            full,
            full,
            full,
            full,
            buffer(8, blocks * rows, kind=F32),
            buffer(blocks, cols, HEAD),
            buffer(span, cols),
            buffer(cols, span),
            buffer(n, n, span, HEAD),
            buffer(n, n - 1, span, HEAD),
            buffer(n, span, HEAD),
            buffer(n, span, HEAD),
            buffer(blocks, span, HEAD),
            buffer(span, HEAD, kind=F32),
            buffer(span, HEAD, kind=F32),
            buffer(span, HEAD, kind=F32),
            buffer(blocks, cols, HEAD),
            buffer(n * m, cols, HEAD),
            buffer(n * m, cols, HEAD),
            buffer(n - 1, m, cols, HEAD),
            buffer(m, cols, HEAD),
            buffer(max(m - 1, 1), cols, HEAD),
            buffer(2, cols, rows),
            buffer(cols, rows),
            buffer(3, 2, rows, HEAD),
            buffer(3, rows, HEAD),
            pltpu.SemaphoreType.DMA((9,)),
            pltpu.SemaphoreType.DMA((copies,)),
            pltpu.SemaphoreType.DMA((copies,)),
        ],
        compiler_params=pltpu.CompilerParams(
            collective_id=0, has_side_effects=True, vmem_limit_bytes=48 << 20
        ),
    )(queries[0], key_vectors[0], value_vectors[0], out_weight.T, out_grad[0].T)
    result = pl.pallas_call(
        store_all,
        out_shape=[jax.ShapeDtypeStruct(a.shape, a.dtype) for a in result],
        in_specs=[vmem] * 5,
        out_specs=[pl.BlockSpec(memory_space=pltpu.HBM)] * 5,
        scratch_shapes=[pltpu.SemaphoreType.DMA((5,))],
    )(*result)
    output, grad_queries, grad_keys, grad_values, grad_weight = result
    return (
        output.T[None],
        grad_queries[None],
        grad_keys[None],
        grad_values[None],
        grad_weight.T,
    )


def solution(mesh):
    n = math.isqrt(mesh.shape["row"])
    return jax.shard_map(
        functools.partial(shards, n),
        mesh=mesh,
        in_specs=(
            P("dp", "row", "col"),
            P("dp", "row", "col"),
            P("dp", "row", "col"),
            P("row", "col"),
            P("dp", "row", "col"),
        ),
        out_specs=(
            P("dp", "row", "col"),
            P("dp", "row", "col"),
            P("dp", "row", "col"),
            P("dp", "row", "col"),
            P(("dp", "row"), "col"),
        ),
        check_vma=False,
    )
```

```python
import functools
import math

import jax
import jax.numpy as jnp
from jax import lax
from jax.experimental import pallas as pl
from jax.experimental.pallas import tpu as pltpu
from jax.sharding import PartitionSpec as P

HEAD = 128
NEG = -1e30
SCALE = 1.0 / math.sqrt(HEAD)
F32 = jnp.float32
BF16 = jnp.bfloat16
NT = (((1,), (1,)), ((), ()))
TN = (((0,), (0,)), ((), ()))


def dot(a, b):
    return jnp.dot(a, b, preferred_element_type=F32)


def dot_nt(a, b):
    return lax.dot_general(a, b, NT, preferred_element_type=F32)


def flip(a):
    size = a.shape[0]
    eye = (
        lax.broadcasted_iota(jnp.int32, (size, size), 0)
        == lax.broadcasted_iota(jnp.int32, (size, size), 1)
    )
    eye = jnp.where(eye, 1.0, 0.0).astype(BF16)
    return lax.dot_general(a, eye, TN, preferred_element_type=F32).astype(BF16)


def kernel(
    n,
    rows,
    cols,
    q_hbm,
    k_hbm,
    v_hbm,
    w_hbm,
    g_hbm,
    out_ref,
    dq_ref,
    dk_ref,
    dv_ref,
    gw_ref,
    qs,
    ks,
    vs,
    ws,
    kf,
    vf,
    qf,
    df,
    st,
    wf,
    gf,
    gt,
    hs,
    hx,
    hz,
    hr,
    of,
    top_ref,
    sum_ref,
    acc_ref,
    gp,
    gd,
    gy,
    gyr,
    gz,
    gzr,
    ox,
    oxr,
    dx,
    dxr,
    load_sems,
    send_sems,
    recv_sems,
):
    dp, row, col = lax.axis_index("dp"), lax.axis_index("row"), lax.axis_index("col")
    m = n // 2
    y, z = row // n, lax.rem(row, n)
    zh, side = z // 2, lax.rem(z, 2)
    u, x = col // n, lax.rem(col, n)
    pair = y * m + zh
    span = 2 * rows
    chunk = n * rows
    others = list(range(1, n))
    far = sorted(others, key=lambda d: -min(d, n - d))
    near = far[::-1]
    z_steps = [(h, t) for h in range(m) for t in (1, 0) if h or t]

    def at(base, d):
        return lax.rem(base + d + n, n)

    def at_h(d):
        return lax.rem(zh + d + m, m)

    dp_peer = {"dp": 1 - dp}
    twin = {"row": row + 1 - 2 * side}

    def z_row(h, t):
        return y * n + 2 * at_h(h) + (1 - side if t else side)

    def h_peer(d):
        return {"row": z_row(d, 0)}

    def y_peer(d):
        return {"row": at(y, d) * n + z}

    def u_peer(d):
        return {"col": at(u, d) * n + x}

    def x_peer(d):
        return {"col": u * n + at(x, d)}

    def block(i):
        return pl.ds(pl.multiple_of(i * rows, rows), rows)

    def span_of(i):
        return pl.ds(pl.multiple_of(i * span, span), span)

    def group(i):
        return pl.ds(pl.multiple_of(i * chunk, chunk), chunk)

    half = cols // 2
    mine = pl.ds(pl.multiple_of(dp * half, half), half)
    theirs = pl.ds(pl.multiple_of((1 - dp) * half, half), half)
    own_lanes = block(side)
    other_lanes = block(1 - side)

    pieces = [
        (w_hbm.at[mine, own_lanes], wf.at[row, mine, :]),
        (w_hbm.at[mine, other_lanes], ws.at[mine, :]),
        (g_hbm, gt.at[:, own_lanes]),
    ]
    for source, split, full in ((k_hbm, ks, kf), (q_hbm, qs, qf), (v_hbm, vs, vf)):
        pieces.append((source.at[:, own_lanes], full.at[block(row), :]))
        pieces.append((source.at[:, other_lanes], split))
    loads = [
        pltpu.make_async_copy(source, target, load_sems.at[i])
        for i, (source, target) in enumerate(pieces)
    ]

    barrier = pltpu.get_barrier_semaphore()
    peers = [dp_peer] + [{"row": z_row(h, t)} for h, t in z_steps]
    peers += [f(d) for f in (u_peer, y_peer, x_peer) for d in far]
    for peer in peers:
        pl.semaphore_signal(
            barrier, inc=1, device_id=peer, device_id_type=pl.DeviceIdType.MESH
        )
    for load in loads:
        load.start()

    issued = []
    slots = [0]

    def when(cond, body):
        if cond is None:
            body()
        else:
            pl.when(cond)(body)

    def take(count):
        slots[0] += count
        return slots[0] - count

    def send(src, dst, landed, peer, sends=None, receives=None, index=None):
        index = take(1) if index is None else index

        def describe(source, target, which):
            return pltpu.make_async_remote_copy(
                src_ref=source,
                dst_ref=target,
                send_sem=send_sems.at[which],
                recv_sem=recv_sems.at[which],
                device_id=peer,
                device_id_type=pl.DeviceIdType.MESH,
            )

        when(sends, lambda: describe(src, dst, index).start())
        issued.append(
            lambda: when(sends, lambda: describe(src, dst, index).wait_send())
        )
        if landed is None:
            return None
        return lambda inside=False: when(
            None if inside else receives,
            lambda: describe(landed, landed, index).wait_recv(),
        )

    def wait(handles, *inside):
        for handle in handles:
            handle(*inside)

    def spread_z(own, split, view, steps):
        return {
            (h, t): send(
                split if t else own, view(row), view(z_row(-h, t)), {"row": z_row(h, t)}
            )
            for h, t in steps
        }

    def gather_h(view):
        return [
            send(view(pair), view(pair), view(y * m + at_h(-d)), h_peer(d))
            for d in range(1, m)
        ]

    def gather_y(view, h, up):
        handles = {}
        for d in near:
            if up is None:
                sends = receives = None
            elif up:
                sends, receives = y + d < n, y >= d
            else:
                sends, receives = y >= d, y + d < n
            s = -1 if up is False else 1
            mid = at_h(-h)
            handles[d] = send(
                view(y * m + mid),
                view(y * m + mid),
                view(at(y, -s * d) * m + mid),
                y_peer(s * d),
                sends,
                receives,
            )
        return handles

    def gather_full(arrived, view, up):
        handles = []
        for h in range(m):
            wait([arrived[step] for step in z_steps if step[0] == h and step in arrived])
            handles.append(gather_y(view, h, up))
        return {d: [piece[d] for piece in handles] for d in near}

    def k_view(i):
        return kf.at[block(i), :]

    def w_pair(i):
        return wf.at[pl.ds(2 * i, 2), mine, :]

    def w_group(i, part=mine):
        return wf.at[pl.ds(i * n, n), part, :]

    wait([load.wait for load in loads])
    pl.semaphore_wait(barrier, len(peers))

    w_z = spread_z(
        wf.at[row, mine, :], ws.at[mine, :], lambda i: wf.at[i, mine, :], z_steps
    )
    g_s = send(gt.at[:, own_lanes], gt.at[:, own_lanes], gt.at[:, other_lanes], twin)
    k_z = spread_z(kf.at[block(row), :], ks, lambda i: kf.at[block(i), :], z_steps)
    q_s = spread_z(qf.at[block(row), :], qs, lambda i: qf.at[block(i), :], z_steps[:1])
    v_z = spread_z(vf.at[block(row), :], vs, lambda i: vf.at[block(i), :], z_steps)

    w_y = gather_full(w_z, w_pair, None)
    w_d = {0: send(w_group(y), w_group(y), w_group(y, theirs), dp_peer)}
    k_y = gather_full(k_z, lambda i: kf.at[span_of(i), :], True)
    v_y = gather_full(v_z, lambda i: vf.at[span_of(i), :], True)
    g_s()
    gf[...] = flip(gt[...])

    h_x = {}

    def head_terms(d):
        w_d[d]()
        for e in far + [0]:
            hs[d, e] = dot(gf[...], wf[at(y, d) * n + at(x, e)]).astype(BF16)
            if e:
                h_x[d, e] = send(
                    hs.at[d, e], hx.at[d, e - 1], hx.at[d, e - 1], x_peer(e)
                )

    u_base = take(n)

    def head_sums(d):
        total = hs[d, 0].astype(F32)
        for e in far:
            h_x[d, e]()
            total = total + hx[d, e - 1].astype(F32)
        hz[d] = total.astype(BF16)
        target = at(y, d)
        e = lax.rem(target - u + n, n)
        send(
            hz.at[d],
            hr.at[e],
            None,
            {"col": target * n + x},
            target != u,
            index=u_base + e,
        )

    head_terms(0)

    query_pos = pair * span + lax.broadcasted_iota(jnp.int32, (span, chunk), 0)
    key_pos = y * chunk + lax.broadcasted_iota(jnp.int32, (span, chunk), 1)

    def forward(j, first):
        scores = dot_nt(qf[span_of(pair), :], kf[group(j), :]) * SCALE
        if first:
            scores = jnp.where(key_pos <= query_pos, scores, NEG)
        new_top = jnp.max(scores, axis=1, keepdims=True)
        if not first:
            top = top_ref[:, :1]
            new_top = jnp.maximum(top, new_top)
        weights = jnp.exp(scores - new_top)
        total = jnp.sum(weights, axis=1, keepdims=True)
        acc = dot(weights.astype(BF16), vf[group(j), :])
        if not first:
            fade = jnp.exp(top - new_top)
            total = fade * sum_ref[:, :1] + total
            acc = fade * acc_ref[...] + acc
        top_ref[...] = jnp.broadcast_to(new_top, top_ref.shape)
        sum_ref[...] = jnp.broadcast_to(total, sum_ref.shape)
        acc_ref[...] = acc

    for d in near:
        wait(w_y[d])
        source = at(y, -d)
        w_d[n - d] = send(w_group(source), w_group(source), w_group(source, theirs), dp_peer)
    wait(q_s.values())
    forward(y, True)
    for d in near:
        head_terms(n - d)
    q_z = spread_z(qf.at[block(row), :], qs, lambda i: qf.at[block(i), :], z_steps[1:])
    head_sums(0)

    for d in near:

        @pl.when(y >= d)
        def _(d=d):
            wait(k_y[d], True)
            wait(v_y[d], True)
            forward(y - d, False)

    own_of = x * n + u
    total = sum_ref[:, :1]
    of[own_of] = (acc_ref[...] / total).astype(BF16)
    log_norm = top_ref[:, :1] + jnp.log(total)
    o_u = {
        d: send(of.at[own_of], of.at[own_of], of.at[x * n + at(u, -d)], u_peer(d))
        for d in far
    }

    def spread_x(e):
        return [
            send(
                of.at[x * n + at(u, -e)],
                of.at[x * n + at(u, -e)],
                of.at[at(x, -d) * n + at(u, -e)],
                x_peer(d),
            )
            for d in far
        ]

    o_x = spread_x(0)
    for d in near:
        head_sums(n - d)
    q_y = gather_full(q_z, lambda i: qf.at[span_of(i), :], False)

    for d in near:
        o_u[d]()
        o_x += spread_x(d)

    for e in others:
        pltpu.make_async_remote_copy(
            src_ref=hr.at[e],
            dst_ref=hr.at[e],
            send_sem=send_sems.at[u_base + e],
            recv_sem=recv_sems.at[u_base + e],
            device_id=u_peer(e),
            device_id_type=pl.DeviceIdType.MESH,
        ).wait_recv()
    upstream = hz[lax.rem(u - y + n, n)].astype(F32)
    for e in others:
        upstream = upstream + hr[e].astype(F32)
    df[span_of(pair), :] = upstream.astype(BF16)
    d_h = gather_h(lambda i: df.at[span_of(i), :])
    d_y = [gather_y(lambda i: df.at[span_of(i), :], 0, False)]
    attended = of[own_of].astype(F32)
    row_dot = jnp.sum(
        df[span_of(pair), :].astype(F32) * attended, axis=1, keepdims=True
    )
    lane = lax.broadcasted_iota(jnp.int32, (span, HEAD), 1)
    table = jnp.where(lane == 0, log_norm, jnp.where(lane == 1, row_dot, 0.0))
    st[:, span_of(pair)] = jnp.transpose(table)[:8, :]
    s_h = gather_h(lambda i: st.at[:, span_of(i)])
    s_y = [gather_y(lambda i: st.at[:, span_of(i)], 0, False)]

    for h in range(1, m):
        d_h[h - 1]()
        d_y.append(gather_y(lambda i: df.at[span_of(i), :], h, False))
        s_h[h - 1]()
        s_y.append(gather_y(lambda i: st.at[:, span_of(i)], h, False))

    wait(o_x)

    def weight_part(which, target_y):
        first = which * n * m + target_y * m
        for i in range(m):
            c = first + i
            part = dot(gt[...], of[lax.rem(c, n) * n + c // n])
            gp[c] = part.astype(BF16)

    g_d = {}
    for d in far + [0]:
        target_y = at(y, d)
        weight_part(1 - dp, target_y)
        away = pl.ds((1 - dp) * n * m + target_y * m, m)
        here = pl.ds(target_y * m, m)
        g_d[d] = send(gp.at[away], gd.at[here], gd.at[here], dp_peer)
    for d in far + [0]:
        weight_part(dp, at(y, d))

    g_y = []
    for d in far + [0]:
        target_y = at(y, d)
        g_d[d]()
        for i in range(m):
            slot = target_y * m + i
            gy[slot] = (
                gp[dp * n * m + slot].astype(F32) + gd[slot].astype(F32)
            ).astype(BF16)
        if d:
            here = pl.ds(target_y * m, m)
            g_y.append(send(gy.at[here], gyr.at[d - 1], gyr.at[d - 1], y_peer(d)))

    lanes = [slice(h * HEAD, (h + 1) * HEAD) for h in range(2)]

    def project(c, acc):
        return acc + dot_nt(wf[c], of[lax.rem(c, n) * n + c // n])

    projected = lax.fori_loop(0, n * n, project, jnp.zeros((cols, span), F32))
    for h in range(2):
        ox[h] = projected[:, lanes[h]].astype(BF16)
    o_s = send(ox.at[1 - side], oxr, oxr, twin)

    def queries_pass(j, first, acc):
        keys = kf[group(j), :]
        scores = dot_nt(qf[span_of(pair), :], keys) * SCALE
        probs = jnp.exp(scores - log_norm)
        if first:
            probs = jnp.where(key_pos <= query_pos, probs, 0.0)
        slopes = dot_nt(df[span_of(pair), :], vf[group(j), :])
        slopes = (probs * (slopes - row_dot)).astype(BF16)
        return acc + dot(slopes, keys)

    acc = queries_pass(y, True, jnp.zeros((span, HEAD), F32))
    acc = lax.fori_loop(0, y, lambda j, acc: queries_pass(j, False, acc), acc)
    acc = (acc * SCALE).astype(BF16)
    dx[0, 0], dx[0, 1] = acc[:rows], acc[rows:]
    swaps = [send(dx.at[0, 1 - side], dxr.at[0], dxr.at[0], twin)]

    wait(g_y)
    g_z = []
    for d in list(range(1, m)) + [0]:
        target = at_h(d)
        total = gy[y * m + target].astype(F32)
        for e in others:
            total = total + gyr[e - 1, target].astype(F32)
        gz[d] = total.astype(BF16)
        if d:
            g_z.append(send(gz.at[d], gzr.at[d - 1], gzr.at[d - 1], h_peer(d)))

    own_key = pair * span + lax.broadcasted_iota(jnp.int32, (span, chunk), 0)
    ask_pos = y * chunk + lax.broadcasted_iota(jnp.int32, (span, chunk), 1)

    def keys_pass(j, first):
        queries = qf[group(j), :]
        ups = df[group(j), :]
        norm = st[0:1, group(j)]
        away = st[1:2, group(j)]
        scores = dot_nt(kf[span_of(pair), :], queries) * SCALE
        probs = jnp.exp(scores - norm)
        if first:
            probs = jnp.where(ask_pos >= own_key, probs, 0.0)
        slopes = dot_nt(vf[span_of(pair), :], ups)
        slopes = (probs * (slopes - away)).astype(BF16)
        sum_k, sum_v = dot(slopes, queries), dot(probs.astype(BF16), ups)
        if first:
            acc_ref[...], sum_ref[...] = sum_k, sum_v
        else:
            acc_ref[...] += sum_k
            sum_ref[...] += sum_v

    keys_pass(y, True)
    for d in near:

        @pl.when(y + d < n)
        def _(d=d):
            wait(q_y[d], True)
            for h in range(m):
                d_y[h][d](True)
                s_y[h][d](True)
            keys_pass(y + d, False)

    for i, value in ((1, acc_ref[...] * SCALE), (2, sum_ref[...])):
        value = value.astype(BF16)
        dx[i, 0], dx[i, 1] = value[:rows], value[rows:]
        swaps.append(send(dx.at[i, 1 - side], dxr.at[i], dxr.at[i], twin))

    wait(g_z)
    total = gz[0].astype(F32)
    for d in range(1, m):
        total = total + gzr[d - 1].astype(F32)
    gw_ref[...] = total
    o_s()
    out_ref[...] = (ox[side].astype(F32) + oxr[...].astype(F32)).astype(BF16)
    for i, target in enumerate((dq_ref, dk_ref, dv_ref)):
        swaps[i]()
        own, other = dx[i, side], dxr[i]
        for h in range(2):
            target[:, lanes[h]] = jnp.where(side == h, own, other)

    for finish in issued:
        finish()


def store_all(*refs):
    count = len(refs) // 2
    copies = [
        pltpu.make_async_copy(refs[i], refs[count + i], refs[-1].at[i])
        for i in range(count)
    ]
    for copy in copies:
        copy.start()
    for copy in copies:
        copy.wait()


def shards(n, queries, key_vectors, value_vectors, out_weight, out_grad):
    rows, width = queries.shape[1:]
    cols = out_grad.shape[2]
    blocks, m = n * n, n // 2
    copies = 112
    vmem = pl.BlockSpec(memory_space=pltpu.VMEM)

    def buffer(*shape, kind=BF16):
        return pltpu.VMEM(shape, kind)

    full = buffer(blocks * rows, HEAD)
    span = 2 * rows
    result = pl.pallas_call(
        functools.partial(kernel, n, rows, cols),
        out_shape=(
            jax.ShapeDtypeStruct((cols, rows), BF16),
            jax.ShapeDtypeStruct((rows, width), BF16),
            jax.ShapeDtypeStruct((rows, width), BF16),
            jax.ShapeDtypeStruct((rows, width), BF16),
            jax.ShapeDtypeStruct((cols, HEAD), F32),
        ),
        in_specs=[pl.BlockSpec(memory_space=pltpu.HBM)] * 5,
        out_specs=(vmem,) * 5,
        scratch_shapes=[
            buffer(rows, HEAD),
            buffer(rows, HEAD),
            buffer(rows, HEAD),
            buffer(cols, HEAD),
            full,
            full,
            full,
            full,
            buffer(8, blocks * rows, kind=F32),
            buffer(blocks, cols, HEAD),
            buffer(span, cols),
            buffer(cols, span),
            buffer(n, n, span, HEAD),
            buffer(n, n - 1, span, HEAD),
            buffer(n, span, HEAD),
            buffer(n, span, HEAD),
            buffer(blocks, span, HEAD),
            buffer(span, HEAD, kind=F32),
            buffer(span, HEAD, kind=F32),
            buffer(span, HEAD, kind=F32),
            buffer(blocks, cols, HEAD),
            buffer(n * m, cols, HEAD),
            buffer(n * m, cols, HEAD),
            buffer(n - 1, m, cols, HEAD),
            buffer(m, cols, HEAD),
            buffer(max(m - 1, 1), cols, HEAD),
            buffer(2, cols, rows),
            buffer(cols, rows),
            buffer(3, 2, rows, HEAD),
            buffer(3, rows, HEAD),
            pltpu.SemaphoreType.DMA((9,)),
            pltpu.SemaphoreType.DMA((copies,)),
            pltpu.SemaphoreType.DMA((copies,)),
        ],
        compiler_params=pltpu.CompilerParams(
            collective_id=0, has_side_effects=True, vmem_limit_bytes=64 << 20
        ),
    )(queries[0], key_vectors[0], value_vectors[0], out_weight.T, out_grad[0].T)
    result = pl.pallas_call(
        store_all,
        out_shape=[jax.ShapeDtypeStruct(a.shape, a.dtype) for a in result],
        in_specs=[vmem] * 5,
        out_specs=[pl.BlockSpec(memory_space=pltpu.HBM)] * 5,
        scratch_shapes=[pltpu.SemaphoreType.DMA((5,))],
    )(*result)
    output, grad_queries, grad_keys, grad_values, grad_weight = result
    return (
        output.T[None],
        grad_queries[None],
        grad_keys[None],
        grad_values[None],
        grad_weight.T,
    )


def solution(mesh):
    n = math.isqrt(mesh.shape["row"])
    return jax.shard_map(
        functools.partial(shards, n),
        mesh=mesh,
        in_specs=(
            P("dp", "row", "col"),
            P("dp", "row", "col"),
            P("dp", "row", "col"),
            P("row", "col"),
            P("dp", "row", "col"),
        ),
        out_specs=(
            P("dp", "row", "col"),
            P("dp", "row", "col"),
            P("dp", "row", "col"),
            P("dp", "row", "col"),
            P(("dp", "row"), "col"),
        ),
        check_vma=False,
    )
```

```python
import functools
import math

import jax
import jax.numpy as jnp
from jax import lax
from jax.experimental import pallas as pl
from jax.experimental.pallas import tpu as pltpu
from jax.sharding import PartitionSpec as P

HEAD = 128
NEG = -1e30
SCALE = 1.0 / math.sqrt(HEAD)
F32 = jnp.float32
BF16 = jnp.bfloat16
NT = (((1,), (1,)), ((), ()))
TN = (((0,), (0,)), ((), ()))


def dot(a, b):
    return jnp.dot(a, b, preferred_element_type=F32)


def dot_nt(a, b):
    return lax.dot_general(a, b, NT, preferred_element_type=F32)


def flip(a):
    size = a.shape[0]
    eye = (
        lax.broadcasted_iota(jnp.int32, (size, size), 0)
        == lax.broadcasted_iota(jnp.int32, (size, size), 1)
    )
    eye = jnp.where(eye, 1.0, 0.0).astype(BF16)
    return lax.dot_general(a, eye, TN, preferred_element_type=F32).astype(BF16)


def kernel(
    n,
    rows,
    cols,
    q_hbm,
    k_hbm,
    v_hbm,
    w_hbm,
    g_hbm,
    out_ref,
    dq_ref,
    dk_ref,
    dv_ref,
    gw_ref,
    qs,
    ks,
    vs,
    ws,
    kf,
    vf,
    qf,
    df,
    st,
    wf,
    gf,
    gt,
    hs,
    hx,
    hz,
    hr,
    hq,
    of,
    top_ref,
    sum_ref,
    acc_ref,
    gp,
    gd,
    gy,
    gyr,
    gz,
    gzr,
    ox,
    oxr,
    dx,
    dxr,
    load_sems,
    send_sems,
    recv_sems,
):
    dp, row, col = lax.axis_index("dp"), lax.axis_index("row"), lax.axis_index("col")
    m = n // 2
    y, z = row // n, lax.rem(row, n)
    zh, side = z // 2, lax.rem(z, 2)
    u, x = col // n, lax.rem(col, n)
    pair = y * m + zh
    span = 2 * rows
    chunk = n * rows
    others = list(range(1, n))
    far = sorted(others, key=lambda d: -min(d, n - d))
    near = far[::-1]
    z_steps = [(h, t) for h in range(m) for t in (1, 0) if h or t]

    def at(base, d):
        return lax.rem(base + d + n, n)

    def at_h(d):
        return lax.rem(zh + d + m, m)

    dp_peer = {"dp": 1 - dp}
    twin = {"row": row + 1 - 2 * side}

    def z_row(h, t):
        return y * n + 2 * at_h(h) + (1 - side if t else side)

    def h_peer(d):
        return {"row": z_row(d, 0)}

    def y_peer(d):
        return {"row": at(y, d) * n + z}

    def u_peer(d):
        return {"col": at(u, d) * n + x}

    def x_peer(d):
        return {"col": u * n + at(x, d)}

    def block(i):
        return pl.ds(pl.multiple_of(i * rows, rows), rows)

    def span_of(i):
        return pl.ds(pl.multiple_of(i * span, span), span)

    def group(i):
        return pl.ds(pl.multiple_of(i * chunk, chunk), chunk)

    half = cols // 2
    mine = pl.ds(pl.multiple_of(dp * half, half), half)
    theirs = pl.ds(pl.multiple_of((1 - dp) * half, half), half)
    own_lanes = block(side)
    other_lanes = block(1 - side)

    pieces = [
        (w_hbm.at[mine, own_lanes], wf.at[row, mine, :]),
        (w_hbm.at[mine, other_lanes], ws.at[mine, :]),
        (g_hbm, gt.at[:, own_lanes]),
    ]
    for source, split, full in ((k_hbm, ks, kf), (q_hbm, qs, qf), (v_hbm, vs, vf)):
        pieces.append((source.at[:, own_lanes], full.at[block(row), :]))
        pieces.append((source.at[:, other_lanes], split))
    loads = [
        pltpu.make_async_copy(source, target, load_sems.at[i])
        for i, (source, target) in enumerate(pieces)
    ]

    barrier = pltpu.get_barrier_semaphore()
    peers = [dp_peer] + [{"row": z_row(h, t)} for h, t in z_steps]
    peers += [u_peer(d) for d in sorted({1, n - 1})]
    peers += [f(d) for f in (y_peer, x_peer) for d in far]
    for peer in peers:
        pl.semaphore_signal(
            barrier, inc=1, device_id=peer, device_id_type=pl.DeviceIdType.MESH
        )
    for load in loads:
        load.start()

    issued = []
    slots = [0]

    def when(cond, body):
        if cond is None:
            body()
        else:
            pl.when(cond)(body)

    def take(count):
        slots[0] += count
        return slots[0] - count

    def send(src, dst, landed, peer, sends=None, receives=None, index=None):
        index = take(1) if index is None else index

        def describe(source, target, which):
            return pltpu.make_async_remote_copy(
                src_ref=source,
                dst_ref=target,
                send_sem=send_sems.at[which],
                recv_sem=recv_sems.at[which],
                device_id=peer,
                device_id_type=pl.DeviceIdType.MESH,
            )

        when(sends, lambda: describe(src, dst, index).start())
        issued.append(
            lambda: when(sends, lambda: describe(src, dst, index).wait_send())
        )
        if landed is None:
            return None
        return lambda inside=False: when(
            None if inside else receives,
            lambda: describe(landed, landed, index).wait_recv(),
        )

    def wait(handles, *inside):
        for handle in handles:
            handle(*inside)

    def spread_z(own, split, view, steps):
        return {
            (h, t): send(
                split if t else own, view(row), view(z_row(-h, t)), {"row": z_row(h, t)}
            )
            for h, t in steps
        }

    def gather_h(view):
        return [
            send(view(pair), view(pair), view(y * m + at_h(-d)), h_peer(d))
            for d in range(1, m)
        ]

    def gather_y(view, h, up):
        handles = {}
        for d in near:
            if up is None:
                sends = receives = None
            elif up:
                sends, receives = y + d < n, y >= d
            else:
                sends, receives = y >= d, y + d < n
            s = -1 if up is False else 1
            mid = at_h(-h)
            handles[d] = send(
                view(y * m + mid),
                view(y * m + mid),
                view(at(y, -s * d) * m + mid),
                y_peer(s * d),
                sends,
                receives,
            )
        return handles

    def gather_full(arrived, view, up):
        handles = []
        for h in range(m):
            wait([arrived[step] for step in z_steps if step[0] == h and step in arrived])
            handles.append(gather_y(view, h, up))
        return {d: [piece[d] for piece in handles] for d in near}

    def k_view(i):
        return kf.at[block(i), :]

    def w_pair(i):
        return wf.at[pl.ds(2 * i, 2), mine, :]

    def w_group(i, part=mine):
        return wf.at[pl.ds(i * n, n), part, :]

    wait([load.wait for load in loads])
    pl.semaphore_wait(barrier, len(peers))

    w_z = spread_z(
        wf.at[row, mine, :], ws.at[mine, :], lambda i: wf.at[i, mine, :], z_steps
    )
    g_s = send(gt.at[:, own_lanes], gt.at[:, own_lanes], gt.at[:, other_lanes], twin)
    k_z = spread_z(kf.at[block(row), :], ks, lambda i: kf.at[block(i), :], z_steps)
    q_s = spread_z(qf.at[block(row), :], qs, lambda i: qf.at[block(i), :], z_steps[:1])
    v_z = spread_z(vf.at[block(row), :], vs, lambda i: vf.at[block(i), :], z_steps)

    w_y = gather_full(w_z, w_pair, None)
    w_d = {0: send(w_group(y), w_group(y), w_group(y, theirs), dp_peer)}
    k_y = gather_full(k_z, lambda i: kf.at[span_of(i), :], True)
    v_y = gather_full(v_z, lambda i: vf.at[span_of(i), :], True)
    g_s()
    gf[...] = flip(gt[...])

    x_base = take(n * (n - 1))

    def x_send(d, e):
        index = x_base + d * (n - 1) + e - 1
        send(hs.at[d, e], hx.at[d, e - 1], None, x_peer(e), index=index)

    def head_terms(d):
        w_d[d]()
        for e in far + [0]:
            hs[d, e] = dot(gf[...], wf[at(y, d) * n + at(x, e)]).astype(BF16)
            if e:
                x_send(d, e)

    def head_sums(e):
        d = lax.rem(u + e - y + n, n)
        total = hs[d, 0].astype(F32)
        for k in far:
            pltpu.make_async_remote_copy(
                src_ref=hx.at[d, k - 1],
                dst_ref=hx.at[d, k - 1],
                send_sem=send_sems.at[x_base + d * (n - 1) + k - 1],
                recv_sem=recv_sems.at[x_base + d * (n - 1) + k - 1],
                device_id=x_peer(k),
                device_id_type=pl.DeviceIdType.MESH,
            ).wait_recv()
            total = total + hx[d, k - 1].astype(F32)
        return total

    head_terms(0)

    query_pos = pair * span + lax.broadcasted_iota(jnp.int32, (span, chunk), 0)
    key_pos = y * chunk + lax.broadcasted_iota(jnp.int32, (span, chunk), 1)

    def forward(j, first):
        scores = dot_nt(qf[span_of(pair), :], kf[group(j), :]) * SCALE
        if first:
            scores = jnp.where(key_pos <= query_pos, scores, NEG)
        new_top = jnp.max(scores, axis=1, keepdims=True)
        if not first:
            top = top_ref[:, :1]
            new_top = jnp.maximum(top, new_top)
        weights = jnp.exp(scores - new_top)
        total = jnp.sum(weights, axis=1, keepdims=True)
        acc = dot(weights.astype(BF16), vf[group(j), :])
        if not first:
            fade = jnp.exp(top - new_top)
            total = fade * sum_ref[:, :1] + total
            acc = fade * acc_ref[...] + acc
        top_ref[...] = jnp.broadcast_to(new_top, top_ref.shape)
        sum_ref[...] = jnp.broadcast_to(total, sum_ref.shape)
        acc_ref[...] = acc

    for d in near:
        wait(w_y[d])
        source = at(y, -d)
        w_d[n - d] = send(w_group(source), w_group(source), w_group(source, theirs), dp_peer)
    wait(q_s.values())
    forward(y, True)
    for d in near:
        head_terms(n - d)
    q_z = spread_z(qf.at[block(row), :], qs, lambda i: qf.at[block(i), :], z_steps[1:])
    for d in near:

        @pl.when(y >= d)
        def _(d=d):
            wait(k_y[d], True)
            wait(v_y[d], True)
            forward(y - d, False)

    own_of = x * n + u
    total = sum_ref[:, :1]
    of[own_of] = (acc_ref[...] / total).astype(BF16)
    log_norm = top_ref[:, :1] + jnp.log(total)
    last = n - 1
    low, high = slice(0, rows), slice(rows, span)
    before, after = x * n + at(u, -1), x * n + at(u, 1)
    beyond = x * n + at(u, 2)

    o_u = [send(of.at[own_of], of.at[own_of], of.at[before], u_peer(1))]
    if n > 2:
        o_u.append(send(of.at[own_of], of.at[own_of], of.at[after], u_peer(last)))

    def spread_x(e):
        return [
            send(
                of.at[x * n + at(u, e)],
                of.at[x * n + at(u, e)],
                of.at[at(x, -d) * n + at(u, e)],
                x_peer(d),
            )
            for d in far
        ]

    o_x = spread_x(0)
    h_u = []
    if n > 2:
        hz[2] = head_sums(2).astype(BF16)
        relay = [
            send(hz.at[2, low, :], hq.at[0], hq.at[0], u_peer(1)),
            send(hz.at[2, high, :], hq.at[1], hq.at[1], u_peer(last)),
        ]
        for e, part in ((1, high), (last, low)):
            hz[e] = head_sums(e).astype(BF16)
            h_u.append(
                send(hz.at[e, part, :], hr.at[e, part, :], hr.at[e, part, :], u_peer(e))
            )
        for i, e, part in ((0, 1, low), (1, last, high)):
            relay[i]()
            hz[e, part, :] = (hz[e, part, :].astype(F32) + hq[i].astype(F32)).astype(
                BF16
            )
            h_u.append(
                send(hz.at[e, part, :], hr.at[e, part, :], hr.at[e, part, :], u_peer(e))
            )
    else:
        hz[1] = head_sums(1).astype(BF16)
        h_u.append(send(hz.at[1], hr.at[1], hr.at[1], u_peer(1)))
    o_far = []
    o_u[0]()
    if n > 2:
        o_far.append(
            send(of.at[before, low, :], of.at[before, low, :], of.at[beyond, low, :], u_peer(1))
        )
        o_u[1]()
        o_far.append(
            send(of.at[after, high, :], of.at[after, high, :], of.at[beyond, high, :], u_peer(last))
        )
        o_x += spread_x(1)
    o_x += spread_x(-1)
    upstream = head_sums(0)
    q_y = gather_full(q_z, lambda i: qf.at[span_of(i), :], False)
    wait(h_u)
    for e in sorted({1, last}):
        upstream = upstream + hr[e].astype(F32)
    df[span_of(pair), :] = upstream.astype(BF16)
    d_h = gather_h(lambda i: df.at[span_of(i), :])
    d_y = [gather_y(lambda i: df.at[span_of(i), :], 0, False)]
    attended = of[own_of].astype(F32)
    row_dot = jnp.sum(
        df[span_of(pair), :].astype(F32) * attended, axis=1, keepdims=True
    )
    lane = lax.broadcasted_iota(jnp.int32, (span, HEAD), 1)
    table = jnp.where(lane == 0, log_norm, jnp.where(lane == 1, row_dot, 0.0))
    st[:, span_of(pair)] = jnp.transpose(table)[:8, :]
    s_h = gather_h(lambda i: st.at[:, span_of(i)])
    s_y = [gather_y(lambda i: st.at[:, span_of(i)], 0, False)]

    for h in range(1, m):
        d_h[h - 1]()
        d_y.append(gather_y(lambda i: df.at[span_of(i), :], h, False))
        s_h[h - 1]()
        s_y.append(gather_y(lambda i: st.at[:, span_of(i)], h, False))

    if n > 2:
        wait(o_far)
        o_x += spread_x(2)
    wait(o_x)

    def weight_part(which, target_y):
        first = which * n * m + target_y * m
        for i in range(m):
            c = first + i
            part = dot(gt[...], of[lax.rem(c, n) * n + c // n])
            gp[c] = part.astype(BF16)

    g_d = {}
    for d in far + [0]:
        target_y = at(y, d)
        weight_part(1 - dp, target_y)
        away = pl.ds((1 - dp) * n * m + target_y * m, m)
        here = pl.ds(target_y * m, m)
        g_d[d] = send(gp.at[away], gd.at[here], gd.at[here], dp_peer)
    for d in far + [0]:
        weight_part(dp, at(y, d))

    g_y = []
    for d in far + [0]:
        target_y = at(y, d)
        g_d[d]()
        for i in range(m):
            slot = target_y * m + i
            gy[slot] = (
                gp[dp * n * m + slot].astype(F32) + gd[slot].astype(F32)
            ).astype(BF16)
        if d:
            here = pl.ds(target_y * m, m)
            g_y.append(send(gy.at[here], gyr.at[d - 1], gyr.at[d - 1], y_peer(d)))

    lanes = [slice(h * HEAD, (h + 1) * HEAD) for h in range(2)]

    def project(c, acc):
        return acc + dot_nt(wf[c], of[lax.rem(c, n) * n + c // n])

    projected = lax.fori_loop(0, n * n, project, jnp.zeros((cols, span), F32))
    for h in range(2):
        ox[h] = projected[:, lanes[h]].astype(BF16)
    o_s = send(ox.at[1 - side], oxr, oxr, twin)

    def queries_pass(j, first, acc):
        keys = kf[group(j), :]
        scores = dot_nt(qf[span_of(pair), :], keys) * SCALE
        probs = jnp.exp(scores - log_norm)
        if first:
            probs = jnp.where(key_pos <= query_pos, probs, 0.0)
        slopes = dot_nt(df[span_of(pair), :], vf[group(j), :])
        slopes = (probs * (slopes - row_dot)).astype(BF16)
        return acc + dot(slopes, keys)

    acc = queries_pass(y, True, jnp.zeros((span, HEAD), F32))
    acc = lax.fori_loop(0, y, lambda j, acc: queries_pass(j, False, acc), acc)
    acc = (acc * SCALE).astype(BF16)
    dx[0, 0], dx[0, 1] = acc[:rows], acc[rows:]
    swaps = [send(dx.at[0, 1 - side], dxr.at[0], dxr.at[0], twin)]

    wait(g_y)
    g_z = []
    for d in list(range(1, m)) + [0]:
        target = at_h(d)
        total = gy[y * m + target].astype(F32)
        for e in others:
            total = total + gyr[e - 1, target].astype(F32)
        gz[d] = total.astype(BF16)
        if d:
            g_z.append(send(gz.at[d], gzr.at[d - 1], gzr.at[d - 1], h_peer(d)))

    own_key = pair * span + lax.broadcasted_iota(jnp.int32, (span, chunk), 0)
    ask_pos = y * chunk + lax.broadcasted_iota(jnp.int32, (span, chunk), 1)

    def keys_pass(j, first):
        queries = qf[group(j), :]
        ups = df[group(j), :]
        norm = st[0:1, group(j)]
        away = st[1:2, group(j)]
        scores = dot_nt(kf[span_of(pair), :], queries) * SCALE
        probs = jnp.exp(scores - norm)
        if first:
            probs = jnp.where(ask_pos >= own_key, probs, 0.0)
        slopes = dot_nt(vf[span_of(pair), :], ups)
        slopes = (probs * (slopes - away)).astype(BF16)
        sum_k, sum_v = dot(slopes, queries), dot(probs.astype(BF16), ups)
        if first:
            acc_ref[...], sum_ref[...] = sum_k, sum_v
        else:
            acc_ref[...] += sum_k
            sum_ref[...] += sum_v

    keys_pass(y, True)
    for d in near:

        @pl.when(y + d < n)
        def _(d=d):
            wait(q_y[d], True)
            for h in range(m):
                d_y[h][d](True)
                s_y[h][d](True)
            keys_pass(y + d, False)

    for i, value in ((1, acc_ref[...] * SCALE), (2, sum_ref[...])):
        value = value.astype(BF16)
        dx[i, 0], dx[i, 1] = value[:rows], value[rows:]
        swaps.append(send(dx.at[i, 1 - side], dxr.at[i], dxr.at[i], twin))

    wait(g_z)
    total = gz[0].astype(F32)
    for d in range(1, m):
        total = total + gzr[d - 1].astype(F32)
    gw_ref[...] = total
    o_s()
    out_ref[...] = (ox[side].astype(F32) + oxr[...].astype(F32)).astype(BF16)
    for i, target in enumerate((dq_ref, dk_ref, dv_ref)):
        swaps[i]()
        own, other = dx[i, side], dxr[i]
        for h in range(2):
            target[:, lanes[h]] = jnp.where(side == h, own, other)

    for finish in issued:
        finish()


def store_all(*refs):
    count = len(refs) // 2
    copies = [
        pltpu.make_async_copy(refs[i], refs[count + i], refs[-1].at[i])
        for i in range(count)
    ]
    for copy in copies:
        copy.start()
    for copy in copies:
        copy.wait()


def shards(n, queries, key_vectors, value_vectors, out_weight, out_grad):
    rows, width = queries.shape[1:]
    cols = out_grad.shape[2]
    blocks, m = n * n, n // 2
    copies = 112
    vmem = pl.BlockSpec(memory_space=pltpu.VMEM)

    def buffer(*shape, kind=BF16):
        return pltpu.VMEM(shape, kind)

    full = buffer(blocks * rows, HEAD)
    span = 2 * rows
    result = pl.pallas_call(
        functools.partial(kernel, n, rows, cols),
        out_shape=(
            jax.ShapeDtypeStruct((cols, rows), BF16),
            jax.ShapeDtypeStruct((rows, width), BF16),
            jax.ShapeDtypeStruct((rows, width), BF16),
            jax.ShapeDtypeStruct((rows, width), BF16),
            jax.ShapeDtypeStruct((cols, HEAD), F32),
        ),
        in_specs=[pl.BlockSpec(memory_space=pltpu.HBM)] * 5,
        out_specs=(vmem,) * 5,
        scratch_shapes=[
            buffer(rows, HEAD),
            buffer(rows, HEAD),
            buffer(rows, HEAD),
            buffer(cols, HEAD),
            full,
            full,
            full,
            full,
            buffer(8, blocks * rows, kind=F32),
            buffer(blocks, cols, HEAD),
            buffer(span, cols),
            buffer(cols, span),
            buffer(n, n, span, HEAD),
            buffer(n, n - 1, span, HEAD),
            buffer(n, span, HEAD),
            buffer(n, span, HEAD),
            buffer(2, rows, HEAD),
            buffer(blocks, span, HEAD),
            buffer(span, HEAD, kind=F32),
            buffer(span, HEAD, kind=F32),
            buffer(span, HEAD, kind=F32),
            buffer(blocks, cols, HEAD),
            buffer(n * m, cols, HEAD),
            buffer(n * m, cols, HEAD),
            buffer(n - 1, m, cols, HEAD),
            buffer(m, cols, HEAD),
            buffer(max(m - 1, 1), cols, HEAD),
            buffer(2, cols, rows),
            buffer(cols, rows),
            buffer(3, 2, rows, HEAD),
            buffer(3, rows, HEAD),
            pltpu.SemaphoreType.DMA((9,)),
            pltpu.SemaphoreType.DMA((copies,)),
            pltpu.SemaphoreType.DMA((copies,)),
        ],
        compiler_params=pltpu.CompilerParams(
            collective_id=0, has_side_effects=True, vmem_limit_bytes=64 << 20
        ),
    )(queries[0], key_vectors[0], value_vectors[0], out_weight.T, out_grad[0].T)
    result = pl.pallas_call(
        store_all,
        out_shape=[jax.ShapeDtypeStruct(a.shape, a.dtype) for a in result],
        in_specs=[vmem] * 5,
        out_specs=[pl.BlockSpec(memory_space=pltpu.HBM)] * 5,
        scratch_shapes=[pltpu.SemaphoreType.DMA((5,))],
    )(*result)
    output, grad_queries, grad_keys, grad_values, grad_weight = result
    return (
        output.T[None],
        grad_queries[None],
        grad_keys[None],
        grad_values[None],
        grad_weight.T,
    )


def solution(mesh):
    n = math.isqrt(mesh.shape["row"])
    return jax.shard_map(
        functools.partial(shards, n),
        mesh=mesh,
        in_specs=(
            P("dp", "row", "col"),
            P("dp", "row", "col"),
            P("dp", "row", "col"),
            P("row", "col"),
            P("dp", "row", "col"),
        ),
        out_specs=(
            P("dp", "row", "col"),
            P("dp", "row", "col"),
            P("dp", "row", "col"),
            P("dp", "row", "col"),
            P(("dp", "row"), "col"),
        ),
        check_vma=False,
    )
```

```python
import functools
import math

import jax
import jax.numpy as jnp
from jax import lax
from jax.experimental import pallas as pl
from jax.experimental.pallas import tpu as pltpu
from jax.sharding import PartitionSpec as P

HEAD = 128
NEG = -1e30
SCALE = 1.0 / math.sqrt(HEAD)
F32 = jnp.float32
BF16 = jnp.bfloat16
NT = (((1,), (1,)), ((), ()))
TN = (((0,), (0,)), ((), ()))


def dot(a, b):
    return jnp.dot(a, b, preferred_element_type=F32)


def dot_nt(a, b):
    return lax.dot_general(a, b, NT, preferred_element_type=F32)


def flip(a):
    size = a.shape[0]
    eye = (
        lax.broadcasted_iota(jnp.int32, (size, size), 0)
        == lax.broadcasted_iota(jnp.int32, (size, size), 1)
    )
    eye = jnp.where(eye, 1.0, 0.0).astype(BF16)
    return lax.dot_general(a, eye, TN, preferred_element_type=F32).astype(BF16)


def kernel(
    n,
    rows,
    cols,
    q_hbm,
    k_hbm,
    v_hbm,
    w_hbm,
    g_hbm,
    out_ref,
    dq_ref,
    dk_ref,
    dv_ref,
    gw_ref,
    qs,
    ks,
    vs,
    ws,
    kf,
    vf,
    qf,
    df,
    st,
    wf,
    gf,
    gt,
    hs,
    hx,
    hz,
    hr,
    hq,
    of,
    top_ref,
    sum_ref,
    acc_ref,
    gp,
    gd,
    gy,
    gyr,
    gz,
    gzr,
    ox,
    oxr,
    dx,
    dxr,
    load_sems,
    send_sems,
    recv_sems,
):
    dp, row, col = lax.axis_index("dp"), lax.axis_index("row"), lax.axis_index("col")
    m = n // 2
    y, z = row // n, lax.rem(row, n)
    zh, side = z // 2, lax.rem(z, 2)
    u, x = col // n, lax.rem(col, n)
    pair = y * m + zh
    span = 2 * rows
    chunk = n * rows
    others = list(range(1, n))
    far = sorted(others, key=lambda d: -min(d, n - d))
    near = far[::-1]
    z_steps = [(h, t) for h in range(m) for t in (1, 0) if h or t]

    def at(base, d):
        return lax.rem(base + d + n, n)

    def at_h(d):
        return lax.rem(zh + d + m, m)

    dp_peer = {"dp": 1 - dp}
    twin = {"row": row + 1 - 2 * side}

    def z_row(h, t):
        return y * n + 2 * at_h(h) + (1 - side if t else side)

    def h_peer(d):
        return {"row": z_row(d, 0)}

    def y_peer(d):
        return {"row": at(y, d) * n + z}

    def u_peer(d):
        return {"col": at(u, d) * n + x}

    def x_peer(d):
        return {"col": u * n + at(x, d)}

    def block(i):
        return pl.ds(pl.multiple_of(i * rows, rows), rows)

    def span_of(i):
        return pl.ds(pl.multiple_of(i * span, span), span)

    def group(i):
        return pl.ds(pl.multiple_of(i * chunk, chunk), chunk)

    half = cols // 2
    mine = pl.ds(pl.multiple_of(dp * half, half), half)
    theirs = pl.ds(pl.multiple_of((1 - dp) * half, half), half)
    own_lanes = block(side)
    other_lanes = block(1 - side)

    pieces = [
        (w_hbm.at[mine, own_lanes], wf.at[row, mine, :]),
        (w_hbm.at[mine, other_lanes], ws.at[mine, :]),
        (g_hbm, gt.at[:, own_lanes]),
    ]
    for source, split, full in ((k_hbm, ks, kf), (q_hbm, qs, qf), (v_hbm, vs, vf)):
        pieces.append((source.at[:, own_lanes], full.at[block(row), :]))
        pieces.append((source.at[:, other_lanes], split))
    loads = [
        pltpu.make_async_copy(source, target, load_sems.at[i])
        for i, (source, target) in enumerate(pieces)
    ]

    barrier = pltpu.get_barrier_semaphore()
    peers = [dp_peer] + [{"row": z_row(h, t)} for h, t in z_steps]
    peers += [u_peer(d) for d in sorted({1, n - 1})]
    peers += [f(d) for f in (y_peer, x_peer) for d in far]
    for peer in peers:
        pl.semaphore_signal(
            barrier, inc=1, device_id=peer, device_id_type=pl.DeviceIdType.MESH
        )
    for load in loads:
        load.start()

    issued = []
    slots = [0]

    def when(cond, body):
        if cond is None:
            body()
        else:
            pl.when(cond)(body)

    def take(count):
        slots[0] += count
        return slots[0] - count

    def send(src, dst, landed, peer, sends=None, receives=None, index=None):
        index = take(1) if index is None else index

        def describe(source, target, which):
            return pltpu.make_async_remote_copy(
                src_ref=source,
                dst_ref=target,
                send_sem=send_sems.at[which],
                recv_sem=recv_sems.at[which],
                device_id=peer,
                device_id_type=pl.DeviceIdType.MESH,
            )

        when(sends, lambda: describe(src, dst, index).start())
        issued.append(
            lambda: when(sends, lambda: describe(src, dst, index).wait_send())
        )
        if landed is None:
            return None
        return lambda inside=False: when(
            None if inside else receives,
            lambda: describe(landed, landed, index).wait_recv(),
        )

    def wait(handles, *inside):
        for handle in handles:
            handle(*inside)

    def spread_z(own, split, view, steps):
        return {
            (h, t): send(
                split if t else own, view(row), view(z_row(-h, t)), {"row": z_row(h, t)}
            )
            for h, t in steps
        }

    def gather_h(view):
        return [
            send(view(pair), view(pair), view(y * m + at_h(-d)), h_peer(d))
            for d in range(1, m)
        ]

    def gather_y(view, h, up):
        handles = {}
        for d in near:
            if up is None:
                sends = receives = None
            elif up:
                sends, receives = y + d < n, y >= d
            else:
                sends, receives = y >= d, y + d < n
            s = -1 if up is False else 1
            mid = at_h(-h)
            handles[d] = send(
                view(y * m + mid),
                view(y * m + mid),
                view(at(y, -s * d) * m + mid),
                y_peer(s * d),
                sends,
                receives,
            )
        return handles

    def gather_full(arrived, view, up):
        handles = []
        for h in range(m):
            wait([arrived[step] for step in z_steps if step[0] == h and step in arrived])
            handles.append(gather_y(view, h, up))
        return {d: [piece[d] for piece in handles] for d in near}

    def k_view(i):
        return kf.at[block(i), :]

    def w_pair(i):
        return wf.at[pl.ds(2 * i, 2), mine, :]

    def w_group(i, part=mine):
        return wf.at[pl.ds(i * n, n), part, :]

    wait([load.wait for load in loads])
    pl.semaphore_wait(barrier, len(peers))

    w_z = spread_z(
        wf.at[row, mine, :], ws.at[mine, :], lambda i: wf.at[i, mine, :], z_steps
    )
    g_s = send(gt.at[:, own_lanes], gt.at[:, own_lanes], gt.at[:, other_lanes], twin)
    w_parts = []
    for h in range(m):
        wait([w_z[step] for step in z_steps if step[0] == h])
        w_parts.append(gather_y(w_pair, h, None))
        if h == 0:
            k_z = spread_z(
                kf.at[block(row), :], ks, lambda i: kf.at[block(i), :], z_steps
            )
    w_d = {0: send(w_group(y), w_group(y), w_group(y, theirs), dp_peer)}
    q_s = spread_z(qf.at[block(row), :], qs, lambda i: qf.at[block(i), :], z_steps[:1])
    v_z = spread_z(vf.at[block(row), :], vs, lambda i: vf.at[block(i), :], z_steps)
    g_s()
    gf[...] = flip(gt[...])

    x_base = take(n * (n - 1))

    def x_send(d, e):
        index = x_base + d * (n - 1) + e - 1
        send(hs.at[d, e], hx.at[d, e - 1], None, x_peer(e), index=index)

    def head_terms(d):
        w_d[d]()
        for e in far + [0]:
            hs[d, e] = dot(gf[...], wf[at(y, d) * n + at(x, e)]).astype(BF16)
            if e:
                x_send(d, e)

    def head_sums(e):
        d = lax.rem(u + e - y + n, n)
        total = hs[d, 0].astype(F32)
        for k in far:
            pltpu.make_async_remote_copy(
                src_ref=hx.at[d, k - 1],
                dst_ref=hx.at[d, k - 1],
                send_sem=send_sems.at[x_base + d * (n - 1) + k - 1],
                recv_sem=recv_sems.at[x_base + d * (n - 1) + k - 1],
                device_id=x_peer(k),
                device_id_type=pl.DeviceIdType.MESH,
            ).wait_recv()
            total = total + hx[d, k - 1].astype(F32)
        return total

    head_terms(0)
    k_y = gather_full(k_z, lambda i: kf.at[span_of(i), :], True)
    v_y = gather_full(v_z, lambda i: vf.at[span_of(i), :], True)

    query_pos = pair * span + lax.broadcasted_iota(jnp.int32, (span, chunk), 0)
    key_pos = y * chunk + lax.broadcasted_iota(jnp.int32, (span, chunk), 1)

    def forward(j, first):
        scores = dot_nt(qf[span_of(pair), :], kf[group(j), :]) * SCALE
        if first:
            scores = jnp.where(key_pos <= query_pos, scores, NEG)
        new_top = jnp.max(scores, axis=1, keepdims=True)
        if not first:
            top = top_ref[:, :1]
            new_top = jnp.maximum(top, new_top)
        weights = jnp.exp(scores - new_top)
        total = jnp.sum(weights, axis=1, keepdims=True)
        acc = dot(weights.astype(BF16), vf[group(j), :])
        if not first:
            fade = jnp.exp(top - new_top)
            total = fade * sum_ref[:, :1] + total
            acc = fade * acc_ref[...] + acc
        top_ref[...] = jnp.broadcast_to(new_top, top_ref.shape)
        sum_ref[...] = jnp.broadcast_to(total, sum_ref.shape)
        acc_ref[...] = acc

    for d in near:
        wait([part[d] for part in w_parts])
        source = at(y, -d)
        w_d[n - d] = send(w_group(source), w_group(source), w_group(source, theirs), dp_peer)
    wait(q_s.values())
    forward(y, True)
    for d in near:
        head_terms(n - d)
    q_z = spread_z(qf.at[block(row), :], qs, lambda i: qf.at[block(i), :], z_steps[1:])
    for d in near:

        @pl.when(y >= d)
        def _(d=d):
            wait(k_y[d], True)
            wait(v_y[d], True)
            forward(y - d, False)

    own_of = x * n + u
    total = sum_ref[:, :1]
    of[own_of] = (acc_ref[...] / total).astype(BF16)
    log_norm = top_ref[:, :1] + jnp.log(total)
    last = n - 1
    low, high = slice(0, rows), slice(rows, span)
    before, after = x * n + at(u, -1), x * n + at(u, 1)
    beyond = x * n + at(u, 2)

    o_u = [send(of.at[own_of], of.at[own_of], of.at[before], u_peer(1))]
    if n > 2:
        o_u.append(send(of.at[own_of], of.at[own_of], of.at[after], u_peer(last)))

    def spread_x(e):
        return [
            send(
                of.at[x * n + at(u, e)],
                of.at[x * n + at(u, e)],
                of.at[at(x, -d) * n + at(u, e)],
                x_peer(d),
            )
            for d in far
        ]

    o_x = {0: spread_x(0)}
    h_u = []
    if n > 2:
        hz[2] = head_sums(2).astype(BF16)
        relay = [
            send(hz.at[2, low, :], hq.at[0], hq.at[0], u_peer(1)),
            send(hz.at[2, high, :], hq.at[1], hq.at[1], u_peer(last)),
        ]
        for e, part in ((1, high), (last, low)):
            hz[e] = head_sums(e).astype(BF16)
            h_u.append(
                send(hz.at[e, part, :], hr.at[e, part, :], hr.at[e, part, :], u_peer(e))
            )
        for i, e, part in ((0, 1, low), (1, last, high)):
            relay[i]()
            hz[e, part, :] = (hz[e, part, :].astype(F32) + hq[i].astype(F32)).astype(
                BF16
            )
            h_u.append(
                send(hz.at[e, part, :], hr.at[e, part, :], hr.at[e, part, :], u_peer(e))
            )
    else:
        hz[1] = head_sums(1).astype(BF16)
        h_u.append(send(hz.at[1], hr.at[1], hr.at[1], u_peer(1)))
    o_far = []
    o_u[0]()
    if n > 2:
        o_far.append(
            send(of.at[before, low, :], of.at[before, low, :], of.at[beyond, low, :], u_peer(1))
        )
        o_u[1]()
        o_far.append(
            send(of.at[after, high, :], of.at[after, high, :], of.at[beyond, high, :], u_peer(last))
        )
        o_x[1] = spread_x(1)
    o_x[last] = spread_x(-1)

    y_base = take(n)

    def weight_terms(e):
        wait(o_x[e])
        target = at(u, e)
        for i in range(n):
            gp[e, i] = dot(gt[...], of[i * n + target]).astype(BF16)
        ours = target // m == dp
        arrived = send(
            gp.at[e], gd.at[e], gd.at[e], dp_peer, target // m != dp, ours
        )
        arrived()

        @pl.when(ours)
        def _():
            for i in range(n):
                gy[e, i] = (gp[e, i].astype(F32) + gd[e, i].astype(F32)).astype(BF16)

        for i in range(2):
            target_y = 2 * lax.rem(target, m) + i
            d = lax.rem(target_y - y + n, n)
            send(
                gy.at[e, pl.ds(i * m, m)],
                gyr.at[d],
                None,
                {"row": target_y * n + z},
                jnp.logical_and(ours, target_y != y),
                index=y_base + d,
            )

    weight_terms(0)
    upstream = head_sums(0)
    q_y = gather_full(q_z, lambda i: qf.at[span_of(i), :], False)
    if n > 2:
        wait(o_far)
        o_x[2] = spread_x(2)
    wait(h_u)
    for e in sorted({1, last}):
        upstream = upstream + hr[e].astype(F32)
    df[span_of(pair), :] = upstream.astype(BF16)
    d_h = gather_h(lambda i: df.at[span_of(i), :])
    d_y = [gather_y(lambda i: df.at[span_of(i), :], 0, False)]
    attended = of[own_of].astype(F32)
    row_dot = jnp.sum(
        df[span_of(pair), :].astype(F32) * attended, axis=1, keepdims=True
    )
    lane = lax.broadcasted_iota(jnp.int32, (span, HEAD), 1)
    table = jnp.where(lane == 0, log_norm, jnp.where(lane == 1, row_dot, 0.0))
    st[:, span_of(pair)] = jnp.transpose(table)[:8, :]
    s_h = gather_h(lambda i: st.at[:, span_of(i)])
    s_y = [gather_y(lambda i: st.at[:, span_of(i)], 0, False)]

    def queries_pass(j, first, acc):
        keys = kf[group(j), :]
        scores = dot_nt(qf[span_of(pair), :], keys) * SCALE
        probs = jnp.exp(scores - log_norm)
        if first:
            probs = jnp.where(key_pos <= query_pos, probs, 0.0)
        slopes = dot_nt(df[span_of(pair), :], vf[group(j), :])
        slopes = (probs * (slopes - row_dot)).astype(BF16)
        return acc + dot(slopes, keys)

    weight_terms(last)
    for h in range(1, m):
        d_h[h - 1]()
        d_y.append(gather_y(lambda i: df.at[span_of(i), :], h, False))
        s_h[h - 1]()
        s_y.append(gather_y(lambda i: st.at[:, span_of(i)], h, False))
    if n > 2:
        weight_terms(1)
    acc = queries_pass(y, True, jnp.zeros((span, HEAD), F32))
    acc = lax.fori_loop(0, y, lambda j, acc: queries_pass(j, False, acc), acc)
    acc = (acc * SCALE).astype(BF16)
    dx[0, 0], dx[0, 1] = acc[:rows], acc[rows:]
    swaps = [send(dx.at[0, 1 - side], dxr.at[0], dxr.at[0], twin)]
    if n > 2:
        weight_terms(2)

    lanes = [slice(h * HEAD, (h + 1) * HEAD) for h in range(2)]

    def project(c, acc):
        return acc + dot_nt(wf[c], of[lax.rem(c, n) * n + c // n])

    projected = lax.fori_loop(0, n * n, project, jnp.zeros((cols, span), F32))
    for h in range(2):
        ox[h] = projected[:, lanes[h]].astype(BF16)
    o_s = send(ox.at[1 - side], oxr, oxr, twin)

    own_key = pair * span + lax.broadcasted_iota(jnp.int32, (span, chunk), 0)
    ask_pos = y * chunk + lax.broadcasted_iota(jnp.int32, (span, chunk), 1)

    def keys_pass(j, first):
        queries = qf[group(j), :]
        ups = df[group(j), :]
        norm = st[0:1, group(j)]
        away = st[1:2, group(j)]
        scores = dot_nt(kf[span_of(pair), :], queries) * SCALE
        probs = jnp.exp(scores - norm)
        if first:
            probs = jnp.where(ask_pos >= own_key, probs, 0.0)
        slopes = dot_nt(vf[span_of(pair), :], ups)
        slopes = (probs * (slopes - away)).astype(BF16)
        sum_k, sum_v = dot(slopes, queries), dot(probs.astype(BF16), ups)
        if first:
            acc_ref[...], sum_ref[...] = sum_k, sum_v
        else:
            acc_ref[...] += sum_k
            sum_ref[...] += sum_v

    keys_pass(y, True)

    for d in others:
        pltpu.make_async_remote_copy(
            src_ref=gyr.at[d],
            dst_ref=gyr.at[d],
            send_sem=send_sems.at[y_base + d],
            recv_sem=recv_sems.at[y_base + d],
            device_id=y_peer(d),
            device_id_type=pl.DeviceIdType.MESH,
        ).wait_recv()
    own_e = lax.rem(dp * m + y // 2 - u + n, n)
    own_i = lax.rem(y, 2) * m
    g_z = []
    for d in list(range(1, m)) + [0]:
        target = at_h(d)
        total = gy[own_e, own_i + target].astype(F32)
        for e in others:
            total = total + gyr[e, target].astype(F32)
        gz[d] = total.astype(BF16)
        if d:
            g_z.append(send(gz.at[d], gzr.at[d - 1], gzr.at[d - 1], h_peer(d)))
    for d in near:

        @pl.when(y + d < n)
        def _(d=d):
            wait(q_y[d], True)
            for h in range(m):
                d_y[h][d](True)
                s_y[h][d](True)
            keys_pass(y + d, False)

    for i, value in ((1, acc_ref[...] * SCALE), (2, sum_ref[...])):
        value = value.astype(BF16)
        dx[i, 0], dx[i, 1] = value[:rows], value[rows:]
        swaps.append(send(dx.at[i, 1 - side], dxr.at[i], dxr.at[i], twin))

    wait(g_z)
    total = gz[0].astype(F32)
    for d in range(1, m):
        total = total + gzr[d - 1].astype(F32)
    gw_ref[...] = total
    o_s()
    out_ref[...] = (ox[side].astype(F32) + oxr[...].astype(F32)).astype(BF16)
    for i, target in enumerate((dq_ref, dk_ref, dv_ref)):
        swaps[i]()
        own, other = dx[i, side], dxr[i]
        for h in range(2):
            target[:, lanes[h]] = jnp.where(side == h, own, other)

    for finish in issued:
        finish()


def store_all(*refs):
    count = len(refs) // 2
    copies = [
        pltpu.make_async_copy(refs[i], refs[count + i], refs[-1].at[i])
        for i in range(count)
    ]
    for copy in copies:
        copy.start()
    for copy in copies:
        copy.wait()


def shards(n, queries, key_vectors, value_vectors, out_weight, out_grad):
    rows, width = queries.shape[1:]
    cols = out_grad.shape[2]
    blocks, m = n * n, n // 2
    copies = 112
    vmem = pl.BlockSpec(memory_space=pltpu.VMEM)

    def buffer(*shape, kind=BF16):
        return pltpu.VMEM(shape, kind)

    full = buffer(blocks * rows, HEAD)
    span = 2 * rows
    result = pl.pallas_call(
        functools.partial(kernel, n, rows, cols),
        out_shape=(
            jax.ShapeDtypeStruct((cols, rows), BF16),
            jax.ShapeDtypeStruct((rows, width), BF16),
            jax.ShapeDtypeStruct((rows, width), BF16),
            jax.ShapeDtypeStruct((rows, width), BF16),
            jax.ShapeDtypeStruct((cols, HEAD), F32),
        ),
        in_specs=[pl.BlockSpec(memory_space=pltpu.HBM)] * 5,
        out_specs=(vmem,) * 5,
        scratch_shapes=[
            buffer(rows, HEAD),
            buffer(rows, HEAD),
            buffer(rows, HEAD),
            buffer(cols, HEAD),
            full,
            full,
            full,
            full,
            buffer(8, blocks * rows, kind=F32),
            buffer(blocks, cols, HEAD),
            buffer(span, cols),
            buffer(cols, span),
            buffer(n, n, span, HEAD),
            buffer(n, n - 1, span, HEAD),
            buffer(n, span, HEAD),
            buffer(n, span, HEAD),
            buffer(2, rows, HEAD),
            buffer(blocks, span, HEAD),
            buffer(span, HEAD, kind=F32),
            buffer(span, HEAD, kind=F32),
            buffer(span, HEAD, kind=F32),
            buffer(n, n, cols, HEAD),
            buffer(n, n, cols, HEAD),
            buffer(n, n, cols, HEAD),
            buffer(n, m, cols, HEAD),
            buffer(m, cols, HEAD),
            buffer(max(m - 1, 1), cols, HEAD),
            buffer(2, cols, rows),
            buffer(cols, rows),
            buffer(3, 2, rows, HEAD),
            buffer(3, rows, HEAD),
            pltpu.SemaphoreType.DMA((9,)),
            pltpu.SemaphoreType.DMA((copies,)),
            pltpu.SemaphoreType.DMA((copies,)),
        ],
        compiler_params=pltpu.CompilerParams(
            collective_id=0, has_side_effects=True, vmem_limit_bytes=64 << 20
        ),
    )(queries[0], key_vectors[0], value_vectors[0], out_weight.T, out_grad[0].T)
    result = pl.pallas_call(
        store_all,
        out_shape=[jax.ShapeDtypeStruct(a.shape, a.dtype) for a in result],
        in_specs=[vmem] * 5,
        out_specs=[pl.BlockSpec(memory_space=pltpu.HBM)] * 5,
        scratch_shapes=[pltpu.SemaphoreType.DMA((5,))],
    )(*result)
    output, grad_queries, grad_keys, grad_values, grad_weight = result
    return (
        output.T[None],
        grad_queries[None],
        grad_keys[None],
        grad_values[None],
        grad_weight.T,
    )


def solution(mesh):
    n = math.isqrt(mesh.shape["row"])
    return jax.shard_map(
        functools.partial(shards, n),
        mesh=mesh,
        in_specs=(
            P("dp", "row", "col"),
            P("dp", "row", "col"),
            P("dp", "row", "col"),
            P("row", "col"),
            P("dp", "row", "col"),
        ),
        out_specs=(
            P("dp", "row", "col"),
            P("dp", "row", "col"),
            P("dp", "row", "col"),
            P("dp", "row", "col"),
            P(("dp", "row"), "col"),
        ),
        check_vma=False,
    )
```

```python
import functools
import math

import jax
import jax.numpy as jnp
from jax import lax
from jax.experimental import pallas as pl
from jax.experimental.pallas import tpu as pltpu
from jax.sharding import PartitionSpec as P

HEAD = 128
NEG = -1e30
SCALE = 1.0 / math.sqrt(HEAD)
F32 = jnp.float32
BF16 = jnp.bfloat16
NT = (((1,), (1,)), ((), ()))
TN = (((0,), (0,)), ((), ()))


def dot(a, b):
    return jnp.dot(a, b, preferred_element_type=F32)


def dot_nt(a, b):
    return lax.dot_general(a, b, NT, preferred_element_type=F32)


def flip(a):
    size = a.shape[0]
    eye = (
        lax.broadcasted_iota(jnp.int32, (size, size), 0)
        == lax.broadcasted_iota(jnp.int32, (size, size), 1)
    )
    eye = jnp.where(eye, 1.0, 0.0).astype(BF16)
    return lax.dot_general(a, eye, TN, preferred_element_type=F32).astype(BF16)


def kernel(
    n,
    rows,
    cols,
    q_hbm,
    k_hbm,
    v_hbm,
    w_hbm,
    g_hbm,
    out_ref,
    dq_ref,
    dk_ref,
    dv_ref,
    gw_ref,
    qs,
    ks,
    vs,
    ws,
    kf,
    vf,
    qf,
    df,
    st,
    wf,
    gf,
    gt,
    wx,
    px,
    pr,
    hz,
    hr,
    hq,
    of,
    top_ref,
    sum_ref,
    acc_ref,
    gp,
    gd,
    gy,
    gyr,
    gz,
    gzr,
    gm,
    ox,
    oxr,
    dx,
    dxr,
    load_sems,
    send_sems,
    recv_sems,
):
    dp, row, col = lax.axis_index("dp"), lax.axis_index("row"), lax.axis_index("col")
    m = n // 2
    y, z = row // n, lax.rem(row, n)
    zh, side = z // 2, lax.rem(z, 2)
    u, x = col // n, lax.rem(col, n)
    pair = y * m + zh
    span = 2 * rows
    chunk = n * rows
    others = list(range(1, n))
    far = sorted(others, key=lambda d: -min(d, n - d))
    near = far[::-1]
    z_steps = [(h, t) for h in range(m) for t in (1, 0) if h or t]

    def at(base, d):
        return lax.rem(base + d + n, n)

    def at_h(d):
        return lax.rem(zh + d + m, m)

    dp_peer = {"dp": 1 - dp}
    twin = {"row": row + 1 - 2 * side}

    def z_row(h, t):
        return y * n + 2 * at_h(h) + (1 - side if t else side)

    def h_peer(d):
        return {"row": z_row(d, 0)}

    def y_peer(d):
        return {"row": at(y, d) * n + z}

    def u_peer(d):
        return {"col": at(u, d) * n + x}

    def x_peer(d):
        return {"col": u * n + at(x, d)}

    def block(i):
        return pl.ds(pl.multiple_of(i * rows, rows), rows)

    def span_of(i):
        return pl.ds(pl.multiple_of(i * span, span), span)

    def group(i):
        return pl.ds(pl.multiple_of(i * chunk, chunk), chunk)

    half = cols // 2
    mine = pl.ds(pl.multiple_of(dp * half, half), half)
    theirs = pl.ds(pl.multiple_of((1 - dp) * half, half), half)
    own_lanes = block(side)
    other_lanes = block(1 - side)

    pieces = [
        (w_hbm.at[mine, own_lanes], wf.at[row, mine, :]),
        (w_hbm.at[mine, other_lanes], ws.at[mine, :]),
        (g_hbm, gt.at[x, :, own_lanes]),
    ]
    for source, split, full in ((k_hbm, ks, kf), (q_hbm, qs, qf), (v_hbm, vs, vf)):
        pieces.append((source.at[:, own_lanes], full.at[block(row), :]))
        pieces.append((source.at[:, other_lanes], split))
    loads = [
        pltpu.make_async_copy(source, target, load_sems.at[i])
        for i, (source, target) in enumerate(pieces)
    ]

    barrier = pltpu.get_barrier_semaphore()
    peers = [dp_peer] + [{"row": z_row(h, t)} for h, t in z_steps]
    peers += [u_peer(d) for d in sorted({1, n - 1})]
    peers += [f(d) for f in (y_peer, x_peer) for d in far]
    code = lax.rem(y, 2) * m + zh
    mirror = {
        "row": (y - lax.rem(y, 2) + x // m) * n + 2 * lax.rem(x, m) + side,
        "col": u * n + code,
    }
    moves = code != x

    @pl.when(moves)
    def _():
        pl.semaphore_signal(
            barrier, inc=1, device_id=mirror, device_id_type=pl.DeviceIdType.MESH
        )

    for peer in peers:
        pl.semaphore_signal(
            barrier, inc=1, device_id=peer, device_id_type=pl.DeviceIdType.MESH
        )
    for load in loads:
        load.start()

    issued = []
    slots = [0]

    def when(cond, body):
        if cond is None:
            body()
        else:
            pl.when(cond)(body)

    def take(count):
        slots[0] += count
        return slots[0] - count

    def send(src, dst, landed, peer, sends=None, receives=None, index=None):
        index = take(1) if index is None else index

        def describe(source, target, which):
            return pltpu.make_async_remote_copy(
                src_ref=source,
                dst_ref=target,
                send_sem=send_sems.at[which],
                recv_sem=recv_sems.at[which],
                device_id=peer,
                device_id_type=pl.DeviceIdType.MESH,
            )

        when(sends, lambda: describe(src, dst, index).start())
        issued.append(
            lambda: when(sends, lambda: describe(src, dst, index).wait_send())
        )
        if landed is None:
            return None
        return lambda inside=False: when(
            None if inside else receives,
            lambda: describe(landed, landed, index).wait_recv(),
        )

    def wait(handles, *inside):
        for handle in handles:
            handle(*inside)

    def spread_z(own, split, view, steps):
        return {
            (h, t): send(
                split if t else own, view(row), view(z_row(-h, t)), {"row": z_row(h, t)}
            )
            for h, t in steps
        }

    def gather_h(view):
        return [
            send(view(pair), view(pair), view(y * m + at_h(-d)), h_peer(d))
            for d in range(1, m)
        ]

    def gather_y(view, h, up):
        handles = {}
        for d in near:
            if up is None:
                sends = receives = None
            elif up:
                sends, receives = y + d < n, y >= d
            else:
                sends, receives = y >= d, y + d < n
            s = -1 if up is False else 1
            mid = at_h(-h)
            handles[d] = send(
                view(y * m + mid),
                view(y * m + mid),
                view(at(y, -s * d) * m + mid),
                y_peer(s * d),
                sends,
                receives,
            )
        return handles

    def gather_full(arrived, view, up):
        handles = []
        for h in range(m):
            wait([arrived[step] for step in z_steps if step[0] == h and step in arrived])
            handles.append(gather_y(view, h, up))
        return {d: [piece[d] for piece in handles] for d in near}

    def k_view(i):
        return kf.at[block(i), :]

    def w_pair(i):
        return wf.at[pl.ds(2 * i, 2), mine, :]

    wait([load.wait for load in loads])
    pl.semaphore_wait(barrier, len(peers) + jnp.where(moves, 1, 0))

    w_z = spread_z(
        wf.at[row, mine, :], ws.at[mine, :], lambda i: wf.at[i, mine, :], z_steps
    )
    g_s = send(
        gt.at[x, :, own_lanes], gt.at[x, :, own_lanes], gt.at[x, :, other_lanes], twin
    )
    w_parts = []
    for h in range(m):
        wait([w_z[step] for step in z_steps if step[0] == h])
        w_parts.append(gather_y(w_pair, h, None))
        if h == 0:
            k_z = spread_z(
                kf.at[block(row), :], ks, lambda i: kf.at[block(i), :], z_steps
            )

    def w_across(i):
        j = at(y, i)
        wx[j, x, mine, :] = wf[j * n + x, mine, :]
        return [
            send(
                wf.at[j * n + at(x, e), mine, :],
                wx.at[j, x, mine, :],
                wx.at[j, at(x, -e), mine, :],
                x_peer(e),
            )
            for e in far
        ]

    w_x = {0: w_across(0)}
    q_s = spread_z(qf.at[block(row), :], qs, lambda i: qf.at[block(i), :], z_steps[:1])
    v_z = spread_z(vf.at[block(row), :], vs, lambda i: vf.at[block(i), :], z_steps)
    g_s()
    g_x = {
        e: send(gt.at[x], gt.at[x], gt.at[at(x, -e)], x_peer(e)) for e in far
    }
    gf[x] = flip(gt[x])
    k_y = gather_full(k_z, lambda i: kf.at[span_of(i), :], True)
    v_y = gather_full(v_z, lambda i: vf.at[span_of(i), :], True)

    d_base = take(n)

    def w_swap(i):
        wait(w_x[i])
        j = at(y, i)
        send(wx.at[j, :, mine, :], wx.at[j, :, mine, :], None, dp_peer, index=d_base + i)

    def head_sums(e):
        j = at(u, e)
        i = lax.rem(j - y + n, n)
        pltpu.make_async_remote_copy(
            src_ref=wx.at[j, :, theirs, :],
            dst_ref=wx.at[j, :, theirs, :],
            send_sem=send_sems.at[d_base + i],
            recv_sem=recv_sems.at[d_base + i],
            device_id=dp_peer,
            device_id_type=pl.DeviceIdType.MESH,
        ).wait_recv()
        total = dot(gf[0], wx[j, 0])
        for k in others:
            total = total + dot(gf[k], wx[j, k])
        return total

    query_pos = pair * span + lax.broadcasted_iota(jnp.int32, (span, chunk), 0)
    key_pos = y * chunk + lax.broadcasted_iota(jnp.int32, (span, chunk), 1)

    def forward(j, first):
        scores = dot_nt(qf[span_of(pair), :], kf[group(j), :]) * SCALE
        if first:
            scores = jnp.where(key_pos <= query_pos, scores, NEG)
        new_top = jnp.max(scores, axis=1, keepdims=True)
        if not first:
            top = top_ref[:, :1]
            new_top = jnp.maximum(top, new_top)
        weights = jnp.exp(scores - new_top)
        total = jnp.sum(weights, axis=1, keepdims=True)
        acc = dot(weights.astype(BF16), vf[group(j), :])
        if not first:
            fade = jnp.exp(top - new_top)
            total = fade * sum_ref[:, :1] + total
            acc = fade * acc_ref[...] + acc
        top_ref[...] = jnp.broadcast_to(new_top, top_ref.shape)
        sum_ref[...] = jnp.broadcast_to(total, sum_ref.shape)
        acc_ref[...] = acc

    for d in near:
        wait([part[d] for part in w_parts])
        w_x[n - d] = w_across(n - d)
    wait(q_s.values())
    forward(y, True)
    w_swap(0)
    for e in near:
        g_x[e]()
        gf[at(x, -e)] = flip(gt[at(x, -e)])
    for d in near:
        w_swap(n - d)
    q_z = spread_z(qf.at[block(row), :], qs, lambda i: qf.at[block(i), :], z_steps[1:])

    last = n - 1
    low, high = slice(0, rows), slice(rows, span)
    h_u = []
    if n > 2:
        hz[2] = head_sums(2).astype(BF16)
        relay = [
            send(hz.at[2, low, :], hq.at[0], hq.at[0], u_peer(1)),
            send(hz.at[2, high, :], hq.at[1], hq.at[1], u_peer(last)),
        ]
        for e, part in ((1, high), (last, low)):
            hz[e] = head_sums(e).astype(BF16)
            h_u.append(
                send(hz.at[e, part, :], hr.at[e, part, :], hr.at[e, part, :], u_peer(e))
            )
    else:
        hz[1] = head_sums(1).astype(BF16)
        h_u.append(send(hz.at[1], hr.at[1], hr.at[1], u_peer(1)))
    upstream = head_sums(0)

    for d in near:

        @pl.when(y >= d)
        def _(d=d):
            wait(k_y[d], True)
            wait(v_y[d], True)
            forward(y - d, False)

    own_of = u
    total = sum_ref[:, :1]
    of[own_of] = (acc_ref[...] / total).astype(BF16)
    log_norm = top_ref[:, :1] + jnp.log(total)
    before, after, beyond = at(u, -1), at(u, 1), at(u, 2)

    o_u = [send(of.at[own_of], of.at[own_of], of.at[before], u_peer(1))]
    if n > 2:
        o_u.append(send(of.at[own_of], of.at[own_of], of.at[after], u_peer(last)))

    if n > 2:
        for i, e, part in ((0, 1, low), (1, last, high)):
            relay[i]()
            hz[e, part, :] = (hz[e, part, :].astype(F32) + hq[i].astype(F32)).astype(
                BF16
            )
            h_u.append(
                send(hz.at[e, part, :], hr.at[e, part, :], hr.at[e, part, :], u_peer(e))
            )
    o_far = []
    o_u[0]()
    if n > 2:
        o_far.append(
            send(of.at[before, low, :], of.at[before, low, :], of.at[beyond, low, :], u_peer(1))
        )
        o_u[1]()
        o_far.append(
            send(of.at[after, high, :], of.at[after, high, :], of.at[beyond, high, :], u_peer(last))
        )

    y_base = take(n)

    def weight_terms(e):
        target = at(u, e)
        for i in range(n):
            gp[e, i] = dot(gt[i], of[target]).astype(BF16)
        ours = target // m == dp
        arrived = send(
            gp.at[e], gd.at[e], gd.at[e], dp_peer, target // m != dp, ours
        )
        arrived()

        @pl.when(ours)
        def _():
            for i in range(n):
                gy[e, i] = (gp[e, i].astype(F32) + gd[e, i].astype(F32)).astype(BF16)

        for i in range(2):
            target_y = 2 * lax.rem(target, m) + i
            d = lax.rem(target_y - y + n, n)
            send(
                gy.at[e, pl.ds(i * m, m)],
                gyr.at[d],
                None,
                {"row": target_y * n + z},
                jnp.logical_and(ours, target_y != y),
                index=y_base + d,
            )

    weight_terms(0)
    q_y = gather_full(q_z, lambda i: qf.at[span_of(i), :], False)
    wait(h_u)
    for e in sorted({1, last}):
        upstream = upstream + hr[e].astype(F32)
    df[span_of(pair), :] = upstream.astype(BF16)
    d_h = gather_h(lambda i: df.at[span_of(i), :])
    d_y = [gather_y(lambda i: df.at[span_of(i), :], 0, False)]
    attended = of[own_of].astype(F32)
    row_dot = jnp.sum(
        df[span_of(pair), :].astype(F32) * attended, axis=1, keepdims=True
    )
    lane = lax.broadcasted_iota(jnp.int32, (span, HEAD), 1)
    table = jnp.where(lane == 0, log_norm, jnp.where(lane == 1, row_dot, 0.0))
    st[:, span_of(pair)] = jnp.transpose(table)[:8, :]
    s_h = gather_h(lambda i: st.at[:, span_of(i)])
    s_y = [gather_y(lambda i: st.at[:, span_of(i)], 0, False)]

    def queries_pass(j, first, acc):
        keys = kf[group(j), :]
        scores = dot_nt(qf[span_of(pair), :], keys) * SCALE
        probs = jnp.exp(scores - log_norm)
        if first:
            probs = jnp.where(key_pos <= query_pos, probs, 0.0)
        slopes = dot_nt(df[span_of(pair), :], vf[group(j), :])
        slopes = (probs * (slopes - row_dot)).astype(BF16)
        return acc + dot(slopes, keys)

    if n > 2:
        weight_terms(1)
    for h in range(1, m):
        d_h[h - 1]()
        d_y.append(gather_y(lambda i: df.at[span_of(i), :], h, False))
        s_h[h - 1]()
        s_y.append(gather_y(lambda i: st.at[:, span_of(i)], h, False))
    weight_terms(last)
    acc = queries_pass(y, True, jnp.zeros((span, HEAD), F32))
    acc = lax.fori_loop(0, y, lambda j, acc: queries_pass(j, False, acc), acc)
    acc = (acc * SCALE).astype(BF16)
    dx[0, 0], dx[0, 1] = acc[:rows], acc[rows:]
    swaps = [send(dx.at[0, 1 - side], dxr.at[0], dxr.at[0], twin)]
    if n > 2:
        wait(o_far)
        weight_terms(2)

    lanes = [slice(h * HEAD, (h + 1) * HEAD) for h in range(2)]

    def project(i):
        total = dot_nt(wx[0, i], of[0])
        for j in others:
            total = total + dot_nt(wx[j, i], of[j])
        return total

    p_x = []
    for e in far:
        target_x = at(x, e)
        px[e] = project(target_x).astype(BF16)
        p_x.append(send(px.at[e], pr.at[e], pr.at[e], x_peer(e)))
    projected = project(x)

    own_key = pair * span + lax.broadcasted_iota(jnp.int32, (span, chunk), 0)
    ask_pos = y * chunk + lax.broadcasted_iota(jnp.int32, (span, chunk), 1)

    def keys_pass(j, first):
        queries = qf[group(j), :]
        ups = df[group(j), :]
        norm = st[0:1, group(j)]
        away = st[1:2, group(j)]
        scores = dot_nt(kf[span_of(pair), :], queries) * SCALE
        probs = jnp.exp(scores - norm)
        if first:
            probs = jnp.where(ask_pos >= own_key, probs, 0.0)
        slopes = dot_nt(vf[span_of(pair), :], ups)
        slopes = (probs * (slopes - away)).astype(BF16)
        sum_k, sum_v = dot(slopes, queries), dot(probs.astype(BF16), ups)
        if first:
            acc_ref[...], sum_ref[...] = sum_k, sum_v
        else:
            acc_ref[...] += sum_k
            sum_ref[...] += sum_v

    keys_pass(y, True)
    wait(p_x)
    for e in others:
        projected = projected + pr[e].astype(F32)
    for h in range(2):
        ox[h] = projected[:, lanes[h]].astype(BF16)
    o_s = send(ox.at[1 - side], oxr, oxr, twin)

    for d in others:
        pltpu.make_async_remote_copy(
            src_ref=gyr.at[d],
            dst_ref=gyr.at[d],
            send_sem=send_sems.at[y_base + d],
            recv_sem=recv_sems.at[y_base + d],
            device_id=y_peer(d),
            device_id_type=pl.DeviceIdType.MESH,
        ).wait_recv()
    own_e = lax.rem(dp * m + y // 2 - u + n, n)
    own_i = lax.rem(y, 2) * m
    g_z = []
    for d in list(range(1, m)) + [0]:
        target = at_h(d)
        total = gy[own_e, own_i + target].astype(F32)
        for e in others:
            total = total + gyr[e, target].astype(F32)
        gz[d] = total.astype(BF16)
        if d:
            g_z.append(send(gz.at[d], gzr.at[d - 1], gzr.at[d - 1], h_peer(d)))
    for d in near:

        @pl.when(y + d < n)
        def _(d=d):
            wait(q_y[d], True)
            for h in range(m):
                d_y[h][d](True)
                s_y[h][d](True)
            keys_pass(y + d, False)

    for i, value in ((1, acc_ref[...] * SCALE), (2, sum_ref[...])):
        value = value.astype(BF16)
        dx[i, 0], dx[i, 1] = value[:rows], value[rows:]
        swaps.append(send(dx.at[i, 1 - side], dxr.at[i], dxr.at[i], twin))

    wait(g_z)
    total = gz[0].astype(F32)
    for d in range(1, m):
        total = total + gzr[d - 1].astype(F32)
    gm[0] = total.astype(BF16)
    g_m = send(gm.at[0], gm.at[1], gm.at[1], mirror, moves, moves)
    o_s()
    out_ref[...] = (ox[side].astype(F32) + oxr[...].astype(F32)).astype(BF16)
    for i, target in enumerate((dq_ref, dk_ref, dv_ref)):
        swaps[i]()
        own, other = dx[i, side], dxr[i]
        for h in range(2):
            target[:, lanes[h]] = jnp.where(side == h, own, other)

    gw_ref[...] = total

    @pl.when(moves)
    def _():
        g_m(True)
        gw_ref[...] = gm[1].astype(F32)

    for finish in issued:
        finish()


def store_all(*refs):
    count = len(refs) // 2
    copies = [
        pltpu.make_async_copy(refs[i], refs[count + i], refs[-1].at[i])
        for i in range(count)
    ]
    for copy in copies:
        copy.start()
    for copy in copies:
        copy.wait()


def shards(n, queries, key_vectors, value_vectors, out_weight, out_grad):
    rows, width = queries.shape[1:]
    cols = out_grad.shape[2]
    blocks, m = n * n, n // 2
    copies = 112
    vmem = pl.BlockSpec(memory_space=pltpu.VMEM)

    def buffer(*shape, kind=BF16):
        return pltpu.VMEM(shape, kind)

    full = buffer(blocks * rows, HEAD)
    span = 2 * rows
    result = pl.pallas_call(
        functools.partial(kernel, n, rows, cols),
        out_shape=(
            jax.ShapeDtypeStruct((cols, rows), BF16),
            jax.ShapeDtypeStruct((rows, width), BF16),
            jax.ShapeDtypeStruct((rows, width), BF16),
            jax.ShapeDtypeStruct((rows, width), BF16),
            jax.ShapeDtypeStruct((cols, HEAD), F32),
        ),
        in_specs=[pl.BlockSpec(memory_space=pltpu.HBM)] * 5,
        out_specs=(vmem,) * 5,
        scratch_shapes=[
            buffer(rows, HEAD),
            buffer(rows, HEAD),
            buffer(rows, HEAD),
            buffer(cols, HEAD),
            full,
            full,
            full,
            full,
            buffer(8, blocks * rows, kind=F32),
            buffer(blocks, cols, HEAD),
            buffer(n, span, cols),
            buffer(n, cols, span),
            buffer(n, n, cols, HEAD),
            buffer(n, cols, span),
            buffer(n, cols, span),
            buffer(n, span, HEAD),
            buffer(n, span, HEAD),
            buffer(2, rows, HEAD),
            buffer(n, span, HEAD),
            buffer(span, HEAD, kind=F32),
            buffer(span, HEAD, kind=F32),
            buffer(span, HEAD, kind=F32),
            buffer(n, n, cols, HEAD),
            buffer(n, n, cols, HEAD),
            buffer(n, n, cols, HEAD),
            buffer(n, m, cols, HEAD),
            buffer(m, cols, HEAD),
            buffer(max(m - 1, 1), cols, HEAD),
            buffer(2, cols, HEAD),
            buffer(2, cols, rows),
            buffer(cols, rows),
            buffer(3, 2, rows, HEAD),
            buffer(3, rows, HEAD),
            pltpu.SemaphoreType.DMA((9,)),
            pltpu.SemaphoreType.DMA((copies,)),
            pltpu.SemaphoreType.DMA((copies,)),
        ],
        compiler_params=pltpu.CompilerParams(
            collective_id=0, has_side_effects=True, vmem_limit_bytes=64 << 20
        ),
    )(queries[0], key_vectors[0], value_vectors[0], out_weight.T, out_grad[0].T)
    result = pl.pallas_call(
        store_all,
        out_shape=[jax.ShapeDtypeStruct(a.shape, a.dtype) for a in result],
        in_specs=[vmem] * 5,
        out_specs=[pl.BlockSpec(memory_space=pltpu.HBM)] * 5,
        scratch_shapes=[pltpu.SemaphoreType.DMA((5,))],
    )(*result)
    output, grad_queries, grad_keys, grad_values, grad_weight = result
    return (
        output.T[None],
        grad_queries[None],
        grad_keys[None],
        grad_values[None],
        grad_weight.T,
    )


def solution(mesh):
    n = math.isqrt(mesh.shape["row"])
    return jax.shard_map(
        functools.partial(shards, n),
        mesh=mesh,
        in_specs=(
            P("dp", "row", "col"),
            P("dp", "row", "col"),
            P("dp", "row", "col"),
            P("row", "col"),
            P("dp", "row", "col"),
        ),
        out_specs=(
            P("dp", "row", "col"),
            P("dp", "row", "col"),
            P("dp", "row", "col"),
            P("dp", "row", "col"),
            P(("dp", "row"), "col"),
        ),
        check_vma=False,
    )
```

```python
import functools
import math

import jax
import jax.numpy as jnp
from jax import lax
from jax.experimental import pallas as pl
from jax.experimental.pallas import tpu as pltpu
from jax.sharding import PartitionSpec as P

HEAD = 128
NEG = -1e30
SCALE = 1.0 / math.sqrt(HEAD)
F32 = jnp.float32
BF16 = jnp.bfloat16
NT = (((1,), (1,)), ((), ()))
TN = (((0,), (0,)), ((), ()))


def dot(a, b):
    return jnp.dot(a, b, preferred_element_type=F32)


def dot_nt(a, b):
    return lax.dot_general(a, b, NT, preferred_element_type=F32)


def flip(a):
    size = a.shape[0]
    eye = (
        lax.broadcasted_iota(jnp.int32, (size, size), 0)
        == lax.broadcasted_iota(jnp.int32, (size, size), 1)
    )
    eye = jnp.where(eye, 1.0, 0.0).astype(BF16)
    return lax.dot_general(a, eye, TN, preferred_element_type=F32).astype(BF16)


def kernel(
    n,
    rows,
    cols,
    q_hbm,
    k_hbm,
    v_hbm,
    w_hbm,
    g_hbm,
    out_ref,
    dq_ref,
    dk_ref,
    dv_ref,
    gw_ref,
    qs,
    ks,
    vs,
    ws,
    kf,
    vf,
    qf,
    df,
    st,
    wf,
    gf,
    gt,
    wx,
    px,
    pr,
    hz,
    hr,
    hq,
    of,
    top_ref,
    sum_ref,
    acc_ref,
    gp,
    gd,
    gy,
    gyr,
    gz,
    gzr,
    gm,
    ox,
    oxr,
    dx,
    dxr,
    load_sems,
    send_sems,
    recv_sems,
):
    dp, row, col = lax.axis_index("dp"), lax.axis_index("row"), lax.axis_index("col")
    m = n // 2
    y, z = row // n, lax.rem(row, n)
    zh, side = z // 2, lax.rem(z, 2)
    u, x = col // n, lax.rem(col, n)
    pair = y * m + zh
    span = 2 * rows
    chunk = n * rows
    others = list(range(1, n))
    far = sorted(others, key=lambda d: -min(d, n - d))
    near = far[::-1]
    z_steps = [(h, t) for h in range(m) for t in (1, 0) if h or t]

    def at(base, d):
        return lax.rem(base + d + n, n)

    def at_h(d):
        return lax.rem(zh + d + m, m)

    dp_peer = {"dp": 1 - dp}
    twin = {"row": row + 1 - 2 * side}

    def z_row(h, t):
        return y * n + 2 * at_h(h) + (1 - side if t else side)

    def h_peer(d):
        return {"row": z_row(d, 0)}

    def y_peer(d):
        return {"row": at(y, d) * n + z}

    def u_peer(d):
        return {"col": at(u, d) * n + x}

    def x_peer(d):
        return {"col": u * n + at(x, d)}

    def block(i):
        return pl.ds(pl.multiple_of(i * rows, rows), rows)

    def span_of(i):
        return pl.ds(pl.multiple_of(i * span, span), span)

    def group(i):
        return pl.ds(pl.multiple_of(i * chunk, chunk), chunk)

    half = cols // 2
    mine = pl.ds(pl.multiple_of(dp * half, half), half)
    theirs = pl.ds(pl.multiple_of((1 - dp) * half, half), half)
    own_lanes = block(side)
    other_lanes = block(1 - side)

    pieces = [
        (w_hbm.at[mine, own_lanes], wf.at[row, mine, :]),
        (w_hbm.at[mine, other_lanes], ws.at[mine, :]),
        (g_hbm, gt.at[x, :, own_lanes]),
    ]
    for source, split, full in ((k_hbm, ks, kf), (q_hbm, qs, qf), (v_hbm, vs, vf)):
        pieces.append((source.at[:, own_lanes], full.at[block(row), :]))
        pieces.append((source.at[:, other_lanes], split))
    loads = [
        pltpu.make_async_copy(source, target, load_sems.at[i])
        for i, (source, target) in enumerate(pieces)
    ]

    barrier = pltpu.get_barrier_semaphore()
    peers = [dp_peer] + [{"row": z_row(h, t)} for h, t in z_steps]
    peers += [u_peer(d) for d in sorted({1, n - 1})]
    peers += [f(d) for f in (y_peer, x_peer) for d in far]
    code = lax.rem(y, 2) * m + zh
    mirror = {
        "row": (y - lax.rem(y, 2) + x // m) * n + 2 * lax.rem(x, m) + side,
        "col": u * n + code,
    }
    moves = code != x

    @pl.when(moves)
    def _():
        pl.semaphore_signal(
            barrier, inc=1, device_id=mirror, device_id_type=pl.DeviceIdType.MESH
        )

    for peer in peers:
        pl.semaphore_signal(
            barrier, inc=1, device_id=peer, device_id_type=pl.DeviceIdType.MESH
        )
    for load in loads:
        load.start()

    issued = []
    slots = [0]

    def when(cond, body):
        if cond is None:
            body()
        else:
            pl.when(cond)(body)

    def take(count):
        slots[0] += count
        return slots[0] - count

    def send(src, dst, landed, peer, sends=None, receives=None, index=None):
        index = take(1) if index is None else index

        def describe(source, target, which):
            return pltpu.make_async_remote_copy(
                src_ref=source,
                dst_ref=target,
                send_sem=send_sems.at[which],
                recv_sem=recv_sems.at[which],
                device_id=peer,
                device_id_type=pl.DeviceIdType.MESH,
            )

        when(sends, lambda: describe(src, dst, index).start())
        issued.append(
            lambda: when(sends, lambda: describe(src, dst, index).wait_send())
        )
        if landed is None:
            return None
        return lambda inside=False: when(
            None if inside else receives,
            lambda: describe(landed, landed, index).wait_recv(),
        )

    def wait(handles, *inside):
        for handle in handles:
            handle(*inside)

    def spread_z(own, split, view, steps):
        return {
            (h, t): send(
                split if t else own, view(row), view(z_row(-h, t)), {"row": z_row(h, t)}
            )
            for h, t in steps
        }

    def gather_h(view):
        return [
            send(view(pair), view(pair), view(y * m + at_h(-d)), h_peer(d))
            for d in range(1, m)
        ]

    def gather_y(view, h, up):
        handles = {}
        for d in near:
            if up is None:
                sends = receives = None
            elif up:
                sends, receives = y + d < n, y >= d
            else:
                sends, receives = y >= d, y + d < n
            s = -1 if up is False else 1
            mid = at_h(-h)
            handles[d] = send(
                view(y * m + mid),
                view(y * m + mid),
                view(at(y, -s * d) * m + mid),
                y_peer(s * d),
                sends,
                receives,
            )
        return handles

    def gather_full(arrived, view, up):
        handles = []
        for h in range(m):
            wait([arrived[step] for step in z_steps if step[0] == h and step in arrived])
            handles.append(gather_y(view, h, up))
        return {d: [piece[d] for piece in handles] for d in near}

    def k_view(i):
        return kf.at[block(i), :]

    def w_pair(i):
        return wf.at[pl.ds(2 * i, 2), mine, :]

    wait([load.wait for load in loads])
    pl.semaphore_wait(barrier, len(peers) + jnp.where(moves, 1, 0))

    w_z = spread_z(
        wf.at[row, mine, :], ws.at[mine, :], lambda i: wf.at[i, mine, :], z_steps
    )
    g_s = send(
        gt.at[x, :, own_lanes], gt.at[x, :, own_lanes], gt.at[x, :, other_lanes], twin
    )
    w_parts = []
    for h in range(m):
        wait([w_z[step] for step in z_steps if step[0] == h])
        w_parts.append(gather_y(w_pair, h, None))
        if h == 0:
            k_z = spread_z(
                kf.at[block(row), :], ks, lambda i: kf.at[block(i), :], z_steps
            )

    def w_across(i):
        j = at(y, i)
        wx[j, x, mine, :] = wf[j * n + x, mine, :]
        return [
            send(
                wf.at[j * n + at(x, e), mine, :],
                wx.at[j, x, mine, :],
                wx.at[j, at(x, -e), mine, :],
                x_peer(e),
            )
            for e in far
        ]

    w_x = {0: w_across(0)}
    q_s = spread_z(qf.at[block(row), :], qs, lambda i: qf.at[block(i), :], z_steps[:1])
    v_z = spread_z(vf.at[block(row), :], vs, lambda i: vf.at[block(i), :], z_steps)
    g_s()
    g_x = {
        e: send(gt.at[x], gt.at[x], gt.at[at(x, -e)], x_peer(e)) for e in far
    }
    gf[x] = flip(gt[x])
    k_y = gather_full(k_z, lambda i: kf.at[span_of(i), :], True)
    v_y = gather_full(v_z, lambda i: vf.at[span_of(i), :], True)

    d_base = take(n)

    def w_swap(i):
        wait(w_x[i])
        j = at(y, i)
        send(wx.at[j, :, mine, :], wx.at[j, :, mine, :], None, dp_peer, index=d_base + i)

    def head_sums(e):
        j = at(u, e)
        i = lax.rem(j - y + n, n)
        pltpu.make_async_remote_copy(
            src_ref=wx.at[j, :, theirs, :],
            dst_ref=wx.at[j, :, theirs, :],
            send_sem=send_sems.at[d_base + i],
            recv_sem=recv_sems.at[d_base + i],
            device_id=dp_peer,
            device_id_type=pl.DeviceIdType.MESH,
        ).wait_recv()
        total = dot(gf[0], wx[j, 0])
        for k in others:
            total = total + dot(gf[k], wx[j, k])
        return total

    query_pos = pair * span + lax.broadcasted_iota(jnp.int32, (span, chunk), 0)
    key_pos = y * chunk + lax.broadcasted_iota(jnp.int32, (span, chunk), 1)

    def forward(j, first):
        scores = dot_nt(qf[span_of(pair), :], kf[group(j), :]) * SCALE
        if first:
            scores = jnp.where(key_pos <= query_pos, scores, NEG)
        new_top = jnp.max(scores, axis=1, keepdims=True)
        if not first:
            top = top_ref[:, :1]
            new_top = jnp.maximum(top, new_top)
        weights = jnp.exp(scores - new_top)
        total = jnp.sum(weights, axis=1, keepdims=True)
        acc = dot(weights.astype(BF16), vf[group(j), :])
        if not first:
            fade = jnp.exp(top - new_top)
            total = fade * sum_ref[:, :1] + total
            acc = fade * acc_ref[...] + acc
        top_ref[...] = jnp.broadcast_to(new_top, top_ref.shape)
        sum_ref[...] = jnp.broadcast_to(total, sum_ref.shape)
        acc_ref[...] = acc

    for d in near:
        wait([part[d] for part in w_parts])
        w_x[n - d] = w_across(n - d)
    wait(q_s.values())
    forward(y, True)
    w_swap(0)
    for e in near:
        g_x[e]()
        gf[at(x, -e)] = flip(gt[at(x, -e)])
    for d in near:
        w_swap(n - d)

    last = n - 1
    low, high = slice(0, rows), slice(rows, span)
    h_u = []
    if n > 2:
        hz[2] = head_sums(2).astype(BF16)
        relay = [
            send(hz.at[2, low, :], hq.at[0], hq.at[0], u_peer(1)),
            send(hz.at[2, high, :], hq.at[1], hq.at[1], u_peer(last)),
        ]
        for e, part in ((1, high), (last, low)):
            hz[e] = head_sums(e).astype(BF16)
            h_u.append(
                send(hz.at[e, part, :], hr.at[e, part, :], hr.at[e, part, :], u_peer(e))
            )
    else:
        hz[1] = head_sums(1).astype(BF16)
        h_u.append(send(hz.at[1], hr.at[1], hr.at[1], u_peer(1)))
    upstream = head_sums(0)

    for d in near:

        @pl.when(y >= d)
        def _(d=d):
            wait(k_y[d], True)
            wait(v_y[d], True)
            forward(y - d, False)

    own_of = u
    total = sum_ref[:, :1]
    of[own_of] = (acc_ref[...] / total).astype(BF16)
    log_norm = top_ref[:, :1] + jnp.log(total)
    before, after, beyond = at(u, -1), at(u, 1), at(u, 2)

    o_u = [send(of.at[own_of], of.at[own_of], of.at[before], u_peer(1))]
    if n > 2:
        o_u.append(send(of.at[own_of], of.at[own_of], of.at[after], u_peer(last)))

    if n > 2:
        for i, e, part in ((0, 1, low), (1, last, high)):
            relay[i]()
            hz[e, part, :] = (hz[e, part, :].astype(F32) + hq[i].astype(F32)).astype(
                BF16
            )
            h_u.append(
                send(hz.at[e, part, :], hr.at[e, part, :], hr.at[e, part, :], u_peer(e))
            )
    o_far = []
    o_u[0]()
    if n > 2:
        o_far.append(
            send(of.at[before, low, :], of.at[before, low, :], of.at[beyond, low, :], u_peer(1))
        )
        o_u[1]()
        o_far.append(
            send(of.at[after, high, :], of.at[after, high, :], of.at[beyond, high, :], u_peer(last))
        )

    y_base = take(n)
    g_d = {}

    def weight_terms(e):
        target = at(u, e)
        for i in range(n):
            gp[e, i] = dot(gt[i], of[target]).astype(BF16)
        ours = target // m == dp
        g_d[e] = send(
            gp.at[e], gd.at[e], gd.at[e], dp_peer, target // m != dp, ours
        )

    def weight_sums(e):
        target = at(u, e)
        ours = target // m == dp
        g_d[e]()

        @pl.when(ours)
        def _():
            for i in range(n):
                gy[e, i] = (gp[e, i].astype(F32) + gd[e, i].astype(F32)).astype(BF16)

        for i in range(2):
            target_y = 2 * lax.rem(target, m) + i
            d = lax.rem(target_y - y + n, n)
            send(
                gy.at[e, pl.ds(i * m, m)],
                gyr.at[d],
                None,
                {"row": target_y * n + z},
                jnp.logical_and(ours, target_y != y),
                index=y_base + d,
            )

    q_z = spread_z(qf.at[block(row), :], qs, lambda i: qf.at[block(i), :], z_steps[1:])
    weight_terms(0)
    weight_terms(last)
    if n > 2:
        weight_terms(1)
    wait(h_u)
    for e in sorted({1, last}):
        upstream = upstream + hr[e].astype(F32)
    df[span_of(pair), :] = upstream.astype(BF16)
    d_h = gather_h(lambda i: df.at[span_of(i), :])
    d_y = [gather_y(lambda i: df.at[span_of(i), :], 0, False)]
    attended = of[own_of].astype(F32)
    row_dot = jnp.sum(
        df[span_of(pair), :].astype(F32) * attended, axis=1, keepdims=True
    )
    lane = lax.broadcasted_iota(jnp.int32, (span, HEAD), 1)
    table = jnp.where(lane == 0, log_norm, jnp.where(lane == 1, row_dot, 0.0))
    st[:, span_of(pair)] = jnp.transpose(table)[:8, :]
    s_h = gather_h(lambda i: st.at[:, span_of(i)])
    s_y = [gather_y(lambda i: st.at[:, span_of(i)], 0, False)]

    def queries_pass(j, first, acc):
        keys = kf[group(j), :]
        scores = dot_nt(qf[span_of(pair), :], keys) * SCALE
        probs = jnp.exp(scores - log_norm)
        if first:
            probs = jnp.where(key_pos <= query_pos, probs, 0.0)
        slopes = dot_nt(df[span_of(pair), :], vf[group(j), :])
        slopes = (probs * (slopes - row_dot)).astype(BF16)
        return acc + dot(slopes, keys)

    if n > 2:
        wait(o_far)
        weight_terms(2)
    for h in range(1, m):
        d_h[h - 1]()
        d_y.append(gather_y(lambda i: df.at[span_of(i), :], h, False))
        s_h[h - 1]()
        s_y.append(gather_y(lambda i: st.at[:, span_of(i)], h, False))
    for e in [0, last] + ([1, 2] if n > 2 else []):
        weight_sums(e)
    q_y = gather_full(q_z, lambda i: qf.at[span_of(i), :], False)
    lanes = [slice(h * HEAD, (h + 1) * HEAD) for h in range(2)]

    def project(i):
        total = dot_nt(wx[0, i], of[0])
        for j in others:
            total = total + dot_nt(wx[j, i], of[j])
        return total

    p_x = []
    for e in far:
        target_x = at(x, e)
        px[e] = project(target_x).astype(BF16)
        p_x.append(send(px.at[e], pr.at[e], pr.at[e], x_peer(e)))
    projected = project(x)

    acc = queries_pass(y, True, jnp.zeros((span, HEAD), F32))
    acc = lax.fori_loop(0, y, lambda j, acc: queries_pass(j, False, acc), acc)
    acc = (acc * SCALE).astype(BF16)
    dx[0, 0], dx[0, 1] = acc[:rows], acc[rows:]
    swaps = [send(dx.at[0, 1 - side], dxr.at[0], dxr.at[0], twin)]

    own_key = pair * span + lax.broadcasted_iota(jnp.int32, (span, chunk), 0)
    ask_pos = y * chunk + lax.broadcasted_iota(jnp.int32, (span, chunk), 1)

    def keys_pass(j, first):
        queries = qf[group(j), :]
        ups = df[group(j), :]
        norm = st[0:1, group(j)]
        away = st[1:2, group(j)]
        scores = dot_nt(kf[span_of(pair), :], queries) * SCALE
        probs = jnp.exp(scores - norm)
        if first:
            probs = jnp.where(ask_pos >= own_key, probs, 0.0)
        slopes = dot_nt(vf[span_of(pair), :], ups)
        slopes = (probs * (slopes - away)).astype(BF16)
        sum_k, sum_v = dot(slopes, queries), dot(probs.astype(BF16), ups)
        if first:
            acc_ref[...], sum_ref[...] = sum_k, sum_v
        else:
            acc_ref[...] += sum_k
            sum_ref[...] += sum_v

    keys_pass(y, True)
    for d in others:
        pltpu.make_async_remote_copy(
            src_ref=gyr.at[d],
            dst_ref=gyr.at[d],
            send_sem=send_sems.at[y_base + d],
            recv_sem=recv_sems.at[y_base + d],
            device_id=y_peer(d),
            device_id_type=pl.DeviceIdType.MESH,
        ).wait_recv()
    own_e = lax.rem(dp * m + y // 2 - u + n, n)
    own_i = lax.rem(y, 2) * m
    g_z = []
    for d in list(range(1, m)) + [0]:
        target = at_h(d)
        total = gy[own_e, own_i + target].astype(F32)
        for e in others:
            total = total + gyr[e, target].astype(F32)
        gz[d] = total.astype(BF16)
        if d:
            g_z.append(send(gz.at[d], gzr.at[d - 1], gzr.at[d - 1], h_peer(d)))
    for d in near:

        @pl.when(y + d < n)
        def _(d=d):
            wait(q_y[d], True)
            for h in range(m):
                d_y[h][d](True)
                s_y[h][d](True)
            keys_pass(y + d, False)

    for i, value in ((1, acc_ref[...] * SCALE), (2, sum_ref[...])):
        value = value.astype(BF16)
        dx[i, 0], dx[i, 1] = value[:rows], value[rows:]
        swaps.append(send(dx.at[i, 1 - side], dxr.at[i], dxr.at[i], twin))

    wait(g_z)
    total = gz[0].astype(F32)
    for d in range(1, m):
        total = total + gzr[d - 1].astype(F32)
    gm[0] = total.astype(BF16)
    g_m = send(gm.at[0], gm.at[1], gm.at[1], mirror, moves, moves)
    wait(p_x)
    for e in others:
        projected = projected + pr[e].astype(F32)
    for h in range(2):
        ox[h] = projected[:, lanes[h]].astype(BF16)
    o_s = send(ox.at[1 - side], oxr, oxr, twin)

    o_s()
    out_ref[...] = (ox[side].astype(F32) + oxr[...].astype(F32)).astype(BF16)
    for i, target in enumerate((dq_ref, dk_ref, dv_ref)):
        swaps[i]()
        own, other = dx[i, side], dxr[i]
        for h in range(2):
            target[:, lanes[h]] = jnp.where(side == h, own, other)

    gw_ref[...] = total

    @pl.when(moves)
    def _():
        g_m(True)
        gw_ref[...] = gm[1].astype(F32)

    for finish in issued:
        finish()


def store_all(*refs):
    count = len(refs) // 2
    copies = [
        pltpu.make_async_copy(refs[i], refs[count + i], refs[-1].at[i])
        for i in range(count)
    ]
    for copy in copies:
        copy.start()
    for copy in copies:
        copy.wait()


def shards(n, queries, key_vectors, value_vectors, out_weight, out_grad):
    rows, width = queries.shape[1:]
    cols = out_grad.shape[2]
    blocks, m = n * n, n // 2
    copies = 112
    vmem = pl.BlockSpec(memory_space=pltpu.VMEM)

    def buffer(*shape, kind=BF16):
        return pltpu.VMEM(shape, kind)

    full = buffer(blocks * rows, HEAD)
    span = 2 * rows
    result = pl.pallas_call(
        functools.partial(kernel, n, rows, cols),
        out_shape=(
            jax.ShapeDtypeStruct((cols, rows), BF16),
            jax.ShapeDtypeStruct((rows, width), BF16),
            jax.ShapeDtypeStruct((rows, width), BF16),
            jax.ShapeDtypeStruct((rows, width), BF16),
            jax.ShapeDtypeStruct((cols, HEAD), F32),
        ),
        in_specs=[pl.BlockSpec(memory_space=pltpu.HBM)] * 5,
        out_specs=(vmem,) * 5,
        scratch_shapes=[
            buffer(rows, HEAD),
            buffer(rows, HEAD),
            buffer(rows, HEAD),
            buffer(cols, HEAD),
            full,
            full,
            full,
            full,
            buffer(8, blocks * rows, kind=F32),
            buffer(blocks, cols, HEAD),
            buffer(n, span, cols),
            buffer(n, cols, span),
            buffer(n, n, cols, HEAD),
            buffer(n, cols, span),
            buffer(n, cols, span),
            buffer(n, span, HEAD),
            buffer(n, span, HEAD),
            buffer(2, rows, HEAD),
            buffer(n, span, HEAD),
            buffer(span, HEAD, kind=F32),
            buffer(span, HEAD, kind=F32),
            buffer(span, HEAD, kind=F32),
            buffer(n, n, cols, HEAD),
            buffer(n, n, cols, HEAD),
            buffer(n, n, cols, HEAD),
            buffer(n, m, cols, HEAD),
            buffer(m, cols, HEAD),
            buffer(max(m - 1, 1), cols, HEAD),
            buffer(2, cols, HEAD),
            buffer(2, cols, rows),
            buffer(cols, rows),
            buffer(3, 2, rows, HEAD),
            buffer(3, rows, HEAD),
            pltpu.SemaphoreType.DMA((9,)),
            pltpu.SemaphoreType.DMA((copies,)),
            pltpu.SemaphoreType.DMA((copies,)),
        ],
        compiler_params=pltpu.CompilerParams(
            collective_id=0, has_side_effects=True, vmem_limit_bytes=64 << 20
        ),
    )(queries[0], key_vectors[0], value_vectors[0], out_weight.T, out_grad[0].T)
    result = pl.pallas_call(
        store_all,
        out_shape=[jax.ShapeDtypeStruct(a.shape, a.dtype) for a in result],
        in_specs=[vmem] * 5,
        out_specs=[pl.BlockSpec(memory_space=pltpu.HBM)] * 5,
        scratch_shapes=[pltpu.SemaphoreType.DMA((5,))],
    )(*result)
    output, grad_queries, grad_keys, grad_values, grad_weight = result
    return (
        output.T[None],
        grad_queries[None],
        grad_keys[None],
        grad_values[None],
        grad_weight.T,
    )


def solution(mesh):
    n = math.isqrt(mesh.shape["row"])
    return jax.shard_map(
        functools.partial(shards, n),
        mesh=mesh,
        in_specs=(
            P("dp", "row", "col"),
            P("dp", "row", "col"),
            P("dp", "row", "col"),
            P("row", "col"),
            P("dp", "row", "col"),
        ),
        out_specs=(
            P("dp", "row", "col"),
            P("dp", "row", "col"),
            P("dp", "row", "col"),
            P("dp", "row", "col"),
            P(("dp", "row"), "col"),
        ),
        check_vma=False,
    )
```

```python
import functools
import math

import jax
import jax.numpy as jnp
from jax import lax
from jax.experimental import pallas as pl
from jax.experimental.pallas import tpu as pltpu
from jax.sharding import PartitionSpec as P

HEAD = 128
NEG = -1e30
SCALE = 1.0 / math.sqrt(HEAD)
F32 = jnp.float32
BF16 = jnp.bfloat16
NT = (((1,), (1,)), ((), ()))
TN = (((0,), (0,)), ((), ()))


def dot(a, b):
    return jnp.dot(a, b, preferred_element_type=F32)


def dot_nt(a, b):
    return lax.dot_general(a, b, NT, preferred_element_type=F32)


def flip(a):
    size = a.shape[0]
    eye = (
        lax.broadcasted_iota(jnp.int32, (size, size), 0)
        == lax.broadcasted_iota(jnp.int32, (size, size), 1)
    )
    eye = jnp.where(eye, 1.0, 0.0).astype(BF16)
    return lax.dot_general(a, eye, TN, preferred_element_type=F32).astype(BF16)


def kernel(
    n,
    rows,
    cols,
    q_hbm,
    k_hbm,
    v_hbm,
    w_hbm,
    g_hbm,
    out_ref,
    dq_ref,
    dk_ref,
    dv_ref,
    gw_ref,
    qs,
    ks,
    vs,
    ws,
    kf,
    vf,
    qf,
    df,
    st,
    wf,
    gf,
    gt,
    hs,
    hx,
    hz,
    hr,
    hq,
    of,
    top_ref,
    sum_ref,
    acc_ref,
    gp,
    gd,
    gy,
    gyr,
    gz,
    gzr,
    ox,
    oxr,
    dx,
    dxr,
    load_sems,
    send_sems,
    recv_sems,
):
    dp, row, col = lax.axis_index("dp"), lax.axis_index("row"), lax.axis_index("col")
    m = n // 2
    y, z = row // n, lax.rem(row, n)
    zh, side = z // 2, lax.rem(z, 2)
    u, x = col // n, lax.rem(col, n)
    pair = y * m + zh
    span = 2 * rows
    chunk = n * rows
    others = list(range(1, n))
    far = sorted(others, key=lambda d: -min(d, n - d))
    near = far[::-1]
    z_steps = [(h, t) for h in range(m) for t in (1, 0) if h or t]

    def at(base, d):
        return lax.rem(base + d + n, n)

    def at_h(d):
        return lax.rem(zh + d + m, m)

    dp_peer = {"dp": 1 - dp}
    twin = {"row": row + 1 - 2 * side}

    def z_row(h, t):
        return y * n + 2 * at_h(h) + (1 - side if t else side)

    def h_peer(d):
        return {"row": z_row(d, 0)}

    def y_peer(d):
        return {"row": at(y, d) * n + z}

    def u_peer(d):
        return {"col": at(u, d) * n + x}

    def x_peer(d):
        return {"col": u * n + at(x, d)}

    def block(i):
        return pl.ds(pl.multiple_of(i * rows, rows), rows)

    def span_of(i):
        return pl.ds(pl.multiple_of(i * span, span), span)

    def group(i):
        return pl.ds(pl.multiple_of(i * chunk, chunk), chunk)

    half = cols // 2
    mine = pl.ds(pl.multiple_of(dp * half, half), half)
    theirs = pl.ds(pl.multiple_of((1 - dp) * half, half), half)
    own_lanes = block(side)
    other_lanes = block(1 - side)

    pieces = [
        (w_hbm.at[mine, own_lanes], wf.at[row, mine, :]),
        (w_hbm.at[mine, other_lanes], ws.at[mine, :]),
        (g_hbm, gt.at[:, own_lanes]),
    ]
    for source, split, full in ((k_hbm, ks, kf), (q_hbm, qs, qf), (v_hbm, vs, vf)):
        pieces.append((source.at[:, own_lanes], full.at[block(row), :]))
        pieces.append((source.at[:, other_lanes], split))
    loads = [
        pltpu.make_async_copy(source, target, load_sems.at[i])
        for i, (source, target) in enumerate(pieces)
    ]

    barrier = pltpu.get_barrier_semaphore()
    peers = [dp_peer] + [{"row": z_row(h, t)} for h, t in z_steps]
    peers += [u_peer(d) for d in sorted({1, n - 1})]
    peers += [f(d) for f in (y_peer, x_peer) for d in far]
    for peer in peers:
        pl.semaphore_signal(
            barrier, inc=1, device_id=peer, device_id_type=pl.DeviceIdType.MESH
        )
    for load in loads:
        load.start()

    issued = []
    slots = [0]

    def when(cond, body):
        if cond is None:
            body()
        else:
            pl.when(cond)(body)

    def take(count):
        slots[0] += count
        return slots[0] - count

    def send(src, dst, landed, peer, sends=None, receives=None, index=None):
        index = take(1) if index is None else index

        def describe(source, target, which):
            return pltpu.make_async_remote_copy(
                src_ref=source,
                dst_ref=target,
                send_sem=send_sems.at[which],
                recv_sem=recv_sems.at[which],
                device_id=peer,
                device_id_type=pl.DeviceIdType.MESH,
            )

        when(sends, lambda: describe(src, dst, index).start())
        issued.append(
            lambda: when(sends, lambda: describe(src, dst, index).wait_send())
        )
        if landed is None:
            return None
        return lambda inside=False: when(
            None if inside else receives,
            lambda: describe(landed, landed, index).wait_recv(),
        )

    def wait(handles, *inside):
        for handle in handles:
            handle(*inside)

    def spread_z(own, split, view, steps):
        return {
            (h, t): send(
                split if t else own, view(row), view(z_row(-h, t)), {"row": z_row(h, t)}
            )
            for h, t in steps
        }

    def gather_h(view):
        return [
            send(view(pair), view(pair), view(y * m + at_h(-d)), h_peer(d))
            for d in range(1, m)
        ]

    def gather_y(view, h, up):
        handles = {}
        for d in near:
            if up is None:
                sends = receives = None
            elif up:
                sends, receives = y + d < n, y >= d
            else:
                sends, receives = y >= d, y + d < n
            s = -1 if up is False else 1
            mid = at_h(-h)
            handles[d] = send(
                view(y * m + mid),
                view(y * m + mid),
                view(at(y, -s * d) * m + mid),
                y_peer(s * d),
                sends,
                receives,
            )
        return handles

    def gather_full(arrived, view, up):
        handles = []
        for h in range(m):
            wait([arrived[step] for step in z_steps if step[0] == h and step in arrived])
            handles.append(gather_y(view, h, up))
        return {d: [piece[d] for piece in handles] for d in near}

    def k_view(i):
        return kf.at[block(i), :]

    def w_pair(i):
        return wf.at[pl.ds(2 * i, 2), mine, :]

    def w_group(i, part=mine):
        return wf.at[pl.ds(i * n, n), part, :]

    wait([load.wait for load in loads])
    pl.semaphore_wait(barrier, len(peers))

    w_z = spread_z(
        wf.at[row, mine, :], ws.at[mine, :], lambda i: wf.at[i, mine, :], z_steps
    )
    g_s = send(gt.at[:, own_lanes], gt.at[:, own_lanes], gt.at[:, other_lanes], twin)
    w_parts = []
    for h in range(m):
        wait([w_z[step] for step in z_steps if step[0] == h])
        w_parts.append(gather_y(w_pair, h, None))
        if h == 0:
            k_z = spread_z(
                kf.at[block(row), :], ks, lambda i: kf.at[block(i), :], z_steps
            )
    w_d = {0: send(w_group(y), w_group(y), w_group(y, theirs), dp_peer)}
    q_s = spread_z(qf.at[block(row), :], qs, lambda i: qf.at[block(i), :], z_steps[:1])
    v_z = spread_z(vf.at[block(row), :], vs, lambda i: vf.at[block(i), :], z_steps)
    g_s()
    gf[...] = flip(gt[...])

    x_base = take(n * (n - 1))

    def x_send(d, e):
        index = x_base + d * (n - 1) + e - 1
        send(hs.at[d, e], hx.at[d, e - 1], None, x_peer(e), index=index)

    def head_terms(d):
        w_d[d]()
        for e in far + [0]:
            hs[d, e] = dot(gf[...], wf[at(y, d) * n + at(x, e)]).astype(BF16)
            if e:
                x_send(d, e)

    def head_sums(e):
        d = lax.rem(u + e - y + n, n)
        total = hs[d, 0].astype(F32)
        for k in far:
            pltpu.make_async_remote_copy(
                src_ref=hx.at[d, k - 1],
                dst_ref=hx.at[d, k - 1],
                send_sem=send_sems.at[x_base + d * (n - 1) + k - 1],
                recv_sem=recv_sems.at[x_base + d * (n - 1) + k - 1],
                device_id=x_peer(k),
                device_id_type=pl.DeviceIdType.MESH,
            ).wait_recv()
            total = total + hx[d, k - 1].astype(F32)
        return total

    head_terms(0)
    k_y = gather_full(k_z, lambda i: kf.at[span_of(i), :], True)
    v_y = gather_full(v_z, lambda i: vf.at[span_of(i), :], True)

    query_pos = pair * span + lax.broadcasted_iota(jnp.int32, (span, chunk), 0)
    key_pos = y * chunk + lax.broadcasted_iota(jnp.int32, (span, chunk), 1)

    def forward(j, first):
        scores = dot_nt(qf[span_of(pair), :], kf[group(j), :]) * SCALE
        if first:
            scores = jnp.where(key_pos <= query_pos, scores, NEG)
        new_top = jnp.max(scores, axis=1, keepdims=True)
        if not first:
            top = top_ref[:, :1]
            new_top = jnp.maximum(top, new_top)
        weights = jnp.exp(scores - new_top)
        total = jnp.sum(weights, axis=1, keepdims=True)
        acc = dot(weights.astype(BF16), vf[group(j), :])
        if not first:
            fade = jnp.exp(top - new_top)
            total = fade * sum_ref[:, :1] + total
            acc = fade * acc_ref[...] + acc
        top_ref[...] = jnp.broadcast_to(new_top, top_ref.shape)
        sum_ref[...] = jnp.broadcast_to(total, sum_ref.shape)
        acc_ref[...] = acc

    for d in near:
        wait([part[d] for part in w_parts])
        source = at(y, -d)
        w_d[n - d] = send(w_group(source), w_group(source), w_group(source, theirs), dp_peer)
    wait(q_s.values())
    forward(y, True)
    for d in near:
        head_terms(n - d)
    q_z = spread_z(qf.at[block(row), :], qs, lambda i: qf.at[block(i), :], z_steps[1:])
    for d in near:

        @pl.when(y >= d)
        def _(d=d):
            wait(k_y[d], True)
            wait(v_y[d], True)
            forward(y - d, False)

    own_of = x * n + u
    total = sum_ref[:, :1]
    of[own_of] = (acc_ref[...] / total).astype(BF16)
    log_norm = top_ref[:, :1] + jnp.log(total)
    last = n - 1
    low, high = slice(0, rows), slice(rows, span)
    before, after = x * n + at(u, -1), x * n + at(u, 1)
    beyond = x * n + at(u, 2)

    o_u = [send(of.at[own_of], of.at[own_of], of.at[before], u_peer(1))]
    if n > 2:
        o_u.append(send(of.at[own_of], of.at[own_of], of.at[after], u_peer(last)))

    def spread_x(e):
        return [
            send(
                of.at[x * n + at(u, e)],
                of.at[x * n + at(u, e)],
                of.at[at(x, -d) * n + at(u, e)],
                x_peer(d),
            )
            for d in far
        ]

    o_x = {0: spread_x(0)}
    h_u = []
    if n > 2:
        hz[2] = head_sums(2).astype(BF16)
        relay = [
            send(hz.at[2, low, :], hq.at[0], hq.at[0], u_peer(1)),
            send(hz.at[2, high, :], hq.at[1], hq.at[1], u_peer(last)),
        ]
        for e, part in ((1, high), (last, low)):
            hz[e] = head_sums(e).astype(BF16)
            h_u.append(
                send(hz.at[e, part, :], hr.at[e, part, :], hr.at[e, part, :], u_peer(e))
            )
        for i, e, part in ((0, 1, low), (1, last, high)):
            relay[i]()
            hz[e, part, :] = (hz[e, part, :].astype(F32) + hq[i].astype(F32)).astype(
                BF16
            )
            h_u.append(
                send(hz.at[e, part, :], hr.at[e, part, :], hr.at[e, part, :], u_peer(e))
            )
    else:
        hz[1] = head_sums(1).astype(BF16)
        h_u.append(send(hz.at[1], hr.at[1], hr.at[1], u_peer(1)))
    o_far = []
    o_u[0]()
    if n > 2:
        o_far.append(
            send(of.at[before, low, :], of.at[before, low, :], of.at[beyond, low, :], u_peer(1))
        )
        o_u[1]()
        o_far.append(
            send(of.at[after, high, :], of.at[after, high, :], of.at[beyond, high, :], u_peer(last))
        )
        o_x[1] = spread_x(1)
    o_x[last] = spread_x(-1)

    y_base = take(n)

    def weight_terms(e):
        wait(o_x[e])
        target = at(u, e)
        for i in range(n):
            gp[e, i] = dot(gt[...], of[i * n + target]).astype(BF16)
        ours = target // m == dp
        arrived = send(
            gp.at[e], gd.at[e], gd.at[e], dp_peer, target // m != dp, ours
        )
        arrived()

        @pl.when(ours)
        def _():
            for i in range(n):
                gy[e, i] = (gp[e, i].astype(F32) + gd[e, i].astype(F32)).astype(BF16)

        for i in range(2):
            target_y = 2 * lax.rem(target, m) + i
            d = lax.rem(target_y - y + n, n)
            send(
                gy.at[e, pl.ds(i * m, m)],
                gyr.at[d],
                None,
                {"row": target_y * n + z},
                jnp.logical_and(ours, target_y != y),
                index=y_base + d,
            )

    weight_terms(0)
    upstream = head_sums(0)
    q_y = gather_full(q_z, lambda i: qf.at[span_of(i), :], False)
    if n > 2:
        wait(o_far)
        o_x[2] = spread_x(2)
    wait(h_u)
    for e in sorted({1, last}):
        upstream = upstream + hr[e].astype(F32)
    df[span_of(pair), :] = upstream.astype(BF16)
    d_h = gather_h(lambda i: df.at[span_of(i), :])
    d_y = [gather_y(lambda i: df.at[span_of(i), :], 0, False)]
    attended = of[own_of].astype(F32)
    row_dot = jnp.sum(
        df[span_of(pair), :].astype(F32) * attended, axis=1, keepdims=True
    )
    lane = lax.broadcasted_iota(jnp.int32, (span, HEAD), 1)
    table = jnp.where(lane == 0, log_norm, jnp.where(lane == 1, row_dot, 0.0))
    st[:, span_of(pair)] = jnp.transpose(table)[:8, :]
    s_h = gather_h(lambda i: st.at[:, span_of(i)])
    s_y = [gather_y(lambda i: st.at[:, span_of(i)], 0, False)]

    def queries_pass(j, first, acc):
        keys = kf[group(j), :]
        scores = dot_nt(qf[span_of(pair), :], keys) * SCALE
        probs = jnp.exp(scores - log_norm)
        if first:
            probs = jnp.where(key_pos <= query_pos, probs, 0.0)
        slopes = dot_nt(df[span_of(pair), :], vf[group(j), :])
        slopes = (probs * (slopes - row_dot)).astype(BF16)
        return acc + dot(slopes, keys)

    weight_terms(last)
    for h in range(1, m):
        d_h[h - 1]()
        d_y.append(gather_y(lambda i: df.at[span_of(i), :], h, False))
        s_h[h - 1]()
        s_y.append(gather_y(lambda i: st.at[:, span_of(i)], h, False))
    if n > 2:
        weight_terms(1)
    acc = queries_pass(y, True, jnp.zeros((span, HEAD), F32))
    acc = lax.fori_loop(0, y, lambda j, acc: queries_pass(j, False, acc), acc)
    acc = (acc * SCALE).astype(BF16)
    dx[0, 0], dx[0, 1] = acc[:rows], acc[rows:]
    swaps = [send(dx.at[0, 1 - side], dxr.at[0], dxr.at[0], twin)]
    if n > 2:
        weight_terms(2)

    lanes = [slice(h * HEAD, (h + 1) * HEAD) for h in range(2)]

    projected = jnp.zeros((cols, span), F32)
    for c in range(n * n):
        projected = projected + dot_nt(wf[c], of[c % n * n + c // n])
    for h in range(2):
        ox[h] = projected[:, lanes[h]].astype(BF16)
    o_s = send(ox.at[1 - side], oxr, oxr, twin)

    own_key = pair * span + lax.broadcasted_iota(jnp.int32, (span, chunk), 0)
    ask_pos = y * chunk + lax.broadcasted_iota(jnp.int32, (span, chunk), 1)

    def keys_pass(j, first):
        queries = qf[group(j), :]
        ups = df[group(j), :]
        norm = st[0:1, group(j)]
        away = st[1:2, group(j)]
        scores = dot_nt(kf[span_of(pair), :], queries) * SCALE
        probs = jnp.exp(scores - norm)
        if first:
            probs = jnp.where(ask_pos >= own_key, probs, 0.0)
        slopes = dot_nt(vf[span_of(pair), :], ups)
        slopes = (probs * (slopes - away)).astype(BF16)
        sum_k, sum_v = dot(slopes, queries), dot(probs.astype(BF16), ups)
        if first:
            acc_ref[...], sum_ref[...] = sum_k, sum_v
        else:
            acc_ref[...] += sum_k
            sum_ref[...] += sum_v

    keys_pass(y, True)

    for d in others:
        pltpu.make_async_remote_copy(
            src_ref=gyr.at[d],
            dst_ref=gyr.at[d],
            send_sem=send_sems.at[y_base + d],
            recv_sem=recv_sems.at[y_base + d],
            device_id=y_peer(d),
            device_id_type=pl.DeviceIdType.MESH,
        ).wait_recv()
    own_e = lax.rem(dp * m + y // 2 - u + n, n)
    own_i = lax.rem(y, 2) * m
    g_z = []
    for d in list(range(1, m)) + [0]:
        target = at_h(d)
        total = gy[own_e, own_i + target].astype(F32)
        for e in others:
            total = total + gyr[e, target].astype(F32)
        gz[d] = total.astype(BF16)
        if d:
            g_z.append(send(gz.at[d], gzr.at[d - 1], gzr.at[d - 1], h_peer(d)))
    for d in near:

        @pl.when(y + d < n)
        def _(d=d):
            wait(q_y[d], True)
            for h in range(m):
                d_y[h][d](True)
                s_y[h][d](True)
            keys_pass(y + d, False)

    for i, value in ((1, acc_ref[...] * SCALE), (2, sum_ref[...])):
        value = value.astype(BF16)
        dx[i, 0], dx[i, 1] = value[:rows], value[rows:]
        swaps.append(send(dx.at[i, 1 - side], dxr.at[i], dxr.at[i], twin))

    wait(g_z)
    total = gz[0].astype(F32)
    for d in range(1, m):
        total = total + gzr[d - 1].astype(F32)
    gw_ref[...] = total
    o_s()
    out_ref[...] = (ox[side].astype(F32) + oxr[...].astype(F32)).astype(BF16)
    for i, target in enumerate((dq_ref, dk_ref, dv_ref)):
        swaps[i]()
        own, other = dx[i, side], dxr[i]
        for h in range(2):
            target[:, lanes[h]] = jnp.where(side == h, own, other)

    for finish in issued:
        finish()


def store_all(*refs):
    count = len(refs) // 2
    copies = [
        pltpu.make_async_copy(refs[i], refs[count + i], refs[-1].at[i])
        for i in range(count)
    ]
    for copy in copies:
        copy.start()
    for copy in copies:
        copy.wait()


def shards(n, queries, key_vectors, value_vectors, out_weight, out_grad):
    rows, width = queries.shape[1:]
    cols = out_grad.shape[2]
    blocks, m = n * n, n // 2
    copies = 112
    vmem = pl.BlockSpec(memory_space=pltpu.VMEM)

    def buffer(*shape, kind=BF16):
        return pltpu.VMEM(shape, kind)

    full = buffer(blocks * rows, HEAD)
    span = 2 * rows
    result = pl.pallas_call(
        functools.partial(kernel, n, rows, cols),
        out_shape=(
            jax.ShapeDtypeStruct((cols, rows), BF16),
            jax.ShapeDtypeStruct((rows, width), BF16),
            jax.ShapeDtypeStruct((rows, width), BF16),
            jax.ShapeDtypeStruct((rows, width), BF16),
            jax.ShapeDtypeStruct((cols, HEAD), F32),
        ),
        in_specs=[pl.BlockSpec(memory_space=pltpu.HBM)] * 5,
        out_specs=(vmem,) * 5,
        scratch_shapes=[
            buffer(rows, HEAD),
            buffer(rows, HEAD),
            buffer(rows, HEAD),
            buffer(cols, HEAD),
            full,
            full,
            full,
            full,
            buffer(8, blocks * rows, kind=F32),
            buffer(blocks, cols, HEAD),
            buffer(span, cols),
            buffer(cols, span),
            buffer(n, n, span, HEAD),
            buffer(n, n - 1, span, HEAD),
            buffer(n, span, HEAD),
            buffer(n, span, HEAD),
            buffer(2, rows, HEAD),
            buffer(blocks, span, HEAD),
            buffer(span, HEAD, kind=F32),
            buffer(span, HEAD, kind=F32),
            buffer(span, HEAD, kind=F32),
            buffer(n, n, cols, HEAD),
            buffer(n, n, cols, HEAD),
            buffer(n, n, cols, HEAD),
            buffer(n, m, cols, HEAD),
            buffer(m, cols, HEAD),
            buffer(max(m - 1, 1), cols, HEAD),
            buffer(2, cols, rows),
            buffer(cols, rows),
            buffer(3, 2, rows, HEAD),
            buffer(3, rows, HEAD),
            pltpu.SemaphoreType.DMA((9,)),
            pltpu.SemaphoreType.DMA((copies,)),
            pltpu.SemaphoreType.DMA((copies,)),
        ],
        compiler_params=pltpu.CompilerParams(
            collective_id=0, has_side_effects=True, vmem_limit_bytes=64 << 20
        ),
    )(queries[0], key_vectors[0], value_vectors[0], out_weight.T, out_grad[0].T)
    result = pl.pallas_call(
        store_all,
        out_shape=[jax.ShapeDtypeStruct(a.shape, a.dtype) for a in result],
        in_specs=[vmem] * 5,
        out_specs=[pl.BlockSpec(memory_space=pltpu.HBM)] * 5,
        scratch_shapes=[pltpu.SemaphoreType.DMA((5,))],
    )(*result)
    output, grad_queries, grad_keys, grad_values, grad_weight = result
    return (
        output.T[None],
        grad_queries[None],
        grad_keys[None],
        grad_values[None],
        grad_weight.T,
    )


def solution(mesh):
    n = math.isqrt(mesh.shape["row"])
    return jax.shard_map(
        functools.partial(shards, n),
        mesh=mesh,
        in_specs=(
            P("dp", "row", "col"),
            P("dp", "row", "col"),
            P("dp", "row", "col"),
            P("row", "col"),
            P("dp", "row", "col"),
        ),
        out_specs=(
            P("dp", "row", "col"),
            P("dp", "row", "col"),
            P("dp", "row", "col"),
            P("dp", "row", "col"),
            P(("dp", "row"), "col"),
        ),
        check_vma=False,
    )
```

```python
import functools
import math

import jax
import jax.numpy as jnp
from jax import lax
from jax.experimental import pallas as pl
from jax.experimental.pallas import tpu as pltpu
from jax.sharding import PartitionSpec as P

HEAD = 128
NEG = -1e30
SCALE = 1.0 / math.sqrt(HEAD)
F32 = jnp.float32
BF16 = jnp.bfloat16
NT = (((1,), (1,)), ((), ()))
TN = (((0,), (0,)), ((), ()))


def dot(a, b):
    return jnp.dot(a, b, preferred_element_type=F32)


def dot_nt(a, b):
    return lax.dot_general(a, b, NT, preferred_element_type=F32)


def flip(a):
    size = a.shape[0]
    eye = (
        lax.broadcasted_iota(jnp.int32, (size, size), 0)
        == lax.broadcasted_iota(jnp.int32, (size, size), 1)
    )
    eye = jnp.where(eye, 1.0, 0.0).astype(BF16)
    return lax.dot_general(a, eye, TN, preferred_element_type=F32).astype(BF16)


def kernel(
    n,
    rows,
    cols,
    q_hbm,
    k_hbm,
    v_hbm,
    w_hbm,
    g_hbm,
    out_ref,
    dq_ref,
    dk_ref,
    dv_ref,
    gw_ref,
    qs,
    ks,
    vs,
    ws,
    kf,
    vf,
    qf,
    df,
    st,
    wf,
    gf,
    gt,
    hs,
    hx,
    hz,
    hr,
    hq,
    of,
    top_ref,
    sum_ref,
    acc_ref,
    gp,
    gd,
    gy,
    gyr,
    gz,
    gzr,
    ox,
    oxr,
    dx,
    dxr,
    load_sems,
    send_sems,
    recv_sems,
):
    dp, row, col = lax.axis_index("dp"), lax.axis_index("row"), lax.axis_index("col")
    m = n // 2
    y, z = row // n, lax.rem(row, n)
    zh, side = z // 2, lax.rem(z, 2)
    u, x = col // n, lax.rem(col, n)
    pair = y * m + zh
    span = 2 * rows
    chunk = n * rows
    others = list(range(1, n))
    far = sorted(others, key=lambda d: -min(d, n - d))
    near = far[::-1]
    z_steps = [(h, t) for h in range(m) for t in (1, 0) if h or t]

    def at(base, d):
        return lax.rem(base + d + n, n)

    def at_h(d):
        return lax.rem(zh + d + m, m)

    dp_peer = {"dp": 1 - dp}
    twin = {"row": row + 1 - 2 * side}

    def z_row(h, t):
        return y * n + 2 * at_h(h) + (1 - side if t else side)

    def h_peer(d):
        return {"row": z_row(d, 0)}

    def y_peer(d):
        return {"row": at(y, d) * n + z}

    def u_peer(d):
        return {"col": at(u, d) * n + x}

    def x_peer(d):
        return {"col": u * n + at(x, d)}

    def block(i):
        return pl.ds(pl.multiple_of(i * rows, rows), rows)

    def span_of(i):
        return pl.ds(pl.multiple_of(i * span, span), span)

    def group(i):
        return pl.ds(pl.multiple_of(i * chunk, chunk), chunk)

    half = cols // 2
    mine = pl.ds(pl.multiple_of(dp * half, half), half)
    theirs = pl.ds(pl.multiple_of((1 - dp) * half, half), half)
    own_lanes = block(side)
    other_lanes = block(1 - side)

    pieces = [
        (w_hbm.at[mine, own_lanes], wf.at[row, mine, :]),
        (w_hbm.at[mine, other_lanes], ws.at[mine, :]),
        (g_hbm, gt.at[:, own_lanes]),
    ]
    for source, split, full in ((k_hbm, ks, kf), (q_hbm, qs, qf), (v_hbm, vs, vf)):
        pieces.append((source.at[:, own_lanes], full.at[block(row), :]))
        pieces.append((source.at[:, other_lanes], split))
    loads = [
        pltpu.make_async_copy(source, target, load_sems.at[i])
        for i, (source, target) in enumerate(pieces)
    ]

    barrier = pltpu.get_barrier_semaphore()
    peers = [dp_peer] + [{"row": z_row(h, t)} for h, t in z_steps]
    peers += [u_peer(d) for d in sorted({1, n - 1})]
    peers += [f(d) for f in (y_peer, x_peer) for d in far]
    for peer in peers:
        pl.semaphore_signal(
            barrier, inc=1, device_id=peer, device_id_type=pl.DeviceIdType.MESH
        )
    for load in loads:
        load.start()

    issued = []
    slots = [0]

    def when(cond, body):
        if cond is None:
            body()
        else:
            pl.when(cond)(body)

    def take(count):
        slots[0] += count
        return slots[0] - count

    def send(src, dst, landed, peer, sends=None, receives=None, index=None):
        index = take(1) if index is None else index

        def describe(source, target, which):
            return pltpu.make_async_remote_copy(
                src_ref=source,
                dst_ref=target,
                send_sem=send_sems.at[which],
                recv_sem=recv_sems.at[which],
                device_id=peer,
                device_id_type=pl.DeviceIdType.MESH,
            )

        when(sends, lambda: describe(src, dst, index).start())
        issued.append(
            lambda: when(sends, lambda: describe(src, dst, index).wait_send())
        )
        if landed is None:
            return None
        return lambda inside=False: when(
            None if inside else receives,
            lambda: describe(landed, landed, index).wait_recv(),
        )

    def wait(handles, *inside):
        for handle in handles:
            handle(*inside)

    def spread_z(own, split, view, steps):
        return {
            (h, t): send(
                split if t else own, view(row), view(z_row(-h, t)), {"row": z_row(h, t)}
            )
            for h, t in steps
        }

    def gather_h(view):
        return [
            send(view(pair), view(pair), view(y * m + at_h(-d)), h_peer(d))
            for d in range(1, m)
        ]

    def gather_y(view, h, up):
        handles = {}
        for d in near:
            if up is None:
                sends = receives = None
            elif up:
                sends, receives = y + d < n, y >= d
            else:
                sends, receives = y >= d, y + d < n
            s = -1 if up is False else 1
            mid = at_h(-h)
            handles[d] = send(
                view(y * m + mid),
                view(y * m + mid),
                view(at(y, -s * d) * m + mid),
                y_peer(s * d),
                sends,
                receives,
            )
        return handles

    def gather_full(arrived, view, up):
        handles = []
        for h in range(m):
            wait([arrived[step] for step in z_steps if step[0] == h and step in arrived])
            handles.append(gather_y(view, h, up))
        return {d: [piece[d] for piece in handles] for d in near}

    def k_view(i):
        return kf.at[block(i), :]

    def w_pair(i):
        return wf.at[pl.ds(2 * i, 2), mine, :]

    def w_group(i, part=mine):
        return wf.at[pl.ds(i * n, n), part, :]

    wait([load.wait for load in loads])
    pl.semaphore_wait(barrier, len(peers))

    w_z = spread_z(
        wf.at[row, mine, :], ws.at[mine, :], lambda i: wf.at[i, mine, :], z_steps
    )
    g_s = send(gt.at[:, own_lanes], gt.at[:, own_lanes], gt.at[:, other_lanes], twin)
    w_parts = []
    for h in range(m):
        wait([w_z[step] for step in z_steps if step[0] == h])
        w_parts.append(gather_y(w_pair, h, None))
        if h == 0:
            k_z = spread_z(
                kf.at[block(row), :], ks, lambda i: kf.at[block(i), :], z_steps
            )
    w_d = {0: send(w_group(y), w_group(y), w_group(y, theirs), dp_peer)}
    q_s = spread_z(qf.at[block(row), :], qs, lambda i: qf.at[block(i), :], z_steps[:1])
    v_z = spread_z(vf.at[block(row), :], vs, lambda i: vf.at[block(i), :], z_steps)
    q_z = spread_z(qf.at[block(row), :], qs, lambda i: qf.at[block(i), :], z_steps[1:])
    g_s()
    gf[...] = flip(gt[...])

    x_base = take(n * (n - 1))

    def x_send(d, e):
        index = x_base + d * (n - 1) + e - 1
        send(hs.at[d, e], hx.at[d, e - 1], None, x_peer(e), index=index)

    def head_terms(d):
        w_d[d]()
        for e in far + [0]:
            hs[d, e] = dot(gf[...], wf[at(y, d) * n + at(x, e)]).astype(BF16)
            if e:
                x_send(d, e)

    def head_sums(e):
        d = lax.rem(u + e - y + n, n)
        total = hs[d, 0].astype(F32)
        for k in far:
            pltpu.make_async_remote_copy(
                src_ref=hx.at[d, k - 1],
                dst_ref=hx.at[d, k - 1],
                send_sem=send_sems.at[x_base + d * (n - 1) + k - 1],
                recv_sem=recv_sems.at[x_base + d * (n - 1) + k - 1],
                device_id=x_peer(k),
                device_id_type=pl.DeviceIdType.MESH,
            ).wait_recv()
            total = total + hx[d, k - 1].astype(F32)
        return total

    head_terms(0)
    k_y = gather_full(k_z, lambda i: kf.at[span_of(i), :], True)
    v_y = gather_full(v_z, lambda i: vf.at[span_of(i), :], True)

    query_pos = pair * span + lax.broadcasted_iota(jnp.int32, (span, chunk), 0)
    key_pos = y * chunk + lax.broadcasted_iota(jnp.int32, (span, chunk), 1)

    def forward(j, first):
        scores = dot_nt(qf[span_of(pair), :], kf[group(j), :]) * SCALE
        if first:
            scores = jnp.where(key_pos <= query_pos, scores, NEG)
        new_top = jnp.max(scores, axis=1, keepdims=True)
        if not first:
            top = top_ref[:, :1]
            new_top = jnp.maximum(top, new_top)
        weights = jnp.exp(scores - new_top)
        total = jnp.sum(weights, axis=1, keepdims=True)
        acc = dot(weights.astype(BF16), vf[group(j), :])
        if not first:
            fade = jnp.exp(top - new_top)
            total = fade * sum_ref[:, :1] + total
            acc = fade * acc_ref[...] + acc
        top_ref[...] = jnp.broadcast_to(new_top, top_ref.shape)
        sum_ref[...] = jnp.broadcast_to(total, sum_ref.shape)
        acc_ref[...] = acc

    for d in near:
        wait([part[d] for part in w_parts])
        source = at(y, -d)
        w_d[n - d] = send(w_group(source), w_group(source), w_group(source, theirs), dp_peer)
    wait(q_s.values())
    forward(y, True)
    for d in near:
        head_terms(n - d)
    for d in near:

        @pl.when(y >= d)
        def _(d=d):
            wait(k_y[d], True)
            wait(v_y[d], True)
            forward(y - d, False)

    own_of = x * n + u
    total = sum_ref[:, :1]
    of[own_of] = (acc_ref[...] / total).astype(BF16)
    log_norm = top_ref[:, :1] + jnp.log(total)
    last = n - 1
    low, high = slice(0, rows), slice(rows, span)
    before, after = x * n + at(u, -1), x * n + at(u, 1)
    beyond = x * n + at(u, 2)

    o_u = [send(of.at[own_of], of.at[own_of], of.at[before], u_peer(1))]
    if n > 2:
        o_u.append(send(of.at[own_of], of.at[own_of], of.at[after], u_peer(last)))

    def spread_x(e):
        return [
            send(
                of.at[x * n + at(u, e)],
                of.at[x * n + at(u, e)],
                of.at[at(x, -d) * n + at(u, e)],
                x_peer(d),
            )
            for d in far
        ]

    o_x = {0: spread_x(0)}
    h_u = []
    if n > 2:
        hz[2] = head_sums(2).astype(BF16)
        relay = [
            send(hz.at[2, low, :], hq.at[0], hq.at[0], u_peer(1)),
            send(hz.at[2, high, :], hq.at[1], hq.at[1], u_peer(last)),
        ]
        for e, part in ((1, high), (last, low)):
            hz[e] = head_sums(e).astype(BF16)
            h_u.append(
                send(hz.at[e, part, :], hr.at[e, part, :], hr.at[e, part, :], u_peer(e))
            )
        for i, e, part in ((0, 1, low), (1, last, high)):
            relay[i]()
            hz[e, part, :] = (hz[e, part, :].astype(F32) + hq[i].astype(F32)).astype(
                BF16
            )
            h_u.append(
                send(hz.at[e, part, :], hr.at[e, part, :], hr.at[e, part, :], u_peer(e))
            )
    else:
        hz[1] = head_sums(1).astype(BF16)
        h_u.append(send(hz.at[1], hr.at[1], hr.at[1], u_peer(1)))
    o_far = []
    o_u[0]()
    if n > 2:
        o_far.append(
            send(of.at[before, low, :], of.at[before, low, :], of.at[beyond, low, :], u_peer(1))
        )
        o_u[1]()
        o_far.append(
            send(of.at[after, high, :], of.at[after, high, :], of.at[beyond, high, :], u_peer(last))
        )
        o_x[1] = spread_x(1)
    o_x[last] = spread_x(-1)

    y_base = take(n)

    def weight_terms(e):
        wait(o_x[e])
        target = at(u, e)
        for i in range(n):
            gp[e, i] = dot(gt[...], of[i * n + target]).astype(BF16)
        ours = target // m == dp
        arrived = send(
            gp.at[e], gd.at[e], gd.at[e], dp_peer, target // m != dp, ours
        )
        arrived()

        @pl.when(ours)
        def _():
            for i in range(n):
                gy[e, i] = (gp[e, i].astype(F32) + gd[e, i].astype(F32)).astype(BF16)

        for i in range(2):
            target_y = 2 * lax.rem(target, m) + i
            d = lax.rem(target_y - y + n, n)
            send(
                gy.at[e, pl.ds(i * m, m)],
                gyr.at[d],
                None,
                {"row": target_y * n + z},
                jnp.logical_and(ours, target_y != y),
                index=y_base + d,
            )

    weight_terms(0)
    upstream = head_sums(0)
    q_y = gather_full(q_z, lambda i: qf.at[span_of(i), :], False)
    if n > 2:
        wait(o_far)
        o_x[2] = spread_x(2)
    wait(h_u)
    for e in sorted({1, last}):
        upstream = upstream + hr[e].astype(F32)
    df[span_of(pair), :] = upstream.astype(BF16)
    d_h = gather_h(lambda i: df.at[span_of(i), :])
    d_y = [gather_y(lambda i: df.at[span_of(i), :], 0, False)]
    attended = of[own_of].astype(F32)
    row_dot = jnp.sum(
        df[span_of(pair), :].astype(F32) * attended, axis=1, keepdims=True
    )
    lane = lax.broadcasted_iota(jnp.int32, (span, HEAD), 1)
    table = jnp.where(lane == 0, log_norm, jnp.where(lane == 1, row_dot, 0.0))
    st[:, span_of(pair)] = jnp.transpose(table)[:8, :]
    s_h = gather_h(lambda i: st.at[:, span_of(i)])
    s_y = [gather_y(lambda i: st.at[:, span_of(i)], 0, False)]

    def queries_pass(j, first, acc):
        keys = kf[group(j), :]
        scores = dot_nt(qf[span_of(pair), :], keys) * SCALE
        probs = jnp.exp(scores - log_norm)
        if first:
            probs = jnp.where(key_pos <= query_pos, probs, 0.0)
        slopes = dot_nt(df[span_of(pair), :], vf[group(j), :])
        slopes = (probs * (slopes - row_dot)).astype(BF16)
        return acc + dot(slopes, keys)

    weight_terms(last)
    for h in range(1, m):
        d_h[h - 1]()
        d_y.append(gather_y(lambda i: df.at[span_of(i), :], h, False))
        s_h[h - 1]()
        s_y.append(gather_y(lambda i: st.at[:, span_of(i)], h, False))
    if n > 2:
        weight_terms(1)
    acc = queries_pass(y, True, jnp.zeros((span, HEAD), F32))
    acc = lax.fori_loop(0, y, lambda j, acc: queries_pass(j, False, acc), acc)
    acc = (acc * SCALE).astype(BF16)
    dx[0, 0], dx[0, 1] = acc[:rows], acc[rows:]
    swaps = [send(dx.at[0, 1 - side], dxr.at[0], dxr.at[0], twin)]
    if n > 2:
        weight_terms(2)

    lanes = [slice(h * HEAD, (h + 1) * HEAD) for h in range(2)]

    projected = jnp.zeros((cols, span), F32)
    for c in range(n * n):
        projected = projected + dot_nt(wf[c], of[c % n * n + c // n])
    for h in range(2):
        ox[h] = projected[:, lanes[h]].astype(BF16)
    o_s = send(ox.at[1 - side], oxr, oxr, twin)

    own_key = pair * span + lax.broadcasted_iota(jnp.int32, (span, chunk), 0)
    ask_pos = y * chunk + lax.broadcasted_iota(jnp.int32, (span, chunk), 1)

    def keys_pass(j, first):
        queries = qf[group(j), :]
        ups = df[group(j), :]
        norm = st[0:1, group(j)]
        away = st[1:2, group(j)]
        scores = dot_nt(kf[span_of(pair), :], queries) * SCALE
        probs = jnp.exp(scores - norm)
        if first:
            probs = jnp.where(ask_pos >= own_key, probs, 0.0)
        slopes = dot_nt(vf[span_of(pair), :], ups)
        slopes = (probs * (slopes - away)).astype(BF16)
        sum_k, sum_v = dot(slopes, queries), dot(probs.astype(BF16), ups)
        if first:
            acc_ref[...], sum_ref[...] = sum_k, sum_v
        else:
            acc_ref[...] += sum_k
            sum_ref[...] += sum_v

    keys_pass(y, True)

    for d in others:
        pltpu.make_async_remote_copy(
            src_ref=gyr.at[d],
            dst_ref=gyr.at[d],
            send_sem=send_sems.at[y_base + d],
            recv_sem=recv_sems.at[y_base + d],
            device_id=y_peer(d),
            device_id_type=pl.DeviceIdType.MESH,
        ).wait_recv()
    own_e = lax.rem(dp * m + y // 2 - u + n, n)
    own_i = lax.rem(y, 2) * m
    g_z = []
    for d in list(range(1, m)) + [0]:
        target = at_h(d)
        total = gy[own_e, own_i + target].astype(F32)
        for e in others:
            total = total + gyr[e, target].astype(F32)
        gz[d] = total.astype(BF16)
        if d:
            g_z.append(send(gz.at[d], gzr.at[d - 1], gzr.at[d - 1], h_peer(d)))
    for d in near:

        @pl.when(y + d < n)
        def _(d=d):
            wait(q_y[d], True)
            for h in range(m):
                d_y[h][d](True)
                s_y[h][d](True)
            keys_pass(y + d, False)

    for i, value in ((1, acc_ref[...] * SCALE), (2, sum_ref[...])):
        value = value.astype(BF16)
        dx[i, 0], dx[i, 1] = value[:rows], value[rows:]
        swaps.append(send(dx.at[i, 1 - side], dxr.at[i], dxr.at[i], twin))

    wait(g_z)
    total = gz[0].astype(F32)
    for d in range(1, m):
        total = total + gzr[d - 1].astype(F32)
    gw_ref[...] = total
    o_s()
    out_ref[...] = (ox[side].astype(F32) + oxr[...].astype(F32)).astype(BF16)
    for i, target in enumerate((dq_ref, dk_ref, dv_ref)):
        swaps[i]()
        own, other = dx[i, side], dxr[i]
        for h in range(2):
            target[:, lanes[h]] = jnp.where(side == h, own, other)

    for finish in issued:
        finish()


def store_all(*refs):
    count = len(refs) // 2
    copies = [
        pltpu.make_async_copy(refs[i], refs[count + i], refs[-1].at[i])
        for i in range(count)
    ]
    for copy in copies:
        copy.start()
    for copy in copies:
        copy.wait()


def shards(n, queries, key_vectors, value_vectors, out_weight, out_grad):
    rows, width = queries.shape[1:]
    cols = out_grad.shape[2]
    blocks, m = n * n, n // 2
    copies = 112
    vmem = pl.BlockSpec(memory_space=pltpu.VMEM)

    def buffer(*shape, kind=BF16):
        return pltpu.VMEM(shape, kind)

    full = buffer(blocks * rows, HEAD)
    span = 2 * rows
    result = pl.pallas_call(
        functools.partial(kernel, n, rows, cols),
        out_shape=(
            jax.ShapeDtypeStruct((cols, rows), BF16),
            jax.ShapeDtypeStruct((rows, width), BF16),
            jax.ShapeDtypeStruct((rows, width), BF16),
            jax.ShapeDtypeStruct((rows, width), BF16),
            jax.ShapeDtypeStruct((cols, HEAD), F32),
        ),
        in_specs=[pl.BlockSpec(memory_space=pltpu.HBM)] * 5,
        out_specs=(vmem,) * 5,
        scratch_shapes=[
            buffer(rows, HEAD),
            buffer(rows, HEAD),
            buffer(rows, HEAD),
            buffer(cols, HEAD),
            full,
            full,
            full,
            full,
            buffer(8, blocks * rows, kind=F32),
            buffer(blocks, cols, HEAD),
            buffer(span, cols),
            buffer(cols, span),
            buffer(n, n, span, HEAD),
            buffer(n, n - 1, span, HEAD),
            buffer(n, span, HEAD),
            buffer(n, span, HEAD),
            buffer(2, rows, HEAD),
            buffer(blocks, span, HEAD),
            buffer(span, HEAD, kind=F32),
            buffer(span, HEAD, kind=F32),
            buffer(span, HEAD, kind=F32),
            buffer(n, n, cols, HEAD),
            buffer(n, n, cols, HEAD),
            buffer(n, n, cols, HEAD),
            buffer(n, m, cols, HEAD),
            buffer(m, cols, HEAD),
            buffer(max(m - 1, 1), cols, HEAD),
            buffer(2, cols, rows),
            buffer(cols, rows),
            buffer(3, 2, rows, HEAD),
            buffer(3, rows, HEAD),
            pltpu.SemaphoreType.DMA((9,)),
            pltpu.SemaphoreType.DMA((copies,)),
            pltpu.SemaphoreType.DMA((copies,)),
        ],
        compiler_params=pltpu.CompilerParams(
            collective_id=0, has_side_effects=True, vmem_limit_bytes=64 << 20
        ),
    )(queries[0], key_vectors[0], value_vectors[0], out_weight.T, out_grad[0].T)
    result = pl.pallas_call(
        store_all,
        out_shape=[jax.ShapeDtypeStruct(a.shape, a.dtype) for a in result],
        in_specs=[vmem] * 5,
        out_specs=[pl.BlockSpec(memory_space=pltpu.HBM)] * 5,
        scratch_shapes=[pltpu.SemaphoreType.DMA((5,))],
    )(*result)
    output, grad_queries, grad_keys, grad_values, grad_weight = result
    return (
        output.T[None],
        grad_queries[None],
        grad_keys[None],
        grad_values[None],
        grad_weight.T,
    )


def solution(mesh):
    n = math.isqrt(mesh.shape["row"])
    return jax.shard_map(
        functools.partial(shards, n),
        mesh=mesh,
        in_specs=(
            P("dp", "row", "col"),
            P("dp", "row", "col"),
            P("dp", "row", "col"),
            P("row", "col"),
            P("dp", "row", "col"),
        ),
        out_specs=(
            P("dp", "row", "col"),
            P("dp", "row", "col"),
            P("dp", "row", "col"),
            P("dp", "row", "col"),
            P(("dp", "row"), "col"),
        ),
        check_vma=False,
    )
```

```python
import functools
import math

import jax
import jax.numpy as jnp
from jax import lax
from jax.experimental import pallas as pl
from jax.experimental.pallas import tpu as pltpu
from jax.sharding import PartitionSpec as P

HEAD = 128
NEG = -1e30
SCALE = 1.0 / math.sqrt(HEAD)
F32 = jnp.float32
BF16 = jnp.bfloat16
NT = (((1,), (1,)), ((), ()))
TN = (((0,), (0,)), ((), ()))


def dot(a, b):
    return jnp.dot(a, b, preferred_element_type=F32)


def dot_nt(a, b):
    return lax.dot_general(a, b, NT, preferred_element_type=F32)


def flip(a):
    size = a.shape[0]
    eye = (
        lax.broadcasted_iota(jnp.int32, (size, size), 0)
        == lax.broadcasted_iota(jnp.int32, (size, size), 1)
    )
    eye = jnp.where(eye, 1.0, 0.0).astype(BF16)
    return lax.dot_general(a, eye, TN, preferred_element_type=F32).astype(BF16)


def kernel(
    n,
    rows,
    cols,
    q_hbm,
    k_hbm,
    v_hbm,
    w_hbm,
    g_hbm,
    out_ref,
    dq_ref,
    dk_ref,
    dv_ref,
    gw_ref,
    qs,
    ks,
    vs,
    ws,
    kf,
    vf,
    qf,
    df,
    st,
    wf,
    gf,
    gt,
    hs,
    hx,
    hz,
    hr,
    hq,
    of,
    top_ref,
    sum_ref,
    acc_ref,
    gp,
    gd,
    gy,
    gyr,
    gz,
    gzr,
    ox,
    oxr,
    dx,
    dxr,
    load_sems,
    send_sems,
    recv_sems,
):
    dp, row, col = lax.axis_index("dp"), lax.axis_index("row"), lax.axis_index("col")
    m = n // 2
    y, z = row // n, lax.rem(row, n)
    zh, side = z // 2, lax.rem(z, 2)
    u, x = col // n, lax.rem(col, n)
    pair = y * m + zh
    span = 2 * rows
    chunk = n * rows
    others = list(range(1, n))
    far = sorted(others, key=lambda d: -min(d, n - d))
    near = far[::-1]
    z_steps = [(h, t) for h in range(m) for t in (1, 0) if h or t]

    def at(base, d):
        return lax.rem(base + d + n, n)

    def at_h(d):
        return lax.rem(zh + d + m, m)

    dp_peer = {"dp": 1 - dp}
    twin = {"row": row + 1 - 2 * side}

    def z_row(h, t):
        return y * n + 2 * at_h(h) + (1 - side if t else side)

    def h_peer(d):
        return {"row": z_row(d, 0)}

    def y_peer(d):
        return {"row": at(y, d) * n + z}

    def u_peer(d):
        return {"col": at(u, d) * n + x}

    def x_peer(d):
        return {"col": u * n + at(x, d)}

    def block(i):
        return pl.ds(pl.multiple_of(i * rows, rows), rows)

    def span_of(i):
        return pl.ds(pl.multiple_of(i * span, span), span)

    def group(i):
        return pl.ds(pl.multiple_of(i * chunk, chunk), chunk)

    half = cols // 2
    mine = pl.ds(pl.multiple_of(dp * half, half), half)
    theirs = pl.ds(pl.multiple_of((1 - dp) * half, half), half)
    own_lanes = block(side)
    other_lanes = block(1 - side)

    pieces = [
        (w_hbm.at[mine, own_lanes], wf.at[row, mine, :]),
        (w_hbm.at[mine, other_lanes], ws.at[mine, :]),
        (g_hbm, gt.at[:, own_lanes]),
    ]
    for source, split, full in ((k_hbm, ks, kf), (q_hbm, qs, qf), (v_hbm, vs, vf)):
        pieces.append((source.at[:, own_lanes], full.at[block(row), :]))
        pieces.append((source.at[:, other_lanes], split))
    loads = [
        pltpu.make_async_copy(source, target, load_sems.at[i])
        for i, (source, target) in enumerate(pieces)
    ]

    barrier = pltpu.get_barrier_semaphore()
    peers = [dp_peer] + [{"row": z_row(h, t)} for h, t in z_steps]
    peers += [u_peer(d) for d in sorted({1, n - 1})]
    peers += [f(d) for f in (y_peer, x_peer) for d in far]
    for peer in peers:
        pl.semaphore_signal(
            barrier, inc=1, device_id=peer, device_id_type=pl.DeviceIdType.MESH
        )
    for load in loads:
        load.start()

    issued = []
    slots = [0]

    def when(cond, body):
        if cond is None:
            body()
        else:
            pl.when(cond)(body)

    def take(count):
        slots[0] += count
        return slots[0] - count

    def send(src, dst, landed, peer, sends=None, receives=None, index=None):
        index = take(1) if index is None else index

        def describe(source, target, which):
            return pltpu.make_async_remote_copy(
                src_ref=source,
                dst_ref=target,
                send_sem=send_sems.at[which],
                recv_sem=recv_sems.at[which],
                device_id=peer,
                device_id_type=pl.DeviceIdType.MESH,
            )

        when(sends, lambda: describe(src, dst, index).start())
        issued.append(
            lambda: when(sends, lambda: describe(src, dst, index).wait_send())
        )
        if landed is None:
            return None
        return lambda inside=False: when(
            None if inside else receives,
            lambda: describe(landed, landed, index).wait_recv(),
        )

    def wait(handles, *inside):
        for handle in handles:
            handle(*inside)

    def spread_z(own, split, view, steps):
        return {
            (h, t): send(
                split if t else own, view(row), view(z_row(-h, t)), {"row": z_row(h, t)}
            )
            for h, t in steps
        }

    def gather_h(view):
        return [
            send(view(pair), view(pair), view(y * m + at_h(-d)), h_peer(d))
            for d in range(1, m)
        ]

    def gather_y(view, h, up):
        handles = {}
        for d in near:
            if up is None:
                sends = receives = None
            elif up:
                sends, receives = y + d < n, y >= d
            else:
                sends, receives = y >= d, y + d < n
            s = -1 if up is False else 1
            mid = at_h(-h)
            handles[d] = send(
                view(y * m + mid),
                view(y * m + mid),
                view(at(y, -s * d) * m + mid),
                y_peer(s * d),
                sends,
                receives,
            )
        return handles

    def gather_full(arrived, view, up):
        handles = []
        for h in range(m):
            wait([arrived[step] for step in z_steps if step[0] == h and step in arrived])
            handles.append(gather_y(view, h, up))
        return {d: [piece[d] for piece in handles] for d in near}

    def k_view(i):
        return kf.at[block(i), :]

    def w_pair(i):
        return wf.at[pl.ds(2 * i, 2), mine, :]

    def w_group(i, part=mine):
        return wf.at[pl.ds(i * n, n), part, :]

    wait([load.wait for load in loads])
    pl.semaphore_wait(barrier, len(peers))

    w_z = spread_z(
        wf.at[row, mine, :], ws.at[mine, :], lambda i: wf.at[i, mine, :], z_steps
    )
    g_s = send(gt.at[:, own_lanes], gt.at[:, own_lanes], gt.at[:, other_lanes], twin)
    w_parts = []
    for h in range(m):
        wait([w_z[step] for step in z_steps if step[0] == h])
        w_parts.append(gather_y(w_pair, h, None))
        if h == 0:
            k_z = spread_z(
                kf.at[block(row), :], ks, lambda i: kf.at[block(i), :], z_steps
            )
    w_d = {0: send(w_group(y), w_group(y), w_group(y, theirs), dp_peer)}
    q_s = spread_z(qf.at[block(row), :], qs, lambda i: qf.at[block(i), :], z_steps[:1])
    v_z = spread_z(vf.at[block(row), :], vs, lambda i: vf.at[block(i), :], z_steps)
    q_z = spread_z(qf.at[block(row), :], qs, lambda i: qf.at[block(i), :], z_steps[1:])
    g_s()
    gf[...] = flip(gt[...])

    x_base = take(n * (n - 1))

    def x_send(d, e):
        index = x_base + d * (n - 1) + e - 1
        send(hs.at[d, e], hx.at[d, e - 1], None, x_peer(e), index=index)

    def head_terms(d):
        w_d[d]()
        for e in far + [0]:
            hs[d, e] = dot(gf[...], wf[at(y, d) * n + at(x, e)]).astype(BF16)
            if e:
                x_send(d, e)

    def head_sums(e):
        d = lax.rem(u + e - y + n, n)
        total = hs[d, 0].astype(F32)
        for k in far:
            pltpu.make_async_remote_copy(
                src_ref=hx.at[d, k - 1],
                dst_ref=hx.at[d, k - 1],
                send_sem=send_sems.at[x_base + d * (n - 1) + k - 1],
                recv_sem=recv_sems.at[x_base + d * (n - 1) + k - 1],
                device_id=x_peer(k),
                device_id_type=pl.DeviceIdType.MESH,
            ).wait_recv()
            total = total + hx[d, k - 1].astype(F32)
        return total

    head_terms(0)
    k_y = gather_full(k_z, lambda i: kf.at[span_of(i), :], True)
    v_y = gather_full(v_z, lambda i: vf.at[span_of(i), :], True)

    query_pos = pair * span + lax.broadcasted_iota(jnp.int32, (span, chunk), 0)
    key_pos = y * chunk + lax.broadcasted_iota(jnp.int32, (span, chunk), 1)

    def forward(j, first):
        scores = dot_nt(qf[span_of(pair), :], kf[group(j), :]) * SCALE
        if first:
            scores = jnp.where(key_pos <= query_pos, scores, NEG)
        new_top = jnp.max(scores, axis=1, keepdims=True)
        if not first:
            top = top_ref[:, :1]
            new_top = jnp.maximum(top, new_top)
        weights = jnp.exp(scores - new_top)
        total = jnp.sum(weights, axis=1, keepdims=True)
        acc = dot(weights.astype(BF16), vf[group(j), :])
        if not first:
            fade = jnp.exp(top - new_top)
            total = fade * sum_ref[:, :1] + total
            acc = fade * acc_ref[...] + acc
        top_ref[...] = jnp.broadcast_to(new_top, top_ref.shape)
        sum_ref[...] = jnp.broadcast_to(total, sum_ref.shape)
        acc_ref[...] = acc

    for d in near:
        wait([part[d] for part in w_parts])
        source = at(y, -d)
        w_d[n - d] = send(w_group(source), w_group(source), w_group(source, theirs), dp_peer)
    wait(q_s.values())
    forward(y, True)
    for d in near:
        head_terms(n - d)
    q_y = gather_full(q_z, lambda i: qf.at[span_of(i), :], False)
    for d in near:

        @pl.when(y >= d)
        def _(d=d):
            wait(k_y[d], True)
            wait(v_y[d], True)
            forward(y - d, False)

    own_of = x * n + u
    total = sum_ref[:, :1]
    of[own_of] = (acc_ref[...] / total).astype(BF16)
    log_norm = top_ref[:, :1] + jnp.log(total)
    last = n - 1
    low, high = slice(0, rows), slice(rows, span)
    before, after = x * n + at(u, -1), x * n + at(u, 1)
    beyond = x * n + at(u, 2)

    o_u = [send(of.at[own_of], of.at[own_of], of.at[before], u_peer(1))]
    if n > 2:
        o_u.append(send(of.at[own_of], of.at[own_of], of.at[after], u_peer(last)))

    def spread_x(e):
        return [
            send(
                of.at[x * n + at(u, e)],
                of.at[x * n + at(u, e)],
                of.at[at(x, -d) * n + at(u, e)],
                x_peer(d),
            )
            for d in far
        ]

    o_x = {0: spread_x(0)}
    h_u = []
    if n > 2:
        hz[2] = head_sums(2).astype(BF16)
        relay = [
            send(hz.at[2, low, :], hq.at[0], hq.at[0], u_peer(1)),
            send(hz.at[2, high, :], hq.at[1], hq.at[1], u_peer(last)),
        ]
        for e, part in ((1, high), (last, low)):
            hz[e] = head_sums(e).astype(BF16)
            h_u.append(
                send(hz.at[e, part, :], hr.at[e, part, :], hr.at[e, part, :], u_peer(e))
            )
        for i, e, part in ((0, 1, low), (1, last, high)):
            relay[i]()
            hz[e, part, :] = (hz[e, part, :].astype(F32) + hq[i].astype(F32)).astype(
                BF16
            )
            h_u.append(
                send(hz.at[e, part, :], hr.at[e, part, :], hr.at[e, part, :], u_peer(e))
            )
    else:
        hz[1] = head_sums(1).astype(BF16)
        h_u.append(send(hz.at[1], hr.at[1], hr.at[1], u_peer(1)))
    o_far = []
    o_u[0]()
    if n > 2:
        o_far.append(
            send(of.at[before, low, :], of.at[before, low, :], of.at[beyond, low, :], u_peer(1))
        )
        o_u[1]()
        o_far.append(
            send(of.at[after, high, :], of.at[after, high, :], of.at[beyond, high, :], u_peer(last))
        )
        o_x[1] = spread_x(1)
    o_x[last] = spread_x(-1)

    y_base = take(n)

    def weight_terms(e):
        wait(o_x[e])
        target = at(u, e)
        for i in range(n):
            gp[e, i] = dot(gt[...], of[i * n + target]).astype(BF16)
        ours = target // m == dp
        arrived = send(
            gp.at[e], gd.at[e], gd.at[e], dp_peer, target // m != dp, ours
        )
        arrived()

        @pl.when(ours)
        def _():
            for i in range(n):
                gy[e, i] = (gp[e, i].astype(F32) + gd[e, i].astype(F32)).astype(BF16)

        for i in range(2):
            target_y = 2 * lax.rem(target, m) + i
            d = lax.rem(target_y - y + n, n)
            send(
                gy.at[e, pl.ds(i * m, m)],
                gyr.at[d],
                None,
                {"row": target_y * n + z},
                jnp.logical_and(ours, target_y != y),
                index=y_base + d,
            )

    weight_terms(0)
    upstream = head_sums(0)
    if n > 2:
        wait(o_far)
        o_x[2] = spread_x(2)
    wait(h_u)
    for e in sorted({1, last}):
        upstream = upstream + hr[e].astype(F32)
    df[span_of(pair), :] = upstream.astype(BF16)
    d_h = gather_h(lambda i: df.at[span_of(i), :])
    d_y = [gather_y(lambda i: df.at[span_of(i), :], 0, False)]
    attended = of[own_of].astype(F32)
    row_dot = jnp.sum(
        df[span_of(pair), :].astype(F32) * attended, axis=1, keepdims=True
    )
    lane = lax.broadcasted_iota(jnp.int32, (span, HEAD), 1)
    table = jnp.where(lane == 0, log_norm, jnp.where(lane == 1, row_dot, 0.0))
    st[:, span_of(pair)] = jnp.transpose(table)[:8, :]
    s_h = gather_h(lambda i: st.at[:, span_of(i)])
    s_y = [gather_y(lambda i: st.at[:, span_of(i)], 0, False)]

    def queries_pass(j, first, acc):
        keys = kf[group(j), :]
        scores = dot_nt(qf[span_of(pair), :], keys) * SCALE
        probs = jnp.exp(scores - log_norm)
        if first:
            probs = jnp.where(key_pos <= query_pos, probs, 0.0)
        slopes = dot_nt(df[span_of(pair), :], vf[group(j), :])
        slopes = (probs * (slopes - row_dot)).astype(BF16)
        return acc + dot(slopes, keys)

    weight_terms(last)
    for h in range(1, m):
        d_h[h - 1]()
        d_y.append(gather_y(lambda i: df.at[span_of(i), :], h, False))
        s_h[h - 1]()
        s_y.append(gather_y(lambda i: st.at[:, span_of(i)], h, False))
    if n > 2:
        weight_terms(1)
    acc = queries_pass(y, True, jnp.zeros((span, HEAD), F32))
    acc = lax.fori_loop(0, y, lambda j, acc: queries_pass(j, False, acc), acc)
    acc = (acc * SCALE).astype(BF16)
    dx[0, 0], dx[0, 1] = acc[:rows], acc[rows:]
    swaps = [send(dx.at[0, 1 - side], dxr.at[0], dxr.at[0], twin)]
    if n > 2:
        weight_terms(2)

    lanes = [slice(h * HEAD, (h + 1) * HEAD) for h in range(2)]

    projected = jnp.zeros((cols, span), F32)
    for c in range(n * n):
        projected = projected + dot_nt(wf[c], of[c % n * n + c // n])
    for h in range(2):
        ox[h] = projected[:, lanes[h]].astype(BF16)
    o_s = send(ox.at[1 - side], oxr, oxr, twin)

    own_key = pair * span + lax.broadcasted_iota(jnp.int32, (span, chunk), 0)
    ask_pos = y * chunk + lax.broadcasted_iota(jnp.int32, (span, chunk), 1)

    def keys_pass(j, first):
        queries = qf[group(j), :]
        ups = df[group(j), :]
        norm = st[0:1, group(j)]
        away = st[1:2, group(j)]
        scores = dot_nt(kf[span_of(pair), :], queries) * SCALE
        probs = jnp.exp(scores - norm)
        if first:
            probs = jnp.where(ask_pos >= own_key, probs, 0.0)
        slopes = dot_nt(vf[span_of(pair), :], ups)
        slopes = (probs * (slopes - away)).astype(BF16)
        sum_k, sum_v = dot(slopes, queries), dot(probs.astype(BF16), ups)
        if first:
            acc_ref[...], sum_ref[...] = sum_k, sum_v
        else:
            acc_ref[...] += sum_k
            sum_ref[...] += sum_v

    keys_pass(y, True)

    for d in others:
        pltpu.make_async_remote_copy(
            src_ref=gyr.at[d],
            dst_ref=gyr.at[d],
            send_sem=send_sems.at[y_base + d],
            recv_sem=recv_sems.at[y_base + d],
            device_id=y_peer(d),
            device_id_type=pl.DeviceIdType.MESH,
        ).wait_recv()
    own_e = lax.rem(dp * m + y // 2 - u + n, n)
    own_i = lax.rem(y, 2) * m
    g_z = []
    for d in list(range(1, m)) + [0]:
        target = at_h(d)
        total = gy[own_e, own_i + target].astype(F32)
        for e in others:
            total = total + gyr[e, target].astype(F32)
        gz[d] = total.astype(BF16)
        if d:
            g_z.append(send(gz.at[d], gzr.at[d - 1], gzr.at[d - 1], h_peer(d)))
    for d in near:

        @pl.when(y + d < n)
        def _(d=d):
            wait(q_y[d], True)
            for h in range(m):
                d_y[h][d](True)
                s_y[h][d](True)
            keys_pass(y + d, False)

    for i, value in ((1, acc_ref[...] * SCALE), (2, sum_ref[...])):
        value = value.astype(BF16)
        dx[i, 0], dx[i, 1] = value[:rows], value[rows:]
        swaps.append(send(dx.at[i, 1 - side], dxr.at[i], dxr.at[i], twin))

    wait(g_z)
    total = gz[0].astype(F32)
    for d in range(1, m):
        total = total + gzr[d - 1].astype(F32)
    gw_ref[...] = total
    o_s()
    out_ref[...] = (ox[side].astype(F32) + oxr[...].astype(F32)).astype(BF16)
    for i, target in enumerate((dq_ref, dk_ref, dv_ref)):
        swaps[i]()
        own, other = dx[i, side], dxr[i]
        for h in range(2):
            target[:, lanes[h]] = jnp.where(side == h, own, other)

    for finish in issued:
        finish()


def store_all(*refs):
    count = len(refs) // 2
    copies = [
        pltpu.make_async_copy(refs[i], refs[count + i], refs[-1].at[i])
        for i in range(count)
    ]
    for copy in copies:
        copy.start()
    for copy in copies:
        copy.wait()


def shards(n, queries, key_vectors, value_vectors, out_weight, out_grad):
    rows, width = queries.shape[1:]
    cols = out_grad.shape[2]
    blocks, m = n * n, n // 2
    copies = 112
    vmem = pl.BlockSpec(memory_space=pltpu.VMEM)

    def buffer(*shape, kind=BF16):
        return pltpu.VMEM(shape, kind)

    full = buffer(blocks * rows, HEAD)
    span = 2 * rows
    result = pl.pallas_call(
        functools.partial(kernel, n, rows, cols),
        out_shape=(
            jax.ShapeDtypeStruct((cols, rows), BF16),
            jax.ShapeDtypeStruct((rows, width), BF16),
            jax.ShapeDtypeStruct((rows, width), BF16),
            jax.ShapeDtypeStruct((rows, width), BF16),
            jax.ShapeDtypeStruct((cols, HEAD), F32),
        ),
        in_specs=[pl.BlockSpec(memory_space=pltpu.HBM)] * 5,
        out_specs=(vmem,) * 5,
        scratch_shapes=[
            buffer(rows, HEAD),
            buffer(rows, HEAD),
            buffer(rows, HEAD),
            buffer(cols, HEAD),
            full,
            full,
            full,
            full,
            buffer(8, blocks * rows, kind=F32),
            buffer(blocks, cols, HEAD),
            buffer(span, cols),
            buffer(cols, span),
            buffer(n, n, span, HEAD),
            buffer(n, n - 1, span, HEAD),
            buffer(n, span, HEAD),
            buffer(n, span, HEAD),
            buffer(2, rows, HEAD),
            buffer(blocks, span, HEAD),
            buffer(span, HEAD, kind=F32),
            buffer(span, HEAD, kind=F32),
            buffer(span, HEAD, kind=F32),
            buffer(n, n, cols, HEAD),
            buffer(n, n, cols, HEAD),
            buffer(n, n, cols, HEAD),
            buffer(n, m, cols, HEAD),
            buffer(m, cols, HEAD),
            buffer(max(m - 1, 1), cols, HEAD),
            buffer(2, cols, rows),
            buffer(cols, rows),
            buffer(3, 2, rows, HEAD),
            buffer(3, rows, HEAD),
            pltpu.SemaphoreType.DMA((9,)),
            pltpu.SemaphoreType.DMA((copies,)),
            pltpu.SemaphoreType.DMA((copies,)),
        ],
        compiler_params=pltpu.CompilerParams(
            collective_id=0, has_side_effects=True, vmem_limit_bytes=64 << 20
        ),
    )(queries[0], key_vectors[0], value_vectors[0], out_weight.T, out_grad[0].T)
    result = pl.pallas_call(
        store_all,
        out_shape=[jax.ShapeDtypeStruct(a.shape, a.dtype) for a in result],
        in_specs=[vmem] * 5,
        out_specs=[pl.BlockSpec(memory_space=pltpu.HBM)] * 5,
        scratch_shapes=[pltpu.SemaphoreType.DMA((5,))],
    )(*result)
    output, grad_queries, grad_keys, grad_values, grad_weight = result
    return (
        output.T[None],
        grad_queries[None],
        grad_keys[None],
        grad_values[None],
        grad_weight.T,
    )


def solution(mesh):
    n = math.isqrt(mesh.shape["row"])
    return jax.shard_map(
        functools.partial(shards, n),
        mesh=mesh,
        in_specs=(
            P("dp", "row", "col"),
            P("dp", "row", "col"),
            P("dp", "row", "col"),
            P("row", "col"),
            P("dp", "row", "col"),
        ),
        out_specs=(
            P("dp", "row", "col"),
            P("dp", "row", "col"),
            P("dp", "row", "col"),
            P("dp", "row", "col"),
            P(("dp", "row"), "col"),
        ),
        check_vma=False,
    )
```
